32 devices in a mesh: clip: 2 (over y), ha: 4 (over z), wa: 4 (over x, core).
Axes of the slice: x: 2, y: 2, z: 4, core: 2. Of those that a mesh axis runs over, the one named last changes fastest.
Arguments:
- cotangent: float32 [8, 16, 256, 96], P('clip', 'ha', 'wa'), parts along dimension 0, may hold values from -6 to 6
- stored_first: float32 [8, 16, 256, 96], P('clip', 'ha', 'wa'), parts along dimension 0, may hold values from -8 to 8
- stored_second: float32 [8, 16, 256, 96], P('clip', 'ha', 'wa'), parts along dimension 0, may hold values from -8 to 8
- w_first: float32 [3, 3, 3, 96, 96], replicated, may hold values from -0.125 to 0.125
- w_second: float32 [3, 3, 3, 96, 96], replicated, may hold values from -0.125 to 0.125
- w_third: float32 [3, 3, 3, 96, 96], replicated, may hold values from -0.125 to 0.125
Outputs:
- input_grad: float32 [8, 16, 256, 96], P('clip', 'ha', 'wa'), parts along dimension 0
The draws below stay inside these ranges and needn't reach their ends.
There are 2 independent parts, one for each index of `clip`. The reference program is written for one: setup_inputs(seed, part) draws one part's arguments, and reference() takes and returns one part's arrays. A program takes and returns all parts, laid end to end along the dimension named above; an argument that names none is the same for every part. Nothing has to cross between parts.
All inputs are finite; a program needn't handle non-finite values.
Results may differ from the reference program's by a relative error of at most 0.00013.
Values sent between devices are 32-bit elements; how exact they have to be, the bound alone decides.
No kernel may reach another device: no remote copies, remote signals or barrier semaphores. Data moves between devices by JAX's collectives and lax.ppermute only.
A program may use at most 64 MiB of HBM per device.

```python
import jax
import jax.numpy as jnp
from jax import lax

C = 96
F = 4
H = 16
W = 256


def levels(stream_key, extent, shards, smallest, top_value):
    loudness, own = 1.0, jax.random.fold_in(stream_key, 6)
    for position, parts in shards:
        steps = jnp.exp(jax.random.uniform(jax.random.fold_in(own, position), (parts,), jnp.float32, smallest / len(shards), top_value / len(shards)))
        loudness = loudness * jnp.repeat(steps, extent[position] // parts).reshape([-1 if axis == position else 1 for axis in range(len(extent))])
    return loudness


def bell_draw(key, dims, scale, limit, cuts=(), kind=jnp.bfloat16):
    drawn = scale * jax.random.normal(key, dims, jnp.float32)
    if cuts:
        drawn = drawn * levels(key, dims, cuts, -0.22, 0.18)
    return jnp.clip(drawn, -limit, limit).astype(kind)


def setup_inputs(seed: int = 0, part: int = 0) -> dict:
    splits = jax.random.split(jax.random.key(seed), 7)
    own_keys = jax.random.split(jax.random.fold_in(splits[6], part), 7)
    cotangent = bell_draw(own_keys[0], (F, H, W, C), 1.0, 6.0, ((1, 4), (2, 4)), jnp.float32)
    stored_first = bell_draw(own_keys[1], (F, H, W, C), 2.0, 8.0, ((1, 4), (2, 4)), jnp.float32)
    stored_second = bell_draw(own_keys[2], (F, H, W, C), 2.0, 8.0, ((1, 4), (2, 4)), jnp.float32)
    w_first = bell_draw(splits[3], (3, 3, 3, C, C), (27 * C) ** -0.5, 0.125, (), jnp.float32)
    w_second = bell_draw(splits[4], (3, 3, 3, C, C), (27 * C) ** -0.5, 0.125, (), jnp.float32)
    w_third = bell_draw(splits[5], (3, 3, 3, C, C), (27 * C) ** -0.5, 0.125, (), jnp.float32)
    return dict(cotangent=cotangent, stored_first=stored_first, stored_second=stored_second, w_first=w_first, w_second=w_second, w_third=w_third)


def back_conv(gradient, kernel):
    padded = jnp.pad(gradient, ((0, 2), (1, 1), (1, 1), (0, 0)))
    flipped = jnp.transpose(jnp.flip(kernel, (0, 1, 2)), (0, 1, 2, 4, 3))
    result = lax.conv_general_dilated(padded[None], flipped, (1, 1, 1), "VALID",
                                      dimension_numbers=("NDHWC", "DHWIO", "NDHWC"),
                                      precision=lax.Precision.HIGHEST)
    return result[0]


def silu_slope(value):
    sigma = jax.nn.sigmoid(value)
    return sigma * (1.0 + value * (1.0 - sigma))


def reference(cotangent, stored_first, stored_second, w_first, w_second, w_third):
    second_grad = back_conv(cotangent, w_third) * silu_slope(stored_second)
    first_grad = back_conv(second_grad, w_second) * silu_slope(stored_first)
    return back_conv(first_grad, w_first)
```

```python
import functools

import jax
import jax.numpy as jnp
from jax import lax
from jax.experimental import pallas as pl
from jax.experimental.pallas import tpu as pltpu
from jax.sharding import PartitionSpec as P

LANES = 128
SUB = 8
F32 = jnp.float32
BF16 = jnp.bfloat16
VMEM_SPEC = pl.BlockSpec(memory_space=pltpu.VMEM)
SMEM_SPEC = pl.BlockSpec(memory_space=pltpu.SMEM)


def silu_slope(value):
    sigma = 1.0 / (1.0 + jnp.exp(-value))
    return sigma * (1.0 + value * (1.0 - sigma))


def roll(value, shift, axis):
    return pltpu.roll(value, shift % value.shape[axis], axis)


def lane_of(shape):
    return lax.broadcasted_iota(jnp.int32, shape, len(shape) - 1)


def sub_of(shape):
    return lax.broadcasted_iota(jnp.int32, shape, len(shape) - 2)


def group_frames(frames, chans):
    first, second, third, fourth = frames
    part = LANES - chans
    lane = lane_of(first.shape)
    packed = []
    for index, frame in enumerate((first, second, third)):
        packed.append(jnp.where(lane < chans, frame, roll(fourth, chans - part * index, 1)))
    return packed


def ungroup_frames(groups, chans):
    part = LANES - chans
    lane = lane_of(groups[0].shape)
    frames = [jnp.where(lane < chans, group, 0.0) for group in groups]
    fourth = jnp.zeros_like(groups[0])
    for index in reversed(range(3)):
        moved = roll(groups[index], part * (index + 1), 1)
        fourth = jnp.where(lane < part * (index + 1), moved, fourth)
    return frames + [jnp.where(lane < chans, fourth, 0.0)]


def pack_kernel(par_ref, cot_ref, sec_ref, fst_ref, ha0, ha1, hb0, hb1, wp0, wp1, cp_ref, s2_ref, s1_ref):
    frames, rows, cols, chans = cot_ref.shape
    blank = jnp.zeros((frames, rows, cols, LANES), F32)
    cp_ref[...] = blank
    s2_ref[...] = blank
    s1_ref[...] = blank
    for t in range(frames):
        for h in range(rows):
            cp_ref[t, h, :, 0:chans] = cot_ref[t, h]
            s2_ref[t, h, :, 0:chans] = silu_slope(sec_ref[t, h])
            s1_ref[t, h, :, 0:chans] = silu_slope(fst_ref[t, h])

    def rows_out(top_a, top_b, low_a, low_b):
        def put(src, h, dst, at):
            for g, val in enumerate(group_frames([src[t, h] for t in range(frames)], chans)):
                dst[g, at] = val

        for r in range(3):
            put(cp_ref, r, top_a, r)
            put(cp_ref, rows - 3 + r, low_a, r)
        for r in range(2):
            put(s2_ref, r, top_b, r)
            put(s2_ref, rows - 2 + r, low_b, r)
        put(s1_ref, 0, top_b, 2)
        put(s1_ref, rows - 1, low_b, 2)

    @pl.when(par_ref[0] == 0)
    def _():
        rows_out(ha1, hb1, ha0, hb0)

    @pl.when(par_ref[0] != 0)
    def _():
        rows_out(ha0, hb0, ha1, hb1)

    def cols_out(left, right):
        sub = sub_of((SUB, LANES))
        for t in range(frames):
            for h in range(rows):
                last = pl.ds(cols - SUB, SUB)
                c7, a7, b7 = cp_ref[t, h, last], s2_ref[t, h, last], s1_ref[t, h, last]
                c0, a0, b0 = cp_ref[t, h, 0:SUB], s2_ref[t, h, 0:SUB], s1_ref[t, h, 0:SUB]
                right[t, h] = jnp.where(
                    sub >= 5, c7, jnp.where((sub == 2) | (sub == 3), roll(a7, 4, 0), jnp.where(sub == 1, roll(b7, 2, 0), 0.0))
                )
                left[t, h] = jnp.where(
                    sub < 3, c0, jnp.where((sub == 4) | (sub == 5), roll(a0, 4, 0), jnp.where(sub == 6, roll(b0, 6, 0), 0.0))
                )

    @pl.when(par_ref[1] == 0)
    def _():
        cols_out(wp1, wp0)

    @pl.when(par_ref[1] != 0)
    def _():
        cols_out(wp0, wp1)


def corner_kernel(par_ref, rw0, rw1, hc0, hc1, left, right):
    rows = rw0.shape[1]

    @pl.when(par_ref[1] == 0)
    def _():
        left[...] = rw1[...]
        right[...] = rw0[...]

    @pl.when(par_ref[1] != 0)
    def _():
        left[...] = rw0[...]
        right[...] = rw1[...]

    def out(top, low):
        for side, src in enumerate((left, right)):
            for r in range(3):
                top[:, r, side] = src[:, r]
                low[:, r, side] = src[:, rows - 3 + r]

    @pl.when(par_ref[0] == 0)
    def _():
        out(hc1, hc0)

    @pl.when(par_ref[0] != 0)
    def _():
        out(hc0, hc1)


def weight_kernel(w_ref, out_ref):
    chans = w_ref.shape[3]
    out_ref[...] = jnp.zeros(out_ref.shape, BF16)
    for k in range(3):
        for i in range(3):
            f0, f1, f2 = (w_ref[i, 2 - m, k] for m in range(3))
            even, odd = (f0 + f2) * (1 / 6), f1 * (1 / 6)
            far, odd2 = f0 * (1 / 24) + f2 * (1 / 6), f1 * (1 / 12)
            points = (f0 * 0.25, -even - odd, odd - even, far + odd2, far - odd2, f2)
            lanes = pl.ds((2 - i) * LANES, chans)
            for p, u in enumerate(points):
                high = u.astype(BF16)
                out_ref[p, k, 0, 0:chans, lanes] = high
                out_ref[p, k, 1, 0:chans, lanes] = (u - high.astype(F32)).astype(BF16)


def transform(rows, sizes, store):
    base = 0
    for tile, size in enumerate(sizes):
        if size == 4:
            x0, x1, x2, x3, x4, x5 = (rows(base + r) for r in range(6))
            a, b = x4 - 4.0 * x2, x3 - 4.0 * x1
            c, e = x4 - x2, 2.0 * (x3 - x1)
            points = ((4.0 * x0 - 5.0 * x2 + x4, 0), (a + b, 1), (a - b, 2), (c + e, 3), (c - e, 4),
                      (4.0 * x1 - 5.0 * x3 + x5, 5))
        else:
            x0, x1, x2, x3 = (rows(base + r) for r in range(4))
            points = ((4.0 * (x0 - x2), 0), (-3.0 * (x1 + x2), 1), (-3.0 * (x2 - x1), 2), (x3 - x1, 5))
        for value, point in points:
            store(point, tile, value)
        base += size


def conv(read, sizes, width, s_ref, y_ref, w_ref, emit):
    frames = 4
    chunk = 16

    def one(c, carry):
        start = pl.multiple_of(c * chunk, chunk)
        for t in range(frames):
            def store(point, tile, value):
                high = value.astype(BF16)
                low = (value - high.astype(F32)).astype(BF16)
                at = pl.ds(pl.multiple_of(tile * width + start, chunk), chunk)
                s_ref[point, at, t * LANES:(t + 1) * LANES] = high
                s_ref[point, at, (frames + t) * LANES:(frames + t + 1) * LANES] = low

            transform(lambda r: read(t, r, start, chunk), sizes, store)
        return carry

    lax.fori_loop(0, width // chunk, one, 0)

    zero = jnp.zeros((LANES, LANES), BF16)
    half = frames // 2 * LANES
    for p in range(6):
        tiles = sum(1 for size in sizes if size == 4 or p in (0, 1, 2, 5))
        m = tiles * width
        both, late = [], []
        for k in range(3):
            def stack(part):
                r = w_ref[p, k, part]
                return jnp.concatenate([jnp.concatenate([r, zero], 1), jnp.concatenate([zero, r], 1)], 0)

            def stack_late(part):
                r = w_ref[p, k, part]
                return jnp.concatenate([r[:, :2 * LANES], jnp.concatenate([zero, r[:, :LANES]], 1)], 0)

            both.append(jnp.concatenate([stack(0), stack(0), stack(1)], 1))
            late.append(jnp.concatenate([stack_late(0), stack_late(0), stack_late(1)], 1))
        lhs = s_ref[p, 0:m, :]
        high = lhs[:, :2 * half]
        late_high, late_low = lhs[:, half:2 * half], lhs[:, 3 * half:]
        for pair, (left, right) in enumerate((
            (jnp.concatenate([lhs, high], 1), jnp.concatenate(both, 0)),
            (jnp.concatenate([late_high, late_low, late_high], 1), jnp.concatenate(late, 0)),
        )):
            out = lax.dot_general(left, right, (((1,), (1,)), ((), ())), preferred_element_type=F32)
            two = 2 * LANES
            y_ref[pair, p, 0:m] = roll(out[:, :two], -1, 0) + out[:, two:2 * two] + roll(out[:, 2 * two:], 1, 0)

    base = 0
    for tile, size in enumerate(sizes):
        for pair in range(frames // 2):
            for side in range(2):
                lanes = pl.ds(side * LANES, LANES)
                y = {p: y_ref[pair, p, pl.ds(tile * width, width), lanes] for p in (range(6) if size == 4 else (0, 1, 2, 5))}
                plus, minus = y[1] + y[2], y[1] - y[2]
                t = 2 * pair + side
                if size == 4:
                    far, odd = y[3] + y[4], y[3] - y[4]
                    emit(t, base, y[0] + plus + far)
                    emit(t, base + 1, minus + 2.0 * odd)
                    emit(t, base + 2, plus + 4.0 * far)
                    emit(t, base + 3, minus + 8.0 * odd + y[5])
                else:
                    emit(t, base, y[0] + plus)
                    emit(t, base + 1, minus + y[5])
        base += size


def by_parity(par, even, odd, at):
    return jnp.where(par == 0, even[at], odd[at])


def third_kernel(chans, par_ref, cp_ref, ra0, ra1, left, right, rc0, rc1, w_ref, out_ref, x_ref, s_ref, y_ref):
    frames, rows, cols, _ = cp_ref.shape
    width = cols + 2 * SUB
    par = par_ref[0]
    sub = sub_of((SUB, LANES))

    def edges(t, r, lval, rval):
        x_ref[t, r, 0:SUB] = jnp.where(sub >= 5, lval, 0.0)
        x_ref[t, r, width - SUB:width] = jnp.where(sub < 3, rval, 0.0)

    for t in range(frames):
        for h in range(rows):
            x_ref[t, h + 3, SUB:SUB + cols] = cp_ref[t, h]
            edges(t, h + 3, left[t, h], right[t, h])
    for r in range(3):
        for at, even, odd, ceven, codd in ((r, ra1, ra0, rc1, rc0), (r + 3 + rows, ra0, ra1, rc0, rc1)):
            groups = [by_parity(par, even, odd, (g, r)) for g in range(3)]
            for t, frame in enumerate(ungroup_frames(groups, chans)):
                x_ref[t, at, SUB:SUB + cols] = frame
                edges(t, at, by_parity(par, ceven, codd, (t, r, 0)), by_parity(par, ceven, codd, (t, r, 1)))

    def emit(t, o, value):
        out_ref[t, o] = value

    conv(lambda t, r, start, n: x_ref[t, r, pl.ds(start, n)], (4, 4), width, s_ref, y_ref, w_ref, emit)


def last_kernel(chans, par_ref, g_ref, s2_ref, s1_ref, rb0, rb1, left, right, rc0, rc1, w2_ref, w1_ref, out_ref,
                e2_ref, e1_ref, x2_ref, x1_ref, s_ref, y_ref):
    frames, rows, cols, _ = s2_ref.shape
    width = cols + 2 * SUB
    par = par_ref[0]
    sub = sub_of((SUB, LANES))

    def edges2(t, r, lval, rval):
        e2_ref[t, r, 0:SUB] = jnp.where(sub >= 6, roll(lval, 4, 0), 0.0)
        e2_ref[t, r, width - SUB:width] = jnp.where(sub < 2, roll(rval, 4, 0), 0.0)

    def edges1(t, r, lval, rval):
        e1_ref[t, r, 0:SUB] = jnp.where(sub == 7, roll(lval, 6, 0), 0.0)
        e1_ref[t, r, width - SUB:width] = jnp.where(sub == 0, roll(rval, 2, 0), 0.0)

    for t in range(frames):
        for h in range(rows):
            e2_ref[t, h + 2, SUB:SUB + cols] = s2_ref[t, h]
            e1_ref[t, h + 1, SUB:SUB + cols] = s1_ref[t, h]
            edges2(t, h + 2, left[t, h], right[t, h])
            edges1(t, h + 1, left[t, h], right[t, h])
    for top, even, odd, ceven, codd in ((True, rb1, rb0, rc1, rc0), (False, rb0, rb1, rc0, rc1)):
        def corner(t, r, side):
            return by_parity(par, ceven, codd, (t, r, side))

        for r in range(3):
            groups = [by_parity(par, even, odd, (g, r)) for g in range(3)]
            for t, frame in enumerate(ungroup_frames(groups, chans)):
                if r < 2:
                    at, src = (r, r + 1) if top else (r + 2 + rows, r)
                    e2_ref[t, at, SUB:SUB + cols] = frame
                    edges2(t, at, corner(t, src, 0), corner(t, src, 1))
                else:
                    at, src = (0, 2) if top else (1 + rows, 0)
                    e1_ref[t, at, SUB:SUB + cols] = frame
                    edges1(t, at, corner(t, src, 0), corner(t, src, 1))

    def emit2(t, o, value):
        x1_ref[t, o] = value * e1_ref[t, o]

    def emit1(t, o, value):
        out_ref[t, o] = value[SUB:SUB + cols, 0:chans]

    def read2(t, r, start, n):
        return g_ref[t, r, pl.ds(start, n)] * e2_ref[t, r, pl.ds(start, n)]

    conv(read2, (4, 2), width, s_ref, y_ref, w2_ref, emit2)
    conv(lambda t, r, start, n: x1_ref[t, r, pl.ds(start, n)], (4,), width, s_ref, y_ref, w1_ref, emit1)


def swap(value, axis, which):
    count = lax.axis_size(axis)
    pairs = []
    for low in range(which, count - 1, 2):
        pairs += [(low, low + 1), (low + 1, low)]
    return lax.ppermute(value, axis, pairs)


def call(body, out_shape, args, scratch=(), vmem=40 << 20, flops=0, cost=0):
    return pl.pallas_call(
        body,
        out_shape=out_shape,
        in_specs=[SMEM_SPEC if a.dtype == jnp.int32 else VMEM_SPEC for a in args],
        out_specs=jax.tree.map(lambda _: VMEM_SPEC, out_shape),
        scratch_shapes=list(scratch),
        compiler_params=pltpu.CompilerParams(vmem_limit_bytes=vmem),
        cost_estimate=pl.CostEstimate(flops=flops, bytes_accessed=cost, transcendentals=0),
    )(*args)


def local(cotangent, stored_first, stored_second, w_first, w_second, w_third):
    frames, rows, cols, chans = cotangent.shape
    width = cols + 2 * SUB
    par = jnp.stack([lax.axis_index("ha") % 2, lax.axis_index("wa") % 2]).astype(jnp.int32)

    def arr(*shape, dtype=F32):
        return jax.ShapeDtypeStruct(shape, dtype)

    halo = arr(3, 3, cols, LANES)
    edge = arr(frames, rows, SUB, LANES)
    own = arr(frames, rows, cols, LANES)
    ha0, ha1, hb0, hb1, wp0, wp1, cp, s2, s1 = call(
        pack_kernel, (halo, halo, halo, halo, edge, edge, own, own, own), (par, cotangent, stored_second, stored_first)
    )
    ra1, ra0 = swap(ha1, "ha", 1), swap(ha0, "ha", 0)
    rw1, rw0 = swap(wp1, "wa", 1), swap(wp0, "wa", 0)
    rb1, rb0 = swap(hb1, "ha", 1), swap(hb0, "ha", 0)
    corner = arr(frames, 3, 2, SUB, LANES)
    hc0, hc1, left, right = call(corner_kernel, (corner, corner, edge, edge), (par, rw0, rw1))
    rc1, rc0 = swap(hc1, "ha", 1), swap(hc0, "ha", 0)

    weights = arr(6, 3, 2, LANES, 3 * LANES, dtype=BF16)
    u3, u2, u1 = (call(weight_kernel, weights, (w,)) for w in (w_third, w_second, w_first))

    scratch = [pltpu.VMEM((6, 2 * width, 2 * frames * LANES), BF16), pltpu.VMEM((2, 6, 2 * width, 2 * LANES), F32)]
    grad = call(
        functools.partial(third_kernel, chans),
        arr(frames, rows + 4, width, LANES),
        (par, cp, ra0, ra1, left, right, rc0, rc1, u3),
        [pltpu.VMEM((frames, rows + 6, width, LANES), F32)] + scratch,
    )
    return call(
        functools.partial(last_kernel, chans),
        arr(frames, rows, cols, chans),
        (par, grad, s2, s1, rb0, rb1, left, right, rc0, rc1, u2, u1),
        [
            pltpu.VMEM((frames, rows + 4, width, LANES), F32),
            pltpu.VMEM((frames, rows + 2, width, LANES), F32),
            pltpu.VMEM((frames, rows + 4, width, LANES), F32),
            pltpu.VMEM((frames, rows + 2, width, LANES), F32),
        ]
        + scratch,
    )


def solution(mesh):
    in_specs = (
        P("clip", "ha", "wa", None),
        P("clip", "ha", "wa", None),
        P("clip", "ha", "wa", None),
        P(),
        P(),
        P(),
    )
    out_specs = P("clip", "ha", "wa", None)
    return jax.shard_map(local, mesh=mesh, in_specs=in_specs, out_specs=out_specs, check_vma=False)
```

```python
import functools

import jax
import jax.numpy as jnp
from jax import lax
from jax.experimental import pallas as pl
from jax.experimental.pallas import tpu as pltpu
from jax.sharding import PartitionSpec as P

LANES = 128
SUB = 8
F32 = jnp.float32
BF16 = jnp.bfloat16
VMEM_SPEC = pl.BlockSpec(memory_space=pltpu.VMEM)
SMEM_SPEC = pl.BlockSpec(memory_space=pltpu.SMEM)


def silu_slope(value):
    sigma = 1.0 / (1.0 + jnp.exp(-value))
    return sigma * (1.0 + value * (1.0 - sigma))


def roll(value, shift, axis):
    return pltpu.roll(value, shift % value.shape[axis], axis)


def lane_of(shape):
    return lax.broadcasted_iota(jnp.int32, shape, len(shape) - 1)


def sub_of(shape):
    return lax.broadcasted_iota(jnp.int32, shape, len(shape) - 2)


def group_frames(frames, chans):
    first, second, third, fourth = frames
    part = LANES - chans
    lane = lane_of(first.shape)
    packed = []
    for index, frame in enumerate((first, second, third)):
        packed.append(jnp.where(lane < chans, frame, roll(fourth, chans - part * index, 1)))
    return packed


def ungroup_frames(groups, chans):
    part = LANES - chans
    lane = lane_of(groups[0].shape)
    frames = [jnp.where(lane < chans, group, 0.0) for group in groups]
    fourth = jnp.zeros_like(groups[0])
    for index in reversed(range(3)):
        moved = roll(groups[index], part * (index + 1), 1)
        fourth = jnp.where(lane < part * (index + 1), moved, fourth)
    return frames + [jnp.where(lane < chans, fourth, 0.0)]


def edge_kernel(par_ref, cot_hbm, sec_hbm, fst_hbm, wp0, wp1, raw_ref, pad_ref, sems):
    frames, rows, cols, chans = cot_hbm.shape
    copies = []
    for a, src in enumerate((cot_hbm, sec_hbm, fst_hbm)):
        for side, start in enumerate((0, cols - SUB)):
            copies.append(
                pltpu.make_async_copy(src.at[:, :, pl.ds(start, SUB), :], raw_ref.at[a, side], sems.at[a, side])
            )
            copies[-1].start()
    pad_ref[...] = jnp.zeros(pad_ref.shape, F32)
    for copy in copies:
        copy.wait()
    pad_ref[0, :, :, :, :, 0:chans] = raw_ref[0]
    pad_ref[1:3, :, :, :, :, 0:chans] = silu_slope(raw_ref[1:3])

    def cols_out(left, right):
        sub = sub_of((SUB, LANES))
        for t in range(frames):
            for h in range(rows):
                c0, a0, b0 = (pad_ref[a, 0, t, h] for a in range(3))
                c7, a7, b7 = (pad_ref[a, 1, t, h] for a in range(3))
                right[t, h] = jnp.where(
                    sub >= 5, c7, jnp.where((sub == 2) | (sub == 3), roll(a7, 4, 0), jnp.where(sub == 1, roll(b7, 2, 0), 0.0))
                )
                left[t, h] = jnp.where(
                    sub < 3, c0, jnp.where((sub == 4) | (sub == 5), roll(a0, 4, 0), jnp.where(sub == 6, roll(b0, 6, 0), 0.0))
                )

    @pl.when(par_ref[1] == 0)
    def _():
        cols_out(wp1, wp0)

    @pl.when(par_ref[1] != 0)
    def _():
        cols_out(wp0, wp1)


def put_rows(read_cot, read_s2, read_s1, rows, top_a, top_b, low_a, low_b, span, chans):
    def put(read, h, dst, at):
        for g, val in enumerate(group_frames([read(t, h) for t in range(4)], chans)):
            dst[g, at, span] = val

    for r in range(3):
        put(read_cot, r, top_a, r)
        put(read_cot, rows - 3 + r, low_a, r)
    for r in range(2):
        put(read_s2, r, top_b, r)
        put(read_s2, rows - 2 + r, low_b, r)
    put(read_s1, 0, top_b, 2)
    put(read_s1, rows - 1, low_b, 2)


def pack_kernel(par_ref, cot_ref, sec_ref, fst_ref, ma0, ma1, mb0, mb1, cp_ref, s2_ref, s1_ref):
    frames, rows, cols, chans = cot_ref.shape
    blank = jnp.zeros((cols, LANES), F32)
    for t in range(frames):
        for h in range(rows):
            for ref, val in ((cp_ref, cot_ref[t, h]), (s2_ref, silu_slope(sec_ref[t, h])), (s1_ref, silu_slope(fst_ref[t, h]))):
                ref[t, h] = blank
                ref[t, h, :, 0:chans] = val

    def rows_out(*dst):
        reads = [lambda t, h, ref=ref: ref[t, h] for ref in (cp_ref, s2_ref, s1_ref)]
        put_rows(*reads, rows, *dst, slice(0, cols), chans)

    @pl.when(par_ref[0] == 0)
    def _():
        rows_out(ma1, mb1, ma0, mb0)

    @pl.when(par_ref[0] != 0)
    def _():
        rows_out(ma0, mb0, ma1, mb1)


def corner_kernel(chans, par_ref, rw0, rw1, _a0, _a1, _b0, _b1, ma0, ma1, mb0, mb1, cc, c2, c1):
    frames, rows = rw0.shape[:2]
    cols = ma0.shape[2] - SUB
    even = par_ref[1] == 0
    sub = sub_of((SUB, LANES))
    for t in range(frames):
        for h in range(rows):
            left = jnp.where(even, rw1[t, h], rw0[t, h])
            right = jnp.where(even, rw0[t, h], rw1[t, h])
            cc[t, h] = jnp.where(sub < 3, right, jnp.where(sub >= 5, left, 0.0))
            c2[t, h] = jnp.where(sub < 2, roll(right, 4, 0), jnp.where(sub >= 6, roll(left, 4, 0), 0.0))
            c1[t, h] = jnp.where(sub == 0, roll(right, 2, 0), jnp.where(sub == 7, roll(left, 6, 0), 0.0))

    def rows_out(*dst):
        reads = [lambda t, h, ref=ref: ref[t, h] for ref in (cc, c2, c1)]
        put_rows(*reads, rows, *dst, slice(cols, cols + SUB), chans)

    @pl.when(par_ref[0] == 0)
    def _():
        rows_out(ma1, mb1, ma0, mb0)

    @pl.when(par_ref[0] != 0)
    def _():
        rows_out(ma0, mb0, ma1, mb1)


def weight_kernel(w_ref, out_ref):
    chans = w_ref.shape[3]
    out_ref[...] = jnp.zeros(out_ref.shape, BF16)
    for k in range(3):
        for i in range(3):
            f0, f1, f2 = (w_ref[i, 2 - m, k] for m in range(3))
            even, odd = (f0 + f2) * (1 / 6), f1 * (1 / 6)
            far, odd2 = f0 * (1 / 24) + f2 * (1 / 6), f1 * (1 / 12)
            points = (f0 * 0.25, -even - odd, odd - even, far + odd2, far - odd2, f2)
            lanes = pl.ds((2 - i) * LANES, chans)
            for p, u in enumerate(points):
                high = u.astype(BF16)
                out_ref[p, k, 0, 0:chans, lanes] = high
                out_ref[p, k, 1, 0:chans, lanes] = (u - high.astype(F32)).astype(BF16)


def transform(rows, sizes, store):
    base = 0
    for tile, size in enumerate(sizes):
        if size == 4:
            x0, x1, x2, x3, x4, x5 = (rows(base + r) for r in range(6))
            a, b = x4 - 4.0 * x2, x3 - 4.0 * x1
            c, e = x4 - x2, 2.0 * (x3 - x1)
            points = ((4.0 * x0 - 5.0 * x2 + x4, 0), (a + b, 1), (a - b, 2), (c + e, 3), (c - e, 4),
                      (4.0 * x1 - 5.0 * x3 + x5, 5))
        else:
            x0, x1, x2, x3 = (rows(base + r) for r in range(4))
            points = ((4.0 * (x0 - x2), 0), (-3.0 * (x1 + x2), 1), (-3.0 * (x2 - x1), 2), (x3 - x1, 5))
        for value, point in points:
            store(point, tile, value)
        base += size


def right_operands(w_ref, p):
    zero = jnp.zeros((LANES, LANES), BF16)
    near, far = [], []
    for k in range(3):
        parts = [w_ref[p, k, part] for part in range(2)]
        own = [
            jnp.concatenate([r[:, : 2 * LANES], jnp.concatenate([zero, r[:, :LANES]], 1)], 0) for r in parts
        ]
        later = [
            jnp.concatenate([jnp.concatenate([r[:, 2 * LANES :], zero], 1), r[:, LANES:]], 0) for r in parts
        ]
        near.append(jnp.concatenate([own[0], own[0], own[1]], 1))
        far.append(jnp.concatenate([later[0], later[0], later[1]], 1))
    return jnp.concatenate(near, 0), jnp.concatenate(far, 0)


def product(left, right):
    left = jnp.concatenate([left, left[:, : 2 * LANES]], 1)
    return lax.dot_general(left, right, (((1,), (1,)), ((), ())), preferred_element_type=F32)


def shifted_sum(taps):
    two = 2 * LANES
    return roll(taps[:, :two], -1, 0) + taps[:, two : 2 * two] + roll(taps[:, 2 * two :], 1, 0)


def conv(read, sizes, width, s_ref, y_ref, w_ref, emit):
    chunks = width // SUB

    def tiles_of(p):
        return [n for n, size in enumerate(sizes) if size == 4 or p in (0, 1, 2, 5)]

    def one(c, carry):
        at = pl.ds(pl.multiple_of(c * SUB, SUB), SUB)
        for a in range(2):
            found = {}
            for pair in range(2):
                def store(point, tile, value):
                    found[pair, point, tile] = value

                transform(lambda r: read(2 * pair + a, r, at), sizes, store)
            for p in range(6):
                tiles = tiles_of(p)
                if len(tiles) == 2:
                    blocks = [jnp.concatenate([found[pair, p, n] for n in tiles], 0) for pair in range(2)]
                else:
                    blocks = [jnp.concatenate([found[pair, p, tiles[0]] for pair in range(2)], 0)]
                for n, value in enumerate(blocks):
                    high = value.astype(BF16)
                    s_ref[p, c, n, :, a * LANES : (a + 1) * LANES] = high
                    s_ref[p, c, n, :, (2 + a) * LANES : (3 + a) * LANES] = (value - high.astype(F32)).astype(BF16)
        return carry

    lax.fori_loop(0, chunks, one, 0)

    wide = 4 * LANES
    for p in range(6):
        near, far = right_operands(w_ref, p)
        tiles = tiles_of(p)
        if len(tiles) == 2:
            own = product(s_ref[p].reshape(chunks * 4 * SUB, wide), near).reshape(chunks, 2, 2, SUB, 6 * LANES)
            later = product(s_ref[p, :, 1].reshape(chunks * 2 * SUB, wide), far).reshape(chunks, 2, SUB, 6 * LANES)
            for n in tiles:
                y_ref[0, p, n] = shifted_sum((own[:, 0, n] + later[:, n]).reshape(width, 6 * LANES))
                y_ref[1, p, n] = shifted_sum(own[:, 1, n].reshape(width, 6 * LANES))
        else:
            lhs = s_ref[p, :, 0].reshape(chunks * 2 * SUB, wide)
            own = product(lhs, near).reshape(chunks, 2, SUB, 6 * LANES)
            later = product(lhs, far).reshape(chunks, 2, SUB, 6 * LANES)
            y_ref[0, p, tiles[0]] = shifted_sum((own[:, 0] + later[:, 1]).reshape(width, 6 * LANES))
            y_ref[1, p, tiles[0]] = shifted_sum(own[:, 1].reshape(width, 6 * LANES))

    base = 0
    for tile, size in enumerate(sizes):
        for t in range(4):
            lanes = pl.ds(t % 2 * LANES, LANES)
            y = {p: y_ref[t // 2, p, tile, :, lanes] for p in (range(6) if size == 4 else (0, 1, 2, 5))}
            plus, minus = y[1] + y[2], y[1] - y[2]
            if size == 4:
                far, odd = y[3] + y[4], y[3] - y[4]
                emit(t, base, y[0] + plus + far)
                emit(t, base + 1, minus + 2.0 * odd)
                emit(t, base + 2, plus + 4.0 * far)
                emit(t, base + 3, minus + 8.0 * odd + y[5])
            else:
                emit(t, base, y[0] + plus)
                emit(t, base + 1, minus + y[5])
        base += size


def halo_rows(chans, par, from_even, from_odd, r):
    return ungroup_frames([jnp.where(par == 0, from_even[g, r], from_odd[g, r]) for g in range(3)], chans)


def third_kernel(chans, par_ref, cp_ref, cc_ref, ra0, ra1, w_ref, out_ref, x_ref, s_ref, y_ref):
    frames, rows, cols, _ = cp_ref.shape
    width = cols + SUB
    par = par_ref[0]
    x_ref[:, 3 : 3 + rows, 0:cols] = cp_ref[...]
    x_ref[:, 3 : 3 + rows, cols:width] = cc_ref[...]
    for r in range(3):
        for at, even, odd in ((r, ra1, ra0), (r + 3 + rows, ra0, ra1)):
            for t, frame in enumerate(halo_rows(chans, par, even, odd, r)):
                x_ref[t, at] = frame

    def emit(t, o, value):
        out_ref[t, o] = value

    conv(lambda t, r, at: x_ref[t, r, at], (4, 4), width, s_ref, y_ref, w_ref, emit)


def last_kernel(chans, par_ref, g_ref, s2_ref, c2_ref, s1_ref, c1_ref, rb0, rb1, w2_ref, w1_ref, out_ref,
                e2_ref, e1_ref, x1_ref, s_ref, y_ref):
    frames, rows, cols, _ = s2_ref.shape
    width = cols + SUB
    par = par_ref[0]
    for e_ref, s_own, c_own, n in ((e2_ref, s2_ref, c2_ref, 2), (e1_ref, s1_ref, c1_ref, 1)):
        e_ref[:, n : n + rows, 0:cols] = s_own[...]
        e_ref[:, n : n + rows, cols:width] = c_own[...]
    for r in range(3):
        for top, even, odd in ((True, rb1, rb0), (False, rb0, rb1)):
            for t, frame in enumerate(halo_rows(chans, par, even, odd, r)):
                if r < 2:
                    e2_ref[t, r if top else r + 2 + rows] = frame
                else:
                    e1_ref[t, 0 if top else 1 + rows] = frame

    def emit2(t, o, value):
        x1_ref[t, o] = value * e1_ref[t, o]

    def emit1(t, o, value):
        out_ref[t, o] = value[0:cols, 0:chans]

    conv(lambda t, r, at: g_ref[t, r, at] * e2_ref[t, r, at], (4, 2), width, s_ref, y_ref, w2_ref, emit2)
    conv(lambda t, r, at: x1_ref[t, r, at], (4,), width, s_ref, y_ref, w1_ref, emit1)


def swap(value, axis, which):
    count = lax.axis_size(axis)
    pairs = []
    for low in range(which, count - 1, 2):
        pairs += [(low, low + 1), (low + 1, low)]
    return lax.ppermute(value, axis, pairs)


def call(body, out_shape, args, scratch=(), hbm=False, alias=None, vmem=40 << 20, flops=0, cost=0):
    where = pl.BlockSpec(memory_space=pltpu.HBM) if hbm else VMEM_SPEC
    return pl.pallas_call(
        body,
        out_shape=out_shape,
        in_specs=[SMEM_SPEC if a.dtype == jnp.int32 else where for a in args],
        out_specs=jax.tree.map(lambda _: VMEM_SPEC, out_shape),
        scratch_shapes=list(scratch),
        input_output_aliases=alias or {},
        compiler_params=pltpu.CompilerParams(vmem_limit_bytes=vmem),
        cost_estimate=pl.CostEstimate(flops=flops, bytes_accessed=cost, transcendentals=0),
    )(*args)


def local(cotangent, stored_first, stored_second, w_first, w_second, w_third):
    frames, rows, cols, chans = cotangent.shape
    width = cols + SUB
    par = jnp.stack([lax.axis_index("ha") % 2, lax.axis_index("wa") % 2]).astype(jnp.int32)

    def arr(*shape, dtype=F32):
        return jax.ShapeDtypeStruct(shape, dtype)

    def vmem(*shape, dtype=F32):
        return pltpu.VMEM(shape, dtype)

    edge = arr(frames, rows, SUB, LANES)
    own = arr(frames, rows, cols, LANES)
    message = arr(3, 3, width, LANES)
    fields = (cotangent, stored_second, stored_first)
    wp0, wp1 = call(
        edge_kernel,
        (edge, edge),
        (par,) + fields,
        [vmem(3, 2, frames, rows, SUB, chans), vmem(3, 2, frames, rows, SUB, LANES), pltpu.SemaphoreType.DMA((3, 2))],
        hbm=True,
    )
    rw1 = swap(wp1, "wa", 1)
    rw0 = swap(wp0, "wa", 0)
    ma0, ma1, mb0, mb1, cp, s2, s1 = call(pack_kernel, (message,) * 4 + (own,) * 3, (par,) + fields)
    ma0, ma1, mb0, mb1, cc, c2, c1 = call(
        functools.partial(corner_kernel, chans),
        (message,) * 4 + (edge,) * 3,
        (par, rw0, rw1, ma0, ma1, mb0, mb1),
        alias={3: 0, 4: 1, 5: 2, 6: 3},
    )
    ra1 = swap(ma1, "ha", 1)
    ra0 = swap(ma0, "ha", 0)
    rb1 = swap(mb1, "ha", 1)
    rb0 = swap(mb0, "ha", 0)

    weights = arr(6, 3, 2, LANES, 3 * LANES, dtype=BF16)
    u3, u2, u1 = (call(weight_kernel, weights, (w,)) for w in (w_third, w_second, w_first))

    scratch = [
        vmem(6, width // SUB, 2, 2 * SUB, 4 * LANES, dtype=BF16),
        vmem(2, 6, 2, width, 2 * LANES),
    ]
    grad = call(
        functools.partial(third_kernel, chans),
        arr(frames, rows + 4, width, LANES),
        (par, cp, cc, ra0, ra1, u3),
        [vmem(frames, rows + 6, width, LANES)] + scratch,
    )
    return call(
        functools.partial(last_kernel, chans),
        arr(frames, rows, cols, chans),
        (par, grad, s2, c2, s1, c1, rb0, rb1, u2, u1),
        [
            vmem(frames, rows + 4, width, LANES),
            vmem(frames, rows + 2, width, LANES),
            vmem(frames, rows + 2, width, LANES),
        ]
        + scratch,
    )


def solution(mesh):
    in_specs = (
        P("clip", "ha", "wa", None),
        P("clip", "ha", "wa", None),
        P("clip", "ha", "wa", None),
        P(),
        P(),
        P(),
    )
    out_specs = P("clip", "ha", "wa", None)
    return jax.shard_map(local, mesh=mesh, in_specs=in_specs, out_specs=out_specs, check_vma=False)
```

```python
import functools

import jax
import jax.numpy as jnp
from jax import lax
from jax.experimental import pallas as pl
from jax.experimental.pallas import tpu as pltpu
from jax.sharding import PartitionSpec as P

LANES = 128
SUB = 8
F32 = jnp.float32
BF16 = jnp.bfloat16
VMEM_SPEC = pl.BlockSpec(memory_space=pltpu.VMEM)
SMEM_SPEC = pl.BlockSpec(memory_space=pltpu.SMEM)


def silu_slope(value):
    sigma = 1.0 / (1.0 + jnp.exp(-value))
    return sigma * (1.0 + value * (1.0 - sigma))


def roll(value, shift, axis):
    return pltpu.roll(value, shift % value.shape[axis], axis)


def lane_of(shape):
    return lax.broadcasted_iota(jnp.int32, shape, len(shape) - 1)


def sub_of(shape):
    return lax.broadcasted_iota(jnp.int32, shape, len(shape) - 2)


def group_frames(frames, chans):
    first, second, third, fourth = frames
    part = LANES - chans
    lane = lane_of(first.shape)
    packed = []
    for index, frame in enumerate((first, second, third)):
        packed.append(jnp.where(lane < chans, frame, roll(fourth, chans - part * index, 1)))
    return packed


def ungroup_frames(groups, chans):
    part = LANES - chans
    lane = lane_of(groups[0].shape)
    frames = [jnp.where(lane < chans, group, 0.0) for group in groups]
    fourth = jnp.zeros_like(groups[0])
    for index in reversed(range(3)):
        moved = roll(groups[index], part * (index + 1), 1)
        fourth = jnp.where(lane < part * (index + 1), moved, fourth)
    return frames + [jnp.where(lane < chans, fourth, 0.0)]


def edge_kernel(par_ref, cot_hbm, sec_hbm, fst_hbm, wp0, wp1, raw_ref, pad_ref, sems):
    frames, rows, cols, chans = cot_hbm.shape
    copies = []
    for a, src in enumerate((cot_hbm, sec_hbm, fst_hbm)):
        for side, start in enumerate((0, cols - SUB)):
            copies.append(
                pltpu.make_async_copy(src.at[:, :, pl.ds(start, SUB), :], raw_ref.at[a, side], sems.at[a, side])
            )
            copies[-1].start()
    pad_ref[...] = jnp.zeros(pad_ref.shape, F32)
    for copy in copies:
        copy.wait()
    pad_ref[0, :, :, :, :, 0:chans] = raw_ref[0]
    pad_ref[1:3, :, :, :, :, 0:chans] = silu_slope(raw_ref[1:3])

    def cols_out(left, right):
        sub = sub_of((SUB, LANES))
        for t in range(frames):
            for h in range(rows):
                c0, a0, b0 = (pad_ref[a, 0, t, h] for a in range(3))
                c7, a7, b7 = (pad_ref[a, 1, t, h] for a in range(3))
                right[t, h] = jnp.where(
                    sub >= 5, c7, jnp.where((sub == 2) | (sub == 3), roll(a7, 4, 0), jnp.where(sub == 1, roll(b7, 2, 0), 0.0))
                )
                left[t, h] = jnp.where(
                    sub < 3, c0, jnp.where((sub == 4) | (sub == 5), roll(a0, 4, 0), jnp.where(sub == 6, roll(b0, 6, 0), 0.0))
                )

    @pl.when(par_ref[1] == 0)
    def _():
        cols_out(wp1, wp0)

    @pl.when(par_ref[1] != 0)
    def _():
        cols_out(wp0, wp1)


def put_rows(read_cot, read_s2, read_s1, rows, top_a, top_b, low_a, low_b, span, chans):
    def put(read, h, dst, at):
        for g, val in enumerate(group_frames([read(t, h) for t in range(4)], chans)):
            dst[g, at, span] = val

    for r in range(3):
        put(read_cot, r, top_a, r)
        put(read_cot, rows - 3 + r, low_a, r)
    for r in range(2):
        put(read_s2, r, top_b, r)
        put(read_s2, rows - 2 + r, low_b, r)
    put(read_s1, 0, top_b, 2)
    put(read_s1, rows - 1, low_b, 2)


def pack_kernel(par_ref, cot_ref, sec_ref, fst_ref, ma0, ma1, mb0, mb1, cp_ref, s2_ref, s1_ref):
    frames, rows, cols, chans = cot_ref.shape
    outs = (cp_ref, s2_ref, s1_ref)
    blank = jnp.zeros((cols, LANES), F32)
    for a, ref in enumerate(outs):
        for t in range(frames):
            for h in range(rows):
                value = (cot_ref, sec_ref, fst_ref)[a][t, h]
                ref[t, h, 0:cols] = blank
                ref[t, h, 0:cols, 0:chans] = silu_slope(value) if a else value

    def rows_out(*dst):
        reads = [lambda t, h, ref=ref: ref[t, h, 0:cols] for ref in outs]
        put_rows(*reads, rows, *dst, slice(0, cols), chans)

    @pl.when(par_ref[0] == 0)
    def _():
        rows_out(ma1, mb1, ma0, mb0)

    @pl.when(par_ref[0] != 0)
    def _():
        rows_out(ma0, mb0, ma1, mb1)


def corner_kernel(chans, par_ref, rw0, rw1, _a0, _a1, _b0, _b1, _c, _s2, _s1, ma0, ma1, mb0, mb1, cp_ref, s2_ref, s1_ref):
    frames, rows = rw0.shape[:2]
    cols = ma0.shape[2] - SUB
    even = par_ref[1] == 0
    sub = sub_of((SUB, LANES))
    for t in range(frames):
        for h in range(rows):
            left = jnp.where(even, rw1[t, h], rw0[t, h])
            right = jnp.where(even, rw0[t, h], rw1[t, h])
            cp_ref[t, h, cols:] = jnp.where(sub < 3, right, jnp.where(sub >= 5, left, 0.0))
            s2_ref[t, h, cols:] = jnp.where(sub < 2, roll(right, 4, 0), jnp.where(sub >= 6, roll(left, 4, 0), 0.0))
            s1_ref[t, h, cols:] = jnp.where(sub == 0, roll(right, 2, 0), jnp.where(sub == 7, roll(left, 6, 0), 0.0))

    def rows_out(*dst):
        reads = [lambda t, h, ref=ref: ref[t, h, cols:] for ref in (cp_ref, s2_ref, s1_ref)]
        put_rows(*reads, rows, *dst, slice(cols, cols + SUB), chans)

    @pl.when(par_ref[0] == 0)
    def _():
        rows_out(ma1, mb1, ma0, mb0)

    @pl.when(par_ref[0] != 0)
    def _():
        rows_out(ma0, mb0, ma1, mb1)


def weight_kernel(wanted, w_ref, out_ref):
    chans = w_ref.shape[3]
    out_ref[...] = jnp.zeros(out_ref.shape, BF16)
    for k in range(3):
        for i in range(3):
            f0, f1, f2 = (w_ref[i, 2 - m, k] for m in range(3))
            even, odd = (f0 + f2) * (1 / 6), f1 * (1 / 6)
            far, odd2 = f0 * (1 / 24) + f2 * (1 / 6), f1 * (1 / 12)
            points = (f0 * 0.25, -even - odd, odd - even, far + odd2, far - odd2, f2)
            lanes = pl.ds((2 - i) * LANES, chans)
            for n, p in enumerate(wanted):
                u = points[p]
                high = u.astype(BF16)
                out_ref[n, k, 0, 0:chans, lanes] = high
                out_ref[n, k, 1, 0:chans, lanes] = (u - high.astype(F32)).astype(BF16)


POINTS = {2: (0, 1, 2, 5), 3: (0, 1, 2, 3, 5), 4: (0, 1, 2, 3, 4, 5)}


def transform(x, size):
    if size == 2:
        return 4.0 * (x[0] - x[2]), -3.0 * (x[1] + x[2]), 3.0 * (x[1] - x[2]), x[3] - x[1]
    if size == 3:
        a, b = x[3] - x[1], x[3] - 2.0 * x[1]
        return (
            4.0 * (x[0] - x[2]) + 2.0 * a,
            3.0 * (b - x[2]),
            2.0 * x[1] - 3.0 * x[2] + x[3],
            4.0 * a,
            x[4] - x[2] - 2.0 * a,
        )
    a, b = x[4] - 4.0 * x[2], x[3] - 4.0 * x[1]
    c, e = x[4] - x[2], 2.0 * (x[3] - x[1])
    return 4.0 * x[0] - 5.0 * x[2] + x[4], a + b, a - b, c + e, c - e, 4.0 * x[1] - 5.0 * x[3] + x[5]


def outputs(y, size):
    plus, minus = y[1] + y[2], y[1] - y[2]
    if size == 2:
        return y[0] + plus, minus + y[3]
    if size == 3:
        return y[0] + plus + y[3], minus + 2.0 * y[3], plus + 4.0 * y[3] + y[4]
    far, odd = y[3] + y[4], y[3] - y[4]
    return y[0] + plus + far, minus + 2.0 * odd, plus + 4.0 * far, minus + 8.0 * odd + y[5]


def right_operands(w_ref, p):
    zero = jnp.zeros((LANES, LANES), BF16)
    near, far = [], []
    for k in range(3):
        parts = [w_ref[p, k, part] for part in range(2)]
        own = [
            jnp.concatenate([r[:, : 2 * LANES], jnp.concatenate([zero, r[:, :LANES]], 1)], 0) for r in parts
        ]
        later = [
            jnp.concatenate([jnp.concatenate([r[:, 2 * LANES :], zero], 1), r[:, LANES:]], 0) for r in parts
        ]
        near.append(jnp.concatenate([own[0], own[0], own[1]], 1))
        far.append(jnp.concatenate([later[0], later[0], later[1]], 1))
    return jnp.concatenate(near, 0), jnp.concatenate(far, 0)


def product(left, right):
    left = jnp.concatenate([left, left[:, : 2 * LANES]], 1)
    return lax.dot_general(left, right, (((1,), (1,)), ((), ())), preferred_element_type=F32)


def shifted_sum(taps):
    two = 2 * LANES
    return roll(taps[:, :two], -1, 0) + taps[:, two : 2 * two] + roll(taps[:, 2 * two :], 1, 0)


def conv(read, size, width, s_ref, y_ref, w_ref, emit, done=None):
    chunks = width // SUB
    points = len(POINTS[size])

    def one(c, carry):
        at = pl.ds(pl.multiple_of(c * SUB, SUB), SUB)
        for t in range(4):
            pair, a = t // 2, t % 2
            x = [read(t, r, at) for r in range(2 * size + 2)]
            for p, pieces in enumerate(zip(transform(x[: size + 2], size), transform(x[size:], size))):
                value = jnp.concatenate(pieces, 0)
                high = value.astype(BF16)
                s_ref[p, c, pair, :, a * LANES : (a + 1) * LANES] = high
                s_ref[p, c, pair, :, (2 + a) * LANES : (3 + a) * LANES] = (value - high.astype(F32)).astype(BF16)
        return carry

    lax.fori_loop(0, chunks, one, 0)

    wide = 4 * LANES
    for p in range(points):
        near, far = right_operands(w_ref, p)
        own = product(s_ref[p].reshape(chunks * 4 * SUB, wide), near).reshape(chunks, 2, 2, SUB, 6 * LANES)
        later = product(s_ref[p, :, 1].reshape(chunks * 2 * SUB, wide), far).reshape(chunks, 2, SUB, 6 * LANES)
        for n in range(2):
            y_ref[0, p, n] = shifted_sum((own[:, 0, n] + later[:, n]).reshape(width, 6 * LANES))
            y_ref[1, p, n] = shifted_sum(own[:, 1, n].reshape(width, 6 * LANES))

    for t in range(4):
        lanes = pl.ds(t % 2 * LANES, LANES)
        for tile in range(2):
            rows = outputs([y_ref[t // 2, p, tile, :, lanes] for p in range(points)], size)
            for o, value in enumerate(rows):
                emit(t, tile * size + o, value)
        if done is not None:
            done(t)


def halo_rows(chans, par, from_even, from_odd, r):
    return ungroup_frames([jnp.where(par == 0, from_even[g, r], from_odd[g, r]) for g in range(3)], chans)


def third_kernel(chans, par_ref, cp_ref, ra0, ra1, w_ref, out_ref, x_ref, s_ref, y_ref):
    rows, width = cp_ref.shape[1:3]
    for r in range(3):
        for at, even, odd in ((r, ra1, ra0), (r + 3, ra0, ra1)):
            for t, frame in enumerate(halo_rows(chans, par_ref[0], even, odd, r)):
                x_ref[t, at] = frame

    def read(t, r, at):
        if 3 <= r < 3 + rows:
            return cp_ref[t, r - 3, at]
        return x_ref[t, r if r < 3 else r - rows, at]

    def emit(t, o, value):
        out_ref[t, o] = value

    conv(read, rows, width, s_ref, y_ref, w_ref, emit)


def last_kernel(chans, par_ref, g_ref, s2_ref, s1_ref, rb0, rb1, w2_ref, w1_ref, out_hbm,
                e_ref, x1_ref, s_ref, y_ref, stage_ref, sems):
    frames, rows, width, _ = s2_ref.shape
    cols = width - SUB
    for r in range(3):
        for side, even, odd in ((0, rb1, rb0), (1, rb0, rb1)):
            for t, frame in enumerate(halo_rows(chans, par_ref[0], even, odd, r)):
                e_ref[side, r, t] = frame

    def slope2(t, r, at):
        if 2 <= r < 2 + rows:
            return s2_ref[t, r - 2, at]
        return e_ref[0, r, t, at] if r < 2 else e_ref[1, r - 2 - rows, t, at]

    def emit2(t, o, value):
        slope = s1_ref[t, o - 1] if 1 <= o < 1 + rows else e_ref[0 if o < 1 else 1, 2, t]
        x1_ref[t, o] = value * slope

    def emit1(t, o, value):
        stage_ref[t, o] = value[0:cols, 0:chans]

    def copy_out(t):
        return pltpu.make_async_copy(stage_ref.at[t], out_hbm.at[t], sems.at[t])

    conv(lambda t, r, at: g_ref[t, r, at] * slope2(t, r, at), (rows + 2) // 2, width, s_ref, y_ref, w2_ref, emit2)
    conv(
        lambda t, r, at: x1_ref[t, r, at], rows // 2, width, s_ref, y_ref, w1_ref, emit1, lambda t: copy_out(t).start()
    )
    for t in range(frames):
        copy_out(t).wait()


def swap(value, axis, which):
    count = lax.axis_size(axis)
    pairs = []
    for low in range(1 - which, count - 1, 2):
        pairs += [(low, low + 1), (low + 1, low)]
    return lax.ppermute(value, axis, pairs)


def swaps(first, second, axis):
    got = swap(first, axis, 0), swap(second, axis, 1)
    return got


def call(body, out_shape, args, scratch=(), hbm=False, hbm_out=False, alias=None, vmem=40 << 20, flops=0, cost=0):
    hbm_spec = pl.BlockSpec(memory_space=pltpu.HBM)
    where, out = hbm_spec if hbm else VMEM_SPEC, hbm_spec if hbm_out else VMEM_SPEC
    return pl.pallas_call(
        body,
        out_shape=out_shape,
        in_specs=[SMEM_SPEC if a.dtype == jnp.int32 else where for a in args],
        out_specs=jax.tree.map(lambda _: out, out_shape),
        scratch_shapes=list(scratch),
        input_output_aliases=alias or {},
        compiler_params=pltpu.CompilerParams(vmem_limit_bytes=vmem),
        cost_estimate=pl.CostEstimate(flops=flops, bytes_accessed=cost, transcendentals=0),
    )(*args)


def local(cotangent, stored_first, stored_second, w_first, w_second, w_third):
    frames, rows, cols, chans = cotangent.shape
    width = cols + SUB
    par = jnp.stack([(lax.axis_index("ha") + 1) % 2, (lax.axis_index("wa") + 1) % 2]).astype(jnp.int32)

    def arr(*shape, dtype=F32):
        return jax.ShapeDtypeStruct(shape, dtype)

    def vmem(*shape, dtype=F32):
        return pltpu.VMEM(shape, dtype)

    edge = arr(frames, rows, SUB, LANES)
    own = arr(frames, rows, width, LANES)
    message = arr(3, 3, width, LANES)
    fields = (cotangent, stored_second, stored_first)
    wp0, wp1 = call(
        edge_kernel,
        (edge, edge),
        (par,) + fields,
        [vmem(3, 2, frames, rows, SUB, chans), vmem(3, 2, frames, rows, SUB, LANES), pltpu.SemaphoreType.DMA((3, 2))],
        hbm=True,
        vmem=66_700_000,
    )
    rw0, rw1 = swaps(wp0, wp1, "wa")
    packed = call(
        pack_kernel,
        (message,) * 4 + (own,) * 3,
        (par,) + fields,
    )
    ma0, ma1, mb0, mb1, cp, s2, s1 = call(
        functools.partial(corner_kernel, chans),
        (message,) * 4 + (own,) * 3,
        (par, rw0, rw1) + tuple(packed),
        alias={n + 3: n for n in range(7)},
    )
    ra0, ra1 = swaps(ma0, ma1, "ha")
    rb0, rb1 = swaps(mb0, mb1, "ha")

    def prepare(w, size):
        points = POINTS[size]
        shape = arr(len(points), 3, 2, LANES, 3 * LANES, dtype=BF16)
        return call(functools.partial(weight_kernel, points), shape, (w,))

    u3, u2, u1 = prepare(w_third, rows), prepare(w_second, (rows + 2) // 2), prepare(w_first, rows // 2)

    def scratch(size):
        points = len(POINTS[size])
        return [
            vmem(points, width // SUB, 2, 2 * SUB, 4 * LANES, dtype=BF16),
            vmem(2, points, 2, width, 2 * LANES),
        ]

    grad = call(
        functools.partial(third_kernel, chans),
        arr(frames, rows + 4, width, LANES),
        (par, cp, ra0, ra1, u3),
        [vmem(frames, 6, width, LANES)] + scratch(rows),
    )
    return call(
        functools.partial(last_kernel, chans),
        arr(frames, rows, cols, chans),
        (par, grad, s2, s1, rb0, rb1, u2, u1),
        [vmem(2, 3, frames, width, LANES), vmem(frames, rows + 2, width, LANES)]
        + scratch((rows + 2) // 2)
        + [vmem(frames, rows, cols, chans), pltpu.SemaphoreType.DMA((frames,))],
        hbm_out=True,
    )


def solution(mesh):
    in_specs = (
        P("clip", "ha", "wa", None),
        P("clip", "ha", "wa", None),
        P("clip", "ha", "wa", None),
        P(),
        P(),
        P(),
    )
    out_specs = P("clip", "ha", "wa", None)
    return jax.shard_map(local, mesh=mesh, in_specs=in_specs, out_specs=out_specs, check_vma=False)
```

```python
import functools

import jax
import jax.numpy as jnp
from jax import lax
from jax.experimental import pallas as pl
from jax.experimental.pallas import tpu as pltpu
from jax.sharding import PartitionSpec as P

LANES = 128
SUB = 8
F32 = jnp.float32
BF16 = jnp.bfloat16
VMEM_SPEC = pl.BlockSpec(memory_space=pltpu.VMEM)
SMEM_SPEC = pl.BlockSpec(memory_space=pltpu.SMEM)


def silu_slope(value):
    sigma = 1.0 / (1.0 + jnp.exp(-value))
    return sigma * (1.0 + value * (1.0 - sigma))


def roll(value, shift, axis):
    return pltpu.roll(value, shift % value.shape[axis], axis)


def lane_of(shape):
    return lax.broadcasted_iota(jnp.int32, shape, len(shape) - 1)


def sub_of(shape):
    return lax.broadcasted_iota(jnp.int32, shape, len(shape) - 2)


def group_frames(frames, chans):
    first, second, third, fourth = frames
    part = LANES - chans
    lane = lane_of(first.shape)
    packed = []
    for index, frame in enumerate((first, second, third)):
        packed.append(jnp.where(lane < chans, frame, roll(fourth, chans - part * index, 1)))
    return packed


def ungroup_frames(groups, chans):
    part = LANES - chans
    lane = lane_of(groups[0].shape)
    frames = [jnp.where(lane < chans, group, 0.0) for group in groups]
    fourth = jnp.zeros_like(groups[0])
    for index in reversed(range(3)):
        moved = roll(groups[index], part * (index + 1), 1)
        fourth = jnp.where(lane < part * (index + 1), moved, fourth)
    return frames + [jnp.where(lane < chans, fourth, 0.0)]


def edge_kernel(par_ref, cot_hbm, sec_hbm, fst_hbm, wp0, wp1, raw_ref, pad_ref, sems):
    frames, rows, cols, chans = cot_hbm.shape
    copies = []
    for a, src in enumerate((cot_hbm, sec_hbm, fst_hbm)):
        for side, start in enumerate((0, cols - SUB)):
            copies.append(
                pltpu.make_async_copy(src.at[:, :, pl.ds(start, SUB), :], raw_ref.at[a, side], sems.at[a, side])
            )
            copies[-1].start()
    pad_ref[...] = jnp.zeros(pad_ref.shape, F32)
    for copy in copies:
        copy.wait()
    pad_ref[0, :, :, :, :, 0:chans] = raw_ref[0]
    pad_ref[1:3, :, :, :, :, 0:chans] = silu_slope(raw_ref[1:3])

    def cols_out(left, right):
        sub = sub_of((SUB, LANES))
        for t in range(frames):
            for h in range(rows):
                c0, a0, b0 = (pad_ref[a, 0, t, h] for a in range(3))
                c7, a7, b7 = (pad_ref[a, 1, t, h] for a in range(3))
                right[t, h] = jnp.where(
                    sub >= 5, c7, jnp.where((sub == 2) | (sub == 3), roll(a7, 4, 0), jnp.where(sub == 1, roll(b7, 2, 0), 0.0))
                )
                left[t, h] = jnp.where(
                    sub < 3, c0, jnp.where((sub == 4) | (sub == 5), roll(a0, 4, 0), jnp.where(sub == 6, roll(b0, 6, 0), 0.0))
                )

    @pl.when(par_ref[1] == 0)
    def _():
        cols_out(wp1, wp0)

    @pl.when(par_ref[1] != 0)
    def _():
        cols_out(wp0, wp1)


def put_rows(read_cot, read_s2, read_s1, rows, top_a, top_b, low_a, low_b, span, chans):
    def put(read, h, dst, at):
        for g, val in enumerate(group_frames([read(t, h) for t in range(4)], chans)):
            dst[g, at, span] = val

    for r in range(3):
        put(read_cot, r, top_a, r)
        put(read_cot, rows - 3 + r, low_a, r)
    for r in range(2):
        put(read_s2, r, top_b, r)
        put(read_s2, rows - 2 + r, low_b, r)
    put(read_s1, 0, top_b, 2)
    put(read_s1, rows - 1, low_b, 2)


def pack_kernel(par_ref, cot_hbm, sec_hbm, fst_hbm, ma0, ma1, mb0, mb1, cp_ref, s2_ref, s1_ref, raw_ref, sems):
    frames, rows, cols, chans = cot_hbm.shape
    copies = [pltpu.make_async_copy(src, raw_ref.at[a], sems.at[a]) for a, src in enumerate((cot_hbm, sec_hbm, fst_hbm))]
    for copy in copies:
        copy.start()
    outs = (cp_ref, s2_ref, s1_ref)
    for ref in outs:
        ref[...] = jnp.zeros(ref.shape, F32)
    for a, ref in enumerate(outs):
        copies[a].wait()
        for t in range(frames):
            for h in range(rows):
                value = raw_ref[a, t, h]
                ref[t, h, 0:cols, 0:chans] = silu_slope(value) if a else value

    def rows_out(*dst):
        reads = [lambda t, h, ref=ref: ref[t, h, 0:cols] for ref in outs]
        put_rows(*reads, rows, *dst, slice(0, cols), chans)

    @pl.when(par_ref[0] == 0)
    def _():
        rows_out(ma1, mb1, ma0, mb0)

    @pl.when(par_ref[0] != 0)
    def _():
        rows_out(ma0, mb0, ma1, mb1)


def corner_kernel(chans, par_ref, rw0, rw1, _a0, _a1, _b0, _b1, _c, _s2, _s1, ma0, ma1, mb0, mb1, cp_ref, s2_ref, s1_ref):
    frames, rows = rw0.shape[:2]
    cols = ma0.shape[2] - SUB
    even = par_ref[1] == 0
    sub = sub_of((SUB, LANES))
    for t in range(frames):
        for h in range(rows):
            left = jnp.where(even, rw1[t, h], rw0[t, h])
            right = jnp.where(even, rw0[t, h], rw1[t, h])
            cp_ref[t, h, cols:] = jnp.where(sub < 3, right, jnp.where(sub >= 5, left, 0.0))
            s2_ref[t, h, cols:] = jnp.where(sub < 2, roll(right, 4, 0), jnp.where(sub >= 6, roll(left, 4, 0), 0.0))
            s1_ref[t, h, cols:] = jnp.where(sub == 0, roll(right, 2, 0), jnp.where(sub == 7, roll(left, 6, 0), 0.0))

    def rows_out(*dst):
        reads = [lambda t, h, ref=ref: ref[t, h, cols:] for ref in (cp_ref, s2_ref, s1_ref)]
        put_rows(*reads, rows, *dst, slice(cols, cols + SUB), chans)

    @pl.when(par_ref[0] == 0)
    def _():
        rows_out(ma1, mb1, ma0, mb0)

    @pl.when(par_ref[0] != 0)
    def _():
        rows_out(ma0, mb0, ma1, mb1)


def weight_kernel(wanted, w_ref, out_ref):
    chans = w_ref.shape[3]
    out_ref[...] = jnp.zeros(out_ref.shape, BF16)
    for k in range(3):
        for i in range(3):
            f0, f1, f2 = (w_ref[i, 2 - m, k] for m in range(3))
            even, odd = (f0 + f2) * (1 / 6), f1 * (1 / 6)
            far, odd2 = f0 * (1 / 24) + f2 * (1 / 6), f1 * (1 / 12)
            points = (f0 * 0.25, -even - odd, odd - even, far + odd2, far - odd2, f2)
            lanes = pl.ds((2 - i) * LANES, chans)
            for n, p in enumerate(wanted):
                u = points[p]
                high = u.astype(BF16)
                out_ref[n, k, 0, 0:chans, lanes] = high
                out_ref[n, k, 1, 0:chans, lanes] = (u - high.astype(F32)).astype(BF16)


POINTS = {2: (0, 1, 2, 5), 3: (0, 1, 2, 3, 5), 4: (0, 1, 2, 3, 4, 5)}


def transform(x, size):
    if size == 2:
        return 4.0 * (x[0] - x[2]), -3.0 * (x[1] + x[2]), 3.0 * (x[1] - x[2]), x[3] - x[1]
    if size == 3:
        a, b = x[3] - x[1], x[3] - 2.0 * x[1]
        return (
            4.0 * (x[0] - x[2]) + 2.0 * a,
            3.0 * (b - x[2]),
            2.0 * x[1] - 3.0 * x[2] + x[3],
            4.0 * a,
            x[4] - x[2] - 2.0 * a,
        )
    a, b = x[4] - 4.0 * x[2], x[3] - 4.0 * x[1]
    c, e = x[4] - x[2], 2.0 * (x[3] - x[1])
    return 4.0 * x[0] - 5.0 * x[2] + x[4], a + b, a - b, c + e, c - e, 4.0 * x[1] - 5.0 * x[3] + x[5]


def outputs(y, size):
    plus, minus = y[1] + y[2], y[1] - y[2]
    if size == 2:
        return y[0] + plus, minus + y[3]
    if size == 3:
        return y[0] + plus + y[3], minus + 2.0 * y[3], plus + 4.0 * y[3] + y[4]
    far, odd = y[3] + y[4], y[3] - y[4]
    return y[0] + plus + far, minus + 2.0 * odd, plus + 4.0 * far, minus + 8.0 * odd + y[5]


def right_operands(w_ref, p):
    zero = jnp.zeros((LANES, LANES), BF16)
    near, far = [], []
    for k in range(3):
        parts = [w_ref[p, k, part] for part in range(2)]
        own = [
            jnp.concatenate([r[:, : 2 * LANES], jnp.concatenate([zero, r[:, :LANES]], 1)], 0) for r in parts
        ]
        later = [
            jnp.concatenate([jnp.concatenate([r[:, 2 * LANES :], zero], 1), r[:, LANES:]], 0) for r in parts
        ]
        near.append(jnp.concatenate([own[0], own[0], own[1]], 1))
        far.append(jnp.concatenate([later[0], later[0], later[1]], 1))
    return jnp.concatenate(near, 0), jnp.concatenate(far, 0)


def product(left, right):
    left = jnp.concatenate([left, left[:, : 2 * LANES]], 1)
    return lax.dot_general(left, right, (((1,), (1,)), ((), ())), preferred_element_type=F32)


def shifted_sum(taps):
    two = 2 * LANES
    return roll(taps[:, :two], -1, 0) + taps[:, two : 2 * two] + roll(taps[:, 2 * two :], 1, 0)


def conv(read, size, width, s_ref, y_ref, w_ref, emit, done=None):
    chunks = width // SUB
    points = len(POINTS[size])

    def one(c, carry):
        at = pl.ds(pl.multiple_of(c * SUB, SUB), SUB)
        for t in range(4):
            pair, a = t // 2, t % 2
            x = [read(t, r, at) for r in range(2 * size + 2)]
            for p, pieces in enumerate(zip(transform(x[: size + 2], size), transform(x[size:], size))):
                value = jnp.concatenate(pieces, 0)
                high = value.astype(BF16)
                s_ref[p, c, pair, :, a * LANES : (a + 1) * LANES] = high
                s_ref[p, c, pair, :, (2 + a) * LANES : (3 + a) * LANES] = (value - high.astype(F32)).astype(BF16)
        return carry

    lax.fori_loop(0, chunks, one, 0)

    wide = 4 * LANES
    for p in range(points):
        near, far = right_operands(w_ref, p)
        own = product(s_ref[p].reshape(chunks * 4 * SUB, wide), near).reshape(chunks, 2, 2, SUB, 6 * LANES)
        later = product(s_ref[p, :, 1].reshape(chunks * 2 * SUB, wide), far).reshape(chunks, 2, SUB, 6 * LANES)
        for n in range(2):
            y_ref[0, p, n] = shifted_sum((own[:, 0, n] + later[:, n]).reshape(width, 6 * LANES))
            y_ref[1, p, n] = shifted_sum(own[:, 1, n].reshape(width, 6 * LANES))

    for t in range(4):
        lanes = pl.ds(t % 2 * LANES, LANES)
        for tile in range(2):
            rows = outputs([y_ref[t // 2, p, tile, :, lanes] for p in range(points)], size)
            for o, value in enumerate(rows):
                emit(t, tile * size + o, value)
        if done is not None:
            done(t)


def halo_rows(chans, par, from_even, from_odd, r):
    return ungroup_frames([jnp.where(par == 0, from_even[g, r], from_odd[g, r]) for g in range(3)], chans)


def third_kernel(chans, par_ref, cp_ref, ra0, ra1, w_ref, out_ref, x_ref, s_ref, y_ref):
    rows, width = cp_ref.shape[1:3]
    for r in range(3):
        for at, even, odd in ((r, ra1, ra0), (r + 3, ra0, ra1)):
            for t, frame in enumerate(halo_rows(chans, par_ref[0], even, odd, r)):
                x_ref[t, at] = frame

    def read(t, r, at):
        if 3 <= r < 3 + rows:
            return cp_ref[t, r - 3, at]
        return x_ref[t, r if r < 3 else r - rows, at]

    def emit(t, o, value):
        out_ref[t, o] = value

    conv(read, rows, width, s_ref, y_ref, w_ref, emit)


def last_kernel(chans, par_ref, g_ref, s2_ref, s1_ref, rb0, rb1, w2_ref, w1_ref, out_hbm,
                e_ref, x1_ref, s_ref, y_ref, stage_ref, sems):
    frames, rows, width, _ = s2_ref.shape
    cols = width - SUB
    for r in range(3):
        for side, even, odd in ((0, rb1, rb0), (1, rb0, rb1)):
            for t, frame in enumerate(halo_rows(chans, par_ref[0], even, odd, r)):
                e_ref[side, r, t] = frame

    def slope2(t, r, at):
        if 2 <= r < 2 + rows:
            return s2_ref[t, r - 2, at]
        return e_ref[0, r, t, at] if r < 2 else e_ref[1, r - 2 - rows, t, at]

    def emit2(t, o, value):
        slope = s1_ref[t, o - 1] if 1 <= o < 1 + rows else e_ref[0 if o < 1 else 1, 2, t]
        x1_ref[t, o] = value * slope

    def emit1(t, o, value):
        stage_ref[t, o] = value[0:cols, 0:chans]

    def copy_out(t):
        return pltpu.make_async_copy(stage_ref.at[t], out_hbm.at[t], sems.at[t])

    conv(lambda t, r, at: g_ref[t, r, at] * slope2(t, r, at), (rows + 2) // 2, width, s_ref, y_ref, w2_ref, emit2)
    conv(
        lambda t, r, at: x1_ref[t, r, at], rows // 2, width, s_ref, y_ref, w1_ref, emit1, lambda t: copy_out(t).start()
    )
    for t in range(frames):
        copy_out(t).wait()


def swap(value, axis, which):
    count = lax.axis_size(axis)
    pairs = []
    for low in range(1 - which, count - 1, 2):
        pairs += [(low, low + 1), (low + 1, low)]
    return lax.ppermute(value, axis, pairs)


def swaps(first, second, axis):
    got = swap(first, axis, 0), swap(second, axis, 1)
    return got


def call(body, out_shape, args, scratch=(), hbm=False, hbm_out=False, alias=None, vmem=40 << 20, flops=0, cost=0):
    hbm_spec = pl.BlockSpec(memory_space=pltpu.HBM)
    where, out = hbm_spec if hbm else VMEM_SPEC, hbm_spec if hbm_out else VMEM_SPEC
    return pl.pallas_call(
        body,
        out_shape=out_shape,
        in_specs=[SMEM_SPEC if a.dtype == jnp.int32 else where for a in args],
        out_specs=jax.tree.map(lambda _: out, out_shape),
        scratch_shapes=list(scratch),
        input_output_aliases=alias or {},
        compiler_params=pltpu.CompilerParams(vmem_limit_bytes=vmem),
        cost_estimate=pl.CostEstimate(flops=flops, bytes_accessed=cost, transcendentals=0),
    )(*args)


def local(cotangent, stored_first, stored_second, w_first, w_second, w_third):
    frames, rows, cols, chans = cotangent.shape
    width = cols + SUB
    par = jnp.stack([(lax.axis_index("ha") + 1) % 2, (lax.axis_index("wa") + 1) % 2]).astype(jnp.int32)

    def arr(*shape, dtype=F32):
        return jax.ShapeDtypeStruct(shape, dtype)

    def vmem(*shape, dtype=F32):
        return pltpu.VMEM(shape, dtype)

    edge = arr(frames, rows, SUB, LANES)
    own = arr(frames, rows, width, LANES)
    message = arr(3, 3, width, LANES)
    fields = tuple(pltpu.with_memory_space_constraint(x, pltpu.HBM) for x in (cotangent, stored_second, stored_first))
    wp0, wp1 = call(
        edge_kernel,
        (edge, edge),
        (par,) + fields,
        [vmem(3, 2, frames, rows, SUB, chans), vmem(3, 2, frames, rows, SUB, LANES), pltpu.SemaphoreType.DMA((3, 2))],
        hbm=True,
    )
    rw0, rw1 = swaps(wp0, wp1, "wa")
    packed = call(
        pack_kernel,
        (message,) * 4 + (own,) * 3,
        (par,) + fields,
        [vmem(3, frames, rows, cols, chans), pltpu.SemaphoreType.DMA((3,))],
        hbm=True,
    )
    ma0, ma1, mb0, mb1, cp, s2, s1 = call(
        functools.partial(corner_kernel, chans),
        (message,) * 4 + (own,) * 3,
        (par, rw0, rw1) + tuple(packed),
        alias={n + 3: n for n in range(7)},
    )
    ra0, ra1 = swaps(ma0, ma1, "ha")
    rb0, rb1 = swaps(mb0, mb1, "ha")

    def prepare(w, size):
        points = POINTS[size]
        shape = arr(len(points), 3, 2, LANES, 3 * LANES, dtype=BF16)
        return call(functools.partial(weight_kernel, points), shape, (w,))

    u3, u2, u1 = prepare(w_third, rows), prepare(w_second, (rows + 2) // 2), prepare(w_first, rows // 2)

    def scratch(size):
        points = len(POINTS[size])
        return [
            vmem(points, width // SUB, 2, 2 * SUB, 4 * LANES, dtype=BF16),
            vmem(2, points, 2, width, 2 * LANES),
        ]

    grad = call(
        functools.partial(third_kernel, chans),
        arr(frames, rows + 4, width, LANES),
        (par, cp, ra0, ra1, u3),
        [vmem(frames, 6, width, LANES)] + scratch(rows),
    )
    return call(
        functools.partial(last_kernel, chans),
        arr(frames, rows, cols, chans),
        (par, grad, s2, s1, rb0, rb1, u2, u1),
        [vmem(2, 3, frames, width, LANES), vmem(frames, rows + 2, width, LANES)]
        + scratch((rows + 2) // 2)
        + [vmem(frames, rows, cols, chans), pltpu.SemaphoreType.DMA((frames,))],
        hbm_out=True,
    )


def solution(mesh):
    in_specs = (
        P("clip", "ha", "wa", None),
        P("clip", "ha", "wa", None),
        P("clip", "ha", "wa", None),
        P(),
        P(),
        P(),
    )
    out_specs = P("clip", "ha", "wa", None)
    return jax.shard_map(local, mesh=mesh, in_specs=in_specs, out_specs=out_specs, check_vma=False)
```

```python
import functools

import jax
import jax.numpy as jnp
from jax import lax
from jax.experimental import pallas as pl
from jax.experimental.pallas import tpu as pltpu
from jax.sharding import PartitionSpec as P


LANES = 128
SUB = 8
F32 = jnp.float32
BF16 = jnp.bfloat16
VMEM_SPEC = pl.BlockSpec(memory_space=pltpu.VMEM)
SMEM_SPEC = pl.BlockSpec(memory_space=pltpu.SMEM)


def silu_slope(value):
    sigma = 1.0 / (1.0 + jnp.exp(-value))
    return sigma * (1.0 + value * (1.0 - sigma))


def roll(value, shift, axis):
    return pltpu.roll(value, shift % value.shape[axis], axis)


def lane_of(shape):
    return lax.broadcasted_iota(jnp.int32, shape, len(shape) - 1)


def sub_of(shape):
    return lax.broadcasted_iota(jnp.int32, shape, len(shape) - 2)


def group_frames(frames, chans):
    first, second, third, fourth = frames
    part = LANES - chans
    lane = lane_of(first.shape)
    packed = []
    for index, frame in enumerate((first, second, third)):
        packed.append(jnp.where(lane < chans, frame, roll(fourth, chans - part * index, 1)))
    return packed


def ungroup_frames(groups, chans):
    part = LANES - chans
    lane = lane_of(groups[0].shape)
    frames = [jnp.where(lane < chans, group, 0.0) for group in groups]
    fourth = jnp.zeros_like(groups[0])
    for index in reversed(range(3)):
        moved = roll(groups[index], part * (index + 1), 1)
        fourth = jnp.where(lane < part * (index + 1), moved, fourth)
    return frames + [jnp.where(lane < chans, fourth, 0.0)]


def pack_kernel(par_ref, cot_hbm, sec_hbm, fst_hbm, ma0, ma1, mb0, mb1, wp0, wp1, cp_ref, s2_ref, s1_ref, raw_ref, sems):
    frames, rows, cols, chans = cot_hbm.shape
    copies = [pltpu.make_async_copy(src, raw_ref.at[a], sems.at[a]) for a, src in enumerate((cot_hbm, sec_hbm, fst_hbm))]
    for copy in copies:
        copy.start()
    outs = (cp_ref, s2_ref, s1_ref)
    for ref in outs:
        ref[...] = jnp.zeros(ref.shape, F32)
    for a, ref in enumerate(outs):
        copies[a].wait()
        for t in range(frames):
            for h in range(rows):
                value = raw_ref[a, t, h]
                ref[t, h, 0:cols, 0:chans] = silu_slope(value) if a else value

    def rows_out(top_a, top_b, low_a, low_b):
        def put(src, h, dst, at):
            for g, val in enumerate(group_frames([src[t, h, 0:cols] for t in range(frames)], chans)):
                dst[g, at] = val

        for r in range(3):
            put(cp_ref, r, top_a, r)
            put(cp_ref, rows - 3 + r, low_a, r)
        for r in range(2):
            put(s2_ref, r, top_b, r)
            put(s2_ref, rows - 2 + r, low_b, r)
        put(s1_ref, 0, top_b, 2)
        put(s1_ref, rows - 1, low_b, 2)

    @pl.when(par_ref[0] == 0)
    def _():
        rows_out(ma1, mb1, ma0, mb0)

    @pl.when(par_ref[0] != 0)
    def _():
        rows_out(ma0, mb0, ma1, mb1)

    def cols_out(left, right):
        sub = sub_of((SUB, LANES))
        for t in range(frames):
            for h in range(rows):
                c0, a0, b0 = (ref[t, h, 0:SUB] for ref in outs)
                c7, a7, b7 = (ref[t, h, cols - SUB : cols] for ref in outs)
                right[t, h] = jnp.where(
                    sub >= 5, c7, jnp.where((sub == 2) | (sub == 3), roll(a7, 4, 0), jnp.where(sub == 1, roll(b7, 2, 0), 0.0))
                )
                left[t, h] = jnp.where(
                    sub < 3, c0, jnp.where((sub == 4) | (sub == 5), roll(a0, 4, 0), jnp.where(sub == 6, roll(b0, 6, 0), 0.0))
                )

    @pl.when(par_ref[1] == 0)
    def _():
        cols_out(wp1, wp0)

    @pl.when(par_ref[1] != 0)
    def _():
        cols_out(wp0, wp1)


def corner_kernel(chans, par_ref, rw0, rw1, _c, _s2, _s1, _b0, _b1, mc0, mc1, cp_ref, s2_ref, s1_ref, _mb0, _mb1):
    frames, rows = rw0.shape[:2]
    cols = cp_ref.shape[2] - SUB
    even = par_ref[1] == 0
    sub = sub_of((SUB, LANES))
    for t in range(frames):
        for h in range(rows):
            left = jnp.where(even, rw1[t, h], rw0[t, h])
            right = jnp.where(even, rw0[t, h], rw1[t, h])
            cp_ref[t, h, cols:] = jnp.where(sub < 3, right, jnp.where(sub >= 5, left, 0.0))
            s2_ref[t, h, cols:] = jnp.where(sub < 2, roll(right, 4, 0), jnp.where(sub >= 6, roll(left, 4, 0), 0.0))
            s1_ref[t, h, cols:] = jnp.where(sub == 0, roll(right, 2, 0), jnp.where(sub == 7, roll(left, 6, 0), 0.0))

    def out(top, low):
        def put(src, h, dst, at):
            for g, val in enumerate(group_frames([src[t, h, cols:] for t in range(frames)], chans)):
                dst[g, at] = val

        for r in range(3):
            put(cp_ref, r, top, r)
            put(cp_ref, rows - 3 + r, low, r)
        for r in range(2):
            put(s2_ref, r, top, 3 + r)
            put(s2_ref, rows - 2 + r, low, 3 + r)
        put(s1_ref, 0, top, 5)
        put(s1_ref, rows - 1, low, 5)

    @pl.when(par_ref[0] == 0)
    def _():
        out(mc1, mc0)

    @pl.when(par_ref[0] != 0)
    def _():
        out(mc0, mc1)


def weight_kernel(wanted, w_ref, out_ref):
    chans = w_ref.shape[3]
    out_ref[...] = jnp.zeros(out_ref.shape, BF16)
    for k in range(3):
        for i in range(3):
            f0, f1, f2 = (w_ref[i, 2 - m, k] for m in range(3))
            even, odd = (f0 + f2) * (1 / 6), f1 * (1 / 6)
            far, odd2 = f0 * (1 / 24) + f2 * (1 / 6), f1 * (1 / 12)
            points = (f0 * 0.25, -even - odd, odd - even, far + odd2, far - odd2, f2)
            lanes = pl.ds((2 - i) * LANES, chans)
            for n, p in enumerate(wanted):
                u = points[p]
                high = u.astype(BF16)
                out_ref[n, k, 0, 0:chans, lanes] = high
                out_ref[n, k, 1, 0:chans, lanes] = (u - high.astype(F32)).astype(BF16)


POINTS = {2: (0, 1, 2, 5), 3: (0, 1, 2, 3, 5), 4: (0, 1, 2, 3, 4, 5)}


def transform(x, size):
    if size == 2:
        return 4.0 * (x[0] - x[2]), -3.0 * (x[1] + x[2]), 3.0 * (x[1] - x[2]), x[3] - x[1]
    if size == 3:
        a, b = x[3] - x[1], x[3] - 2.0 * x[1]
        return (
            4.0 * (x[0] - x[2]) + 2.0 * a,
            3.0 * (b - x[2]),
            2.0 * x[1] - 3.0 * x[2] + x[3],
            4.0 * a,
            x[4] - x[2] - 2.0 * a,
        )
    a, b = x[4] - 4.0 * x[2], x[3] - 4.0 * x[1]
    c, e = x[4] - x[2], 2.0 * (x[3] - x[1])
    return 4.0 * x[0] - 5.0 * x[2] + x[4], a + b, a - b, c + e, c - e, 4.0 * x[1] - 5.0 * x[3] + x[5]


def outputs(y, size):
    plus, minus = y[1] + y[2], y[1] - y[2]
    if size == 2:
        return y[0] + plus, minus + y[3]
    if size == 3:
        return y[0] + plus + y[3], minus + 2.0 * y[3], plus + 4.0 * y[3] + y[4]
    far, odd = y[3] + y[4], y[3] - y[4]
    return y[0] + plus + far, minus + 2.0 * odd, plus + 4.0 * far, minus + 8.0 * odd + y[5]


def right_operands(w_ref, p):
    zero = jnp.zeros((LANES, LANES), BF16)
    near, far = [], []
    for k in range(3):
        parts = [w_ref[p, k, part] for part in range(2)]
        own = [
            jnp.concatenate([r[:, : 2 * LANES], jnp.concatenate([zero, r[:, :LANES]], 1)], 0) for r in parts
        ]
        later = [
            jnp.concatenate([jnp.concatenate([r[:, 2 * LANES :], zero], 1), r[:, LANES:]], 0) for r in parts
        ]
        near.append(jnp.concatenate([own[0], own[0], own[1]], 1))
        far.append(jnp.concatenate([later[0], later[0], later[1]], 1))
    return jnp.concatenate(near, 0), jnp.concatenate(far, 0)


def product(left, right):
    left = jnp.concatenate([left, left[:, : 2 * LANES]], 1)
    return lax.dot_general(left, right, (((1,), (1,)), ((), ())), preferred_element_type=F32)


def shifted_sum(taps):
    two = 2 * LANES
    return roll(taps[:, :two], -1, 0) + taps[:, two : 2 * two] + roll(taps[:, 2 * two :], 1, 0)


def conv(read, size, width, s_ref, y_ref, w_ref, emit, done=None):
    chunks = width // SUB
    points = len(POINTS[size])

    def one(c, carry):
        at = pl.ds(pl.multiple_of(c * SUB, SUB), SUB)
        for t in range(4):
            pair, a = t // 2, t % 2
            x = [read(t, r, at) for r in range(2 * size + 2)]
            for p, pieces in enumerate(zip(transform(x[: size + 2], size), transform(x[size:], size))):
                value = jnp.concatenate(pieces, 0)
                high = value.astype(BF16)
                s_ref[p, c, pair, :, a * LANES : (a + 1) * LANES] = high
                s_ref[p, c, pair, :, (2 + a) * LANES : (3 + a) * LANES] = (value - high.astype(F32)).astype(BF16)
        return carry

    lax.fori_loop(0, chunks, one, 0)

    wide = 4 * LANES
    for p in range(points):
        near, far = right_operands(w_ref, p)
        own = product(s_ref[p].reshape(chunks * 4 * SUB, wide), near).reshape(chunks, 2, 2, SUB, 6 * LANES)
        later = product(s_ref[p, :, 1].reshape(chunks * 2 * SUB, wide), far).reshape(chunks, 2, SUB, 6 * LANES)
        for n in range(2):
            y_ref[0, p, n] = shifted_sum((own[:, 0, n] + later[:, n]).reshape(width, 6 * LANES))
            y_ref[1, p, n] = shifted_sum(own[:, 1, n].reshape(width, 6 * LANES))

    for t in range(4):
        lanes = pl.ds(t % 2 * LANES, LANES)
        for tile in range(2):
            rows = outputs([y_ref[t // 2, p, tile, :, lanes] for p in range(points)], size)
            for o, value in enumerate(rows):
                emit(t, tile * size + o, value)
        if done is not None:
            done(t)


def halo_rows(chans, par, from_even, from_odd, r):
    return ungroup_frames([jnp.where(par == 0, from_even[g, r], from_odd[g, r]) for g in range(3)], chans)


def third_kernel(chans, par_ref, cp_ref, ra0, ra1, rc0, rc1, w_ref, out_ref, x_ref, s_ref, y_ref):
    rows, width = cp_ref.shape[1:3]
    cols = width - SUB
    for r in range(3):
        for at, even, odd, ceven, codd in ((r, ra1, ra0, rc1, rc0), (r + 3, ra0, ra1, rc0, rc1)):
            for t, frame in enumerate(halo_rows(chans, par_ref[0], even, odd, r)):
                x_ref[t, at, 0:cols] = frame
            for t, frame in enumerate(halo_rows(chans, par_ref[0], ceven, codd, r)):
                x_ref[t, at, cols:] = frame

    def read(t, r, at):
        if 3 <= r < 3 + rows:
            return cp_ref[t, r - 3, at]
        return x_ref[t, r if r < 3 else r - rows, at]

    def emit(t, o, value):
        out_ref[t, o] = value

    conv(read, rows, width, s_ref, y_ref, w_ref, emit)


def last_kernel(chans, par_ref, g_ref, s2_ref, s1_ref, rb0, rb1, rc0, rc1, w2_ref, w1_ref, out_hbm,
                e_ref, x1_ref, s_ref, y_ref, stage_ref, sems):
    frames, rows, width, _ = s2_ref.shape
    cols = width - SUB
    for r in range(3):
        for side, even, odd, ceven, codd in ((0, rb1, rb0, rc1, rc0), (1, rb0, rb1, rc0, rc1)):
            for t, frame in enumerate(halo_rows(chans, par_ref[0], even, odd, r)):
                e_ref[side, r, t, 0:cols] = frame
            for t, frame in enumerate(halo_rows(chans, par_ref[0], ceven, codd, 3 + r)):
                e_ref[side, r, t, cols:] = frame

    def slope2(t, r, at):
        if 2 <= r < 2 + rows:
            return s2_ref[t, r - 2, at]
        return e_ref[0, r, t, at] if r < 2 else e_ref[1, r - 2 - rows, t, at]

    def emit2(t, o, value):
        slope = s1_ref[t, o - 1] if 1 <= o < 1 + rows else e_ref[0 if o < 1 else 1, 2, t]
        x1_ref[t, o] = value * slope

    def emit1(t, o, value):
        stage_ref[t, o] = value[0:cols, 0:chans]

    def copy_out(t):
        return pltpu.make_async_copy(stage_ref.at[t], out_hbm.at[t], sems.at[t])

    conv(lambda t, r, at: g_ref[t, r, at] * slope2(t, r, at), (rows + 2) // 2, width, s_ref, y_ref, w2_ref, emit2)
    conv(
        lambda t, r, at: x1_ref[t, r, at], rows // 2, width, s_ref, y_ref, w1_ref, emit1, lambda t: copy_out(t).start()
    )
    for t in range(frames):
        copy_out(t).wait()


def swap(value, axis, which):
    count = lax.axis_size(axis)
    pairs = []
    for low in range(1 - which, count - 1, 2):
        pairs += [(low, low + 1), (low + 1, low)]
    return lax.ppermute(value, axis, pairs)


def swaps(first, second, axis):
    got = []
    for which, value in enumerate((first, second)):
        got.append(swap(value, axis, which))
    return got


def call(body, out_shape, args, scratch=(), hbm=False, hbm_out=False, alias=None, vmem=40 << 20, flops=0, cost=0):
    hbm_spec = pl.BlockSpec(memory_space=pltpu.HBM)
    where, out = hbm_spec if hbm else VMEM_SPEC, hbm_spec if hbm_out else VMEM_SPEC
    return pl.pallas_call(
        body,
        out_shape=out_shape,
        in_specs=[SMEM_SPEC if a.dtype == jnp.int32 else where for a in args],
        out_specs=jax.tree.map(lambda _: out, out_shape),
        scratch_shapes=list(scratch),
        input_output_aliases=alias or {},
        compiler_params=pltpu.CompilerParams(vmem_limit_bytes=vmem),
        cost_estimate=pl.CostEstimate(flops=flops, bytes_accessed=cost, transcendentals=0),
    )(*args)


def program(cotangent, stored_first, stored_second, w_first, w_second, w_third):
    frames, rows, cols, chans = cotangent.shape
    width = cols + SUB
    par = jnp.stack([(lax.axis_index("ha") + 1) % 2, (lax.axis_index("wa") + 1) % 2]).astype(jnp.int32)

    def arr(*shape, dtype=F32):
        return jax.ShapeDtypeStruct(shape, dtype)

    def vmem(*shape, dtype=F32):
        return pltpu.VMEM(shape, dtype)

    edge = arr(frames, rows, SUB, LANES)
    own = arr(frames, rows, width, LANES)
    message = arr(3, 3, cols, LANES)
    corner = arr(3, 6, SUB, LANES)
    fields = tuple(pltpu.with_memory_space_constraint(x, pltpu.HBM) for x in (cotangent, stored_second, stored_first))
    ma0, ma1, mb0, mb1, wp0, wp1, *kept = call(
        pack_kernel,
        (message,) * 4 + (edge,) * 2 + (own,) * 3,
        (par,) + fields,
        [vmem(3, frames, rows, cols, chans), pltpu.SemaphoreType.DMA((3,))],
        hbm=True,
    )
    ra0, ra1 = swaps(ma0, ma1, "ha")
    rw0, rw1 = swaps(wp0, wp1, "wa")
    mc0, mc1, cp, s2, s1, mb0, mb1 = call(
        functools.partial(corner_kernel, chans),
        (corner,) * 2 + (own,) * 3 + (message,) * 2,
        (par, rw0, rw1, *kept, mb0, mb1),
        alias={n + 3: n + 2 for n in range(5)},
    )
    rc0, rc1 = swaps(mc0, mc1, "ha")
    rb0, rb1 = swaps(mb0, mb1, "ha")

    def prepare(w, size):
        points = POINTS[size]
        shape = arr(len(points), 3, 2, LANES, 3 * LANES, dtype=BF16)
        return call(functools.partial(weight_kernel, points), shape, (w,))

    u3, u2, u1 = prepare(w_third, rows), prepare(w_second, (rows + 2) // 2), prepare(w_first, rows // 2)

    def scratch(size):
        points = len(POINTS[size])
        return [
            vmem(points, width // SUB, 2, 2 * SUB, 4 * LANES, dtype=BF16),
            vmem(2, points, 2, width, 2 * LANES),
        ]

    grad = call(
        functools.partial(third_kernel, chans),
        arr(frames, rows + 4, width, LANES),
        (par, cp, ra0, ra1, rc0, rc1, u3),
        [vmem(frames, 6, width, LANES)] + scratch(rows),
    )
    return call(
        functools.partial(last_kernel, chans),
        arr(frames, rows, cols, chans),
        (par, grad, s2, s1, rb0, rb1, rc0, rc1, u2, u1),
        [vmem(2, 3, frames, width, LANES), vmem(frames, rows + 2, width, LANES)]
        + scratch((rows + 2) // 2)
        + [vmem(frames, rows, cols, chans), pltpu.SemaphoreType.DMA((frames,))],
        hbm_out=True,
    )


def solution(mesh):
    in_specs = (
        P("clip", "ha", "wa", None),
        P("clip", "ha", "wa", None),
        P("clip", "ha", "wa", None),
        P(),
        P(),
        P(),
    )
    out_specs = P("clip", "ha", "wa", None)
    return jax.shard_map(program, mesh=mesh, in_specs=in_specs, out_specs=out_specs, check_vma=False)
```

```python
import functools

import jax
import jax.numpy as jnp
from jax import lax
from jax.experimental import pallas as pl
from jax.experimental.pallas import tpu as pltpu
from jax.sharding import PartitionSpec as P


LANES = 128
SUB = 8
F32 = jnp.float32
BF16 = jnp.bfloat16
VMEM_SPEC = pl.BlockSpec(memory_space=pltpu.VMEM)
SMEM_SPEC = pl.BlockSpec(memory_space=pltpu.SMEM)


def silu_slope(value):
    sigma = 1.0 / (1.0 + jnp.exp(-value))
    return sigma * (1.0 + value * (1.0 - sigma))


def roll(value, shift, axis):
    return pltpu.roll(value, shift % value.shape[axis], axis)


def lane_of(shape):
    return lax.broadcasted_iota(jnp.int32, shape, len(shape) - 1)


def sub_of(shape):
    return lax.broadcasted_iota(jnp.int32, shape, len(shape) - 2)


def group_frames(frames, chans):
    first, second, third, fourth = frames
    part = LANES - chans
    lane = lane_of(first.shape)
    packed = []
    for index, frame in enumerate((first, second, third)):
        packed.append(jnp.where(lane < chans, frame, roll(fourth, chans - part * index, 1)))
    return packed


def ungroup_frames(groups, chans):
    part = LANES - chans
    lane = lane_of(groups[0].shape)
    frames = [jnp.where(lane < chans, group, 0.0) for group in groups]
    fourth = jnp.zeros_like(groups[0])
    for index in reversed(range(3)):
        moved = roll(groups[index], part * (index + 1), 1)
        fourth = jnp.where(lane < part * (index + 1), moved, fourth)
    return frames + [jnp.where(lane < chans, fourth, 0.0)]


def group_row(src, h, cols, chans):
    return group_frames([src[t, h, 0:cols] for t in range(4)], chans)


def pack_kernel(par_ref, cot_hbm, sec_hbm, fst_hbm, ma0, ma1, wp0, wp1, cp_ref, sec_ref, fst_ref, raw_ref, edge_ref, sems):
    frames, rows, cols, chans = cot_hbm.shape
    copies = [
        pltpu.make_async_copy(src, dst, sems.at[a])
        for a, (src, dst) in enumerate(((cot_hbm, raw_ref), (sec_hbm, sec_ref), (fst_hbm, fst_ref)))
    ]
    for copy in copies:
        copy.start()
    cp_ref[...] = jnp.zeros(cp_ref.shape, F32)
    edge_ref[...] = jnp.zeros(edge_ref.shape, F32)
    copies[0].wait()
    cp_ref[:, :, 0:cols, 0:chans] = raw_ref[...]

    def rows_out(top, low):
        for r in range(3):
            for dst, h in ((top, r), (low, rows - 3 + r)):
                for g, val in enumerate(group_row(cp_ref, h, cols, chans)):
                    dst[g, r] = val

    @pl.when(par_ref[0] == 0)
    def _():
        rows_out(ma1, ma0)

    @pl.when(par_ref[0] != 0)
    def _():
        rows_out(ma0, ma1)

    for a, ref in ((0, sec_ref), (1, fst_ref)):
        copies[1 + a].wait()
        for side, start in enumerate((0, cols - SUB)):
            edge_ref[a, side, :, :, :, 0:chans] = silu_slope(ref[:, :, start : start + SUB])

    def cols_out(left, right):
        sub = sub_of((SUB, LANES))
        for t in range(frames):
            for h in range(rows):
                c0, a0, b0 = cp_ref[t, h, 0:SUB], edge_ref[0, 0, t, h], edge_ref[1, 0, t, h]
                c7, a7, b7 = cp_ref[t, h, cols - SUB : cols], edge_ref[0, 1, t, h], edge_ref[1, 1, t, h]
                right[t, h] = jnp.where(
                    sub >= 5, c7, jnp.where((sub == 2) | (sub == 3), roll(a7, 4, 0), jnp.where(sub == 1, roll(b7, 2, 0), 0.0))
                )
                left[t, h] = jnp.where(
                    sub < 3, c0, jnp.where((sub == 4) | (sub == 5), roll(a0, 4, 0), jnp.where(sub == 6, roll(b0, 6, 0), 0.0))
                )

    @pl.when(par_ref[1] == 0)
    def _():
        cols_out(wp1, wp0)

    @pl.when(par_ref[1] != 0)
    def _():
        cols_out(wp0, wp1)


def slope_kernel(par_ref, sec_ref, fst_ref, mb0, mb1, s2_ref, s1_ref):
    frames, rows, cols, chans = sec_ref.shape
    blank = jnp.zeros((cols, LANES), F32)
    for src, ref in ((sec_ref, s2_ref), (fst_ref, s1_ref)):
        for t in range(frames):
            for h in range(rows):
                ref[t, h, 0:cols] = blank
                ref[t, h, 0:cols, 0:chans] = silu_slope(src[t, h])

    def rows_out(top, low):
        for src, h, dst, at in (
            (s2_ref, 0, top, 0),
            (s2_ref, 1, top, 1),
            (s1_ref, 0, top, 2),
            (s2_ref, rows - 2, low, 0),
            (s2_ref, rows - 1, low, 1),
            (s1_ref, rows - 1, low, 2),
        ):
            for g, val in enumerate(group_row(src, h, cols, chans)):
                dst[g, at] = val

    @pl.when(par_ref[0] == 0)
    def _():
        rows_out(mb1, mb0)

    @pl.when(par_ref[0] != 0)
    def _():
        rows_out(mb0, mb1)


def corner_kernel(chans, par_ref, rw0, rw1, _c, _s2, _s1, _b0, _b1, mc0, mc1, cp_ref, s2_ref, s1_ref, _mb0, _mb1):
    frames, rows = rw0.shape[:2]
    cols = cp_ref.shape[2] - SUB
    even = par_ref[1] == 0
    sub = sub_of((SUB, LANES))
    for t in range(frames):
        for h in range(rows):
            left = jnp.where(even, rw1[t, h], rw0[t, h])
            right = jnp.where(even, rw0[t, h], rw1[t, h])
            cp_ref[t, h, cols:] = jnp.where(sub < 3, right, jnp.where(sub >= 5, left, 0.0))
            s2_ref[t, h, cols:] = jnp.where(sub < 2, roll(right, 4, 0), jnp.where(sub >= 6, roll(left, 4, 0), 0.0))
            s1_ref[t, h, cols:] = jnp.where(sub == 0, roll(right, 2, 0), jnp.where(sub == 7, roll(left, 6, 0), 0.0))

    def out(top, low):
        def put(src, h, dst, at):
            for g, val in enumerate(group_frames([src[t, h, cols:] for t in range(frames)], chans)):
                dst[g, at] = val

        for r in range(3):
            put(cp_ref, r, top, r)
            put(cp_ref, rows - 3 + r, low, r)
        for r in range(2):
            put(s2_ref, r, top, 3 + r)
            put(s2_ref, rows - 2 + r, low, 3 + r)
        put(s1_ref, 0, top, 5)
        put(s1_ref, rows - 1, low, 5)

    @pl.when(par_ref[0] == 0)
    def _():
        out(mc1, mc0)

    @pl.when(par_ref[0] != 0)
    def _():
        out(mc0, mc1)


def prepare(w_ref, out_ref, wanted, k, i):
    chans = w_ref.shape[3]
    f0, f1, f2 = (w_ref[i, 2 - m, k] for m in range(3))
    even, odd = (f0 + f2) * (1 / 6), f1 * (1 / 6)
    far, odd2 = f0 * (1 / 24) + f2 * (1 / 6), f1 * (1 / 12)
    points = (f0 * 0.25, -even - odd, odd - even, far + odd2, far - odd2, f2)
    lanes = pl.ds((2 - i) * LANES, chans)
    for n, p in enumerate(wanted):
        high = points[p].astype(BF16)
        out_ref[n, k, 0, 0:chans, lanes] = high
        out_ref[n, k, 1, 0:chans, lanes] = (points[p] - high.astype(F32)).astype(BF16)


def prepare_all(w_ref, out_ref, wanted):
    steps = []
    for n in range(len(wanted)):
        for k in range(3):
            def clear(n=n, k=k):
                out_ref[n, k] = jnp.zeros(out_ref.shape[2:], BF16)

            steps.append(clear)
    for k in range(3):
        for i in range(3):
            steps.append(functools.partial(prepare, w_ref, out_ref, wanted, k, i))
    return steps


def weight_kernel(wanted, w_ref, out_ref):
    for step in prepare_all(w_ref, out_ref, wanted):
        step()


POINTS = {2: (0, 1, 2, 5), 3: (0, 1, 2, 3, 5), 4: (0, 1, 2, 3, 4, 5)}


def transform(x, size):
    if size == 2:
        return 4.0 * (x[0] - x[2]), -3.0 * (x[1] + x[2]), 3.0 * (x[1] - x[2]), x[3] - x[1]
    if size == 3:
        a, b = x[3] - x[1], x[3] - 2.0 * x[1]
        return (
            4.0 * (x[0] - x[2]) + 2.0 * a,
            3.0 * (b - x[2]),
            2.0 * x[1] - 3.0 * x[2] + x[3],
            4.0 * a,
            x[4] - x[2] - 2.0 * a,
        )
    a, b = x[4] - 4.0 * x[2], x[3] - 4.0 * x[1]
    c, e = x[4] - x[2], 2.0 * (x[3] - x[1])
    return 4.0 * x[0] - 5.0 * x[2] + x[4], a + b, a - b, c + e, c - e, 4.0 * x[1] - 5.0 * x[3] + x[5]


def outputs(y, size):
    plus, minus = y[1] + y[2], y[1] - y[2]
    if size == 2:
        return y[0] + plus, minus + y[3]
    if size == 3:
        return y[0] + plus + y[3], minus + 2.0 * y[3], plus + 4.0 * y[3] + y[4]
    far, odd = y[3] + y[4], y[3] - y[4]
    return y[0] + plus + far, minus + 2.0 * odd, plus + 4.0 * far, minus + 8.0 * odd + y[5]


def right_operands(w_ref, p):
    zero = jnp.zeros((LANES, LANES), BF16)
    near, far = [], []
    for k in range(3):
        parts = [w_ref[p, k, part] for part in range(2)]
        own = [
            jnp.concatenate([r[:, : 2 * LANES], jnp.concatenate([zero, r[:, :LANES]], 1)], 0) for r in parts
        ]
        later = [
            jnp.concatenate([jnp.concatenate([r[:, 2 * LANES :], zero], 1), r[:, LANES:]], 0) for r in parts
        ]
        near.append(jnp.concatenate([own[0], own[0], own[1]], 1))
        far.append(jnp.concatenate([later[0], later[0], later[1]], 1))
    return jnp.concatenate(near, 0), jnp.concatenate(far, 0)


def product(left, right):
    left = jnp.concatenate([left, left[:, : 2 * LANES]], 1)
    return lax.dot_general(left, right, (((1,), (1,)), ((), ())), preferred_element_type=F32)


def shifted_sum(taps):
    two = 2 * LANES
    return roll(taps[:, :two], -1, 0) + taps[:, two : 2 * two] + roll(taps[:, 2 * two :], 1, 0)


def conv(read, size, width, s_ref, y_ref, w_ref, emit, done=None, beside=()):
    chunks = width // SUB
    points = len(POINTS[size])

    def one(c, carry):
        at = pl.ds(pl.multiple_of(c * SUB, SUB), SUB)
        for t in range(4):
            pair, a = t // 2, t % 2
            x = [read(t, r, at) for r in range(2 * size + 2)]
            for p, pieces in enumerate(zip(transform(x[: size + 2], size), transform(x[size:], size))):
                value = jnp.concatenate(pieces, 0)
                high = value.astype(BF16)
                s_ref[p, c, pair, :, a * LANES : (a + 1) * LANES] = high
                s_ref[p, c, pair, :, (2 + a) * LANES : (3 + a) * LANES] = (value - high.astype(F32)).astype(BF16)
        return carry

    lax.fori_loop(0, chunks, one, 0)

    wide = 4 * LANES
    for p in range(points):
        near, far = right_operands(w_ref, p)
        own = product(s_ref[p].reshape(chunks * 4 * SUB, wide), near).reshape(chunks, 2, 2, SUB, 6 * LANES)
        later = product(s_ref[p, :, 1].reshape(chunks * 2 * SUB, wide), far).reshape(chunks, 2, SUB, 6 * LANES)
        for n in range(2):
            y_ref[0, p, n] = shifted_sum((own[:, 0, n] + later[:, n]).reshape(width, 6 * LANES))
            y_ref[1, p, n] = shifted_sum(own[:, 1, n].reshape(width, 6 * LANES))
        for step in beside[p * len(beside) // points : (p + 1) * len(beside) // points]:
            step()

    for t in range(4):
        lanes = pl.ds(t % 2 * LANES, LANES)
        for tile in range(2):
            rows = outputs([y_ref[t // 2, p, tile, :, lanes] for p in range(points)], size)
            for o, value in enumerate(rows):
                emit(t, tile * size + o, value)
        if done is not None:
            done(t)


def halo_rows(chans, par, from_even, from_odd, r):
    return ungroup_frames([jnp.where(par == 0, from_even[g, r], from_odd[g, r]) for g in range(3)], chans)


def third_kernel(chans, par_ref, cp_ref, ra0, ra1, rc0, rc1, w_ref, w2_ref, w1_ref, out_ref, u2_ref, u1_ref, x_ref, s_ref, y_ref):
    rows, width = cp_ref.shape[1:3]
    cols = width - SUB
    for r in range(3):
        for at, even, odd, ceven, codd in ((r, ra1, ra0, rc1, rc0), (r + 3, ra0, ra1, rc0, rc1)):
            for t, frame in enumerate(halo_rows(chans, par_ref[0], even, odd, r)):
                x_ref[t, at, 0:cols] = frame
            for t, frame in enumerate(halo_rows(chans, par_ref[0], ceven, codd, r)):
                x_ref[t, at, cols:] = frame

    def read(t, r, at):
        if 3 <= r < 3 + rows:
            return cp_ref[t, r - 3, at]
        return x_ref[t, r if r < 3 else r - rows, at]

    def emit(t, o, value):
        out_ref[t, o] = value

    beside = prepare_all(w2_ref, u2_ref, POINTS[(rows + 2) // 2]) + prepare_all(w1_ref, u1_ref, POINTS[rows // 2])
    conv(read, rows, width, s_ref, y_ref, w_ref, emit, beside=beside)


def last_kernel(chans, par_ref, g_ref, s2_ref, s1_ref, rb0, rb1, rc0, rc1, w2_ref, w1_ref, out_hbm,
                e_ref, x1_ref, s_ref, y_ref, stage_ref, sems):
    frames, rows, width, _ = s2_ref.shape
    cols = width - SUB
    for r in range(3):
        for side, even, odd, ceven, codd in ((0, rb1, rb0, rc1, rc0), (1, rb0, rb1, rc0, rc1)):
            for t, frame in enumerate(halo_rows(chans, par_ref[0], even, odd, r)):
                e_ref[side, r, t, 0:cols] = frame
            for t, frame in enumerate(halo_rows(chans, par_ref[0], ceven, codd, 3 + r)):
                e_ref[side, r, t, cols:] = frame

    def slope2(t, r, at):
        if 2 <= r < 2 + rows:
            return s2_ref[t, r - 2, at]
        return e_ref[0, r, t, at] if r < 2 else e_ref[1, r - 2 - rows, t, at]

    def emit2(t, o, value):
        slope = s1_ref[t, o - 1] if 1 <= o < 1 + rows else e_ref[0 if o < 1 else 1, 2, t]
        x1_ref[t, o] = value * slope

    def emit1(t, o, value):
        stage_ref[t, o] = value[0:cols, 0:chans]

    def copy_out(t):
        return pltpu.make_async_copy(stage_ref.at[t], out_hbm.at[t], sems.at[t])

    conv(lambda t, r, at: g_ref[t, r, at] * slope2(t, r, at), (rows + 2) // 2, width, s_ref, y_ref, w2_ref, emit2)
    conv(
        lambda t, r, at: x1_ref[t, r, at], rows // 2, width, s_ref, y_ref, w1_ref, emit1, lambda t: copy_out(t).start()
    )
    for t in range(frames):
        copy_out(t).wait()


def swap(value, axis, which):
    count = lax.axis_size(axis)
    pairs = []
    for low in range(1 - which, count - 1, 2):
        pairs += [(low, low + 1), (low + 1, low)]
    return lax.ppermute(value, axis, pairs)


def swaps(first, second, axis):
    got = []
    for which, value in enumerate((first, second)):
        got.append(swap(value, axis, which))
    return got


def call(body, out_shape, args, scratch=(), hbm=False, hbm_out=False, alias=None, vmem=40 << 20, flops=0, cost=0):
    hbm_spec = pl.BlockSpec(memory_space=pltpu.HBM)
    where, out = hbm_spec if hbm else VMEM_SPEC, hbm_spec if hbm_out else VMEM_SPEC
    return pl.pallas_call(
        body,
        out_shape=out_shape,
        in_specs=[SMEM_SPEC if a.dtype == jnp.int32 else where for a in args],
        out_specs=jax.tree.map(lambda _: out, out_shape),
        scratch_shapes=list(scratch),
        input_output_aliases=alias or {},
        compiler_params=pltpu.CompilerParams(vmem_limit_bytes=vmem),
        cost_estimate=pl.CostEstimate(flops=flops, bytes_accessed=cost, transcendentals=0),
    )(*args)


def program(cotangent, stored_first, stored_second, w_first, w_second, w_third):
    frames, rows, cols, chans = cotangent.shape
    width = cols + SUB
    par = jnp.stack([(lax.axis_index("ha") + 1) % 2, (lax.axis_index("wa") + 1) % 2]).astype(jnp.int32)

    def arr(*shape, dtype=F32):
        return jax.ShapeDtypeStruct(shape, dtype)

    def vmem(*shape, dtype=F32):
        return pltpu.VMEM(shape, dtype)

    edge = arr(frames, rows, SUB, LANES)
    own = arr(frames, rows, width, LANES)
    message = arr(3, 3, cols, LANES)
    corner = arr(3, 6, SUB, LANES)
    fields = tuple(pltpu.with_memory_space_constraint(x, pltpu.HBM) for x in (cotangent, stored_second, stored_first))
    raw = arr(frames, rows, cols, chans)
    ma0, ma1, wp0, wp1, cp, sec, fst = call(
        pack_kernel,
        (message,) * 2 + (edge,) * 2 + (own, raw, raw),
        (par,) + fields,
        [vmem(frames, rows, cols, chans), vmem(2, 2, frames, rows, SUB, LANES), pltpu.SemaphoreType.DMA((3,))],
        hbm=True,
    )
    ra0, ra1 = swaps(ma0, ma1, "ha")
    rw0, rw1 = swaps(wp0, wp1, "wa")
    mb0, mb1, s2, s1 = call(slope_kernel, (message,) * 2 + (own,) * 2, (par, sec, fst))
    mc0, mc1, cp, s2, s1, mb0, mb1 = call(
        functools.partial(corner_kernel, chans),
        (corner,) * 2 + (own,) * 3 + (message,) * 2,
        (par, rw0, rw1, cp, s2, s1, mb0, mb1),
        alias={n + 3: n + 2 for n in range(5)},
    )
    rc0, rc1 = swaps(mc0, mc1, "ha")
    rb0, rb1 = swaps(mb0, mb1, "ha")

    def weights(size):
        return arr(len(POINTS[size]), 3, 2, LANES, 3 * LANES, dtype=BF16)

    size3, size2, size1 = rows, (rows + 2) // 2, rows // 2
    u3 = call(functools.partial(weight_kernel, POINTS[size3]), weights(size3), (w_third,))

    def scratch(size):
        points = len(POINTS[size])
        return [
            vmem(points, width // SUB, 2, 2 * SUB, 4 * LANES, dtype=BF16),
            vmem(2, points, 2, width, 2 * LANES),
        ]

    grad, u2, u1 = call(
        functools.partial(third_kernel, chans),
        (arr(frames, rows + 4, width, LANES), weights(size2), weights(size1)),
        (par, cp, ra0, ra1, rc0, rc1, u3, w_second, w_first),
        [vmem(frames, 6, width, LANES)] + scratch(size3),
    )
    return call(
        functools.partial(last_kernel, chans),
        arr(frames, rows, cols, chans),
        (par, grad, s2, s1, rb0, rb1, rc0, rc1, u2, u1),
        [vmem(2, 3, frames, width, LANES), vmem(frames, rows + 2, width, LANES)]
        + scratch(size2)
        + [vmem(frames, rows, cols, chans), pltpu.SemaphoreType.DMA((frames,))],
        hbm_out=True,
    )


def solution(mesh):
    in_specs = (
        P("clip", "ha", "wa", None),
        P("clip", "ha", "wa", None),
        P("clip", "ha", "wa", None),
        P(),
        P(),
        P(),
    )
    out_specs = P("clip", "ha", "wa", None)
    return jax.shard_map(program, mesh=mesh, in_specs=in_specs, out_specs=out_specs, check_vma=False)
```

```python
import functools

import jax
import jax.numpy as jnp
from jax import lax
from jax.experimental import pallas as pl
from jax.experimental.pallas import tpu as pltpu
from jax.sharding import PartitionSpec as P


LANES = 128
SUB = 8
F32 = jnp.float32
BF16 = jnp.bfloat16
VMEM_SPEC = pl.BlockSpec(memory_space=pltpu.VMEM)
SMEM_SPEC = pl.BlockSpec(memory_space=pltpu.SMEM)


def silu_slope(value):
    sigma = 1.0 / (1.0 + jnp.exp(-value))
    return sigma * (1.0 + value * (1.0 - sigma))


def roll(value, shift, axis):
    return pltpu.roll(value, shift % value.shape[axis], axis)


def lane_of(shape):
    return lax.broadcasted_iota(jnp.int32, shape, len(shape) - 1)


def sub_of(shape):
    return lax.broadcasted_iota(jnp.int32, shape, len(shape) - 2)


def group_frames(frames, chans):
    first, second, third, fourth = frames
    part = LANES - chans
    lane = lane_of(first.shape)
    packed = []
    for index, frame in enumerate((first, second, third)):
        packed.append(jnp.where(lane < chans, frame, roll(fourth, chans - part * index, 1)))
    return packed


def ungroup_frames(groups, chans):
    part = LANES - chans
    lane = lane_of(groups[0].shape)
    frames = [jnp.where(lane < chans, group, 0.0) for group in groups]
    fourth = jnp.zeros_like(groups[0])
    for index in reversed(range(3)):
        moved = roll(groups[index], part * (index + 1), 1)
        fourth = jnp.where(lane < part * (index + 1), moved, fourth)
    return frames + [jnp.where(lane < chans, fourth, 0.0)]


def group_row(src, h, cols, chans):
    return group_frames([src[t, h, 0:cols] for t in range(4)], chans)


def pack_kernel(par_ref, cot_hbm, sec_hbm, fst_hbm, ma0, ma1, wp0, wp1, cp_ref, sec_ref, fst_ref, raw_ref, edge_ref, sems):
    frames, rows, cols, chans = cot_hbm.shape
    copies = [
        pltpu.make_async_copy(src, dst, sems.at[a])
        for a, (src, dst) in enumerate(((cot_hbm, raw_ref), (sec_hbm, sec_ref), (fst_hbm, fst_ref)))
    ]
    for copy in copies:
        copy.start()
    cp_ref[...] = jnp.zeros(cp_ref.shape, F32)
    edge_ref[...] = jnp.zeros(edge_ref.shape, F32)
    copies[0].wait()
    cp_ref[:, :, 0:cols, 0:chans] = raw_ref[...]

    def rows_out(top, low):
        for r in range(3):
            for dst, h in ((top, r), (low, rows - 3 + r)):
                for g, val in enumerate(group_row(cp_ref, h, cols, chans)):
                    dst[g, r] = val

    @pl.when(par_ref[0] == 0)
    def _():
        rows_out(ma1, ma0)

    @pl.when(par_ref[0] != 0)
    def _():
        rows_out(ma0, ma1)

    for a, ref in ((0, sec_ref), (1, fst_ref)):
        copies[1 + a].wait()
        for side, start in enumerate((0, cols - SUB)):
            edge_ref[a, side, :, :, :, 0:chans] = silu_slope(ref[:, :, start : start + SUB])

    def cols_out(left, right):
        sub = sub_of((SUB, LANES))
        for t in range(frames):
            for h in range(rows):
                c0, a0, b0 = cp_ref[t, h, 0:SUB], edge_ref[0, 0, t, h], edge_ref[1, 0, t, h]
                c7, a7, b7 = cp_ref[t, h, cols - SUB : cols], edge_ref[0, 1, t, h], edge_ref[1, 1, t, h]
                right[t, h] = jnp.where(
                    sub >= 5, c7, jnp.where((sub == 2) | (sub == 3), roll(a7, 4, 0), jnp.where(sub == 1, roll(b7, 2, 0), 0.0))
                )
                left[t, h] = jnp.where(
                    sub < 3, c0, jnp.where((sub == 4) | (sub == 5), roll(a0, 4, 0), jnp.where(sub == 6, roll(b0, 6, 0), 0.0))
                )

    @pl.when(par_ref[1] == 0)
    def _():
        cols_out(wp1, wp0)

    @pl.when(par_ref[1] != 0)
    def _():
        cols_out(wp0, wp1)


def slope_kernel(par_ref, sec_ref, fst_ref, mb0, mb1, s2_ref, s1_ref):
    frames, rows, cols, chans = sec_ref.shape
    blank = jnp.zeros((cols, LANES), F32)
    for src, ref in ((sec_ref, s2_ref), (fst_ref, s1_ref)):
        for t in range(frames):
            for h in range(rows):
                ref[t, h, 0:cols] = blank
                ref[t, h, 0:cols, 0:chans] = silu_slope(src[t, h])

    def rows_out(top, low):
        for src, h, dst, at in (
            (s2_ref, 0, top, 0),
            (s2_ref, 1, top, 1),
            (s1_ref, 0, top, 2),
            (s2_ref, rows - 2, low, 0),
            (s2_ref, rows - 1, low, 1),
            (s1_ref, rows - 1, low, 2),
        ):
            for g, val in enumerate(group_row(src, h, cols, chans)):
                dst[g, at] = val

    @pl.when(par_ref[0] == 0)
    def _():
        rows_out(mb1, mb0)

    @pl.when(par_ref[0] != 0)
    def _():
        rows_out(mb0, mb1)


def corner_kernel(chans, par_ref, rw0, rw1, _c, _s2, _s1, _b0, _b1, mc0, mc1, cp_ref, s2_ref, s1_ref, _mb0, _mb1):
    frames, rows = rw0.shape[:2]
    cols = cp_ref.shape[2] - SUB
    even = par_ref[1] == 0
    sub = sub_of((SUB, LANES))
    for t in range(frames):
        for h in range(rows):
            left = jnp.where(even, rw1[t, h], rw0[t, h])
            right = jnp.where(even, rw0[t, h], rw1[t, h])
            cp_ref[t, h, cols:] = jnp.where(sub < 3, right, jnp.where(sub >= 5, left, 0.0))
            s2_ref[t, h, cols:] = jnp.where(sub < 2, roll(right, 4, 0), jnp.where(sub >= 6, roll(left, 4, 0), 0.0))
            s1_ref[t, h, cols:] = jnp.where(sub == 0, roll(right, 2, 0), jnp.where(sub == 7, roll(left, 6, 0), 0.0))

    def out(top, low):
        def put(src, h, dst, at):
            for g, val in enumerate(group_frames([src[t, h, cols:] for t in range(frames)], chans)):
                dst[g, at] = val

        for r in range(3):
            put(cp_ref, r, top, r)
            put(cp_ref, rows - 3 + r, low, r)
        for r in range(2):
            put(s2_ref, r, top, 3 + r)
            put(s2_ref, rows - 2 + r, low, 3 + r)
        put(s1_ref, 0, top, 5)
        put(s1_ref, rows - 1, low, 5)

    @pl.when(par_ref[0] == 0)
    def _():
        out(mc1, mc0)

    @pl.when(par_ref[0] != 0)
    def _():
        out(mc0, mc1)


def prepare(w_ref, out_ref, wanted, k, i, which):
    chans = w_ref.shape[3]
    blank = jnp.zeros((chans, LANES - chans), F32)
    f0, f1, f2 = (jnp.concatenate([w_ref[i, 2 - m, k], blank], 1) for m in range(3))
    points = {
        0: lambda: f0 * 0.25,
        1: lambda: (f0 + f1 + f2) * (-1 / 6),
        2: lambda: (f1 - f0 - f2) * (1 / 6),
        3: lambda: f0 * (1 / 24) + f1 * (1 / 12) + f2 * (1 / 6),
        4: lambda: f0 * (1 / 24) - f1 * (1 / 12) + f2 * (1 / 6),
        5: lambda: f2,
    }
    lanes = pl.ds((2 - i) * LANES, LANES)
    for n in which:
        value = points[wanted[n]]()
        high = value.astype(BF16)
        out_ref[n, k, 0, 0:chans, lanes] = high
        out_ref[n, k, 1, 0:chans, lanes] = (value - high.astype(F32)).astype(BF16)


def prepare_all(w_ref, out_ref, wanted):
    chans = w_ref.shape[3]

    def clear(n, k):
        out_ref[n, k, :, chans:] = jnp.zeros((2, LANES - chans, 3 * LANES), BF16)

    steps = []
    for k in range(3):
        for n in range(len(wanted)):
            steps.append(functools.partial(clear, n, k))
            for i in range(3):
                steps.append(functools.partial(prepare, w_ref, out_ref, wanted, k, i, (n,)))
    return steps


def weight_kernel(wanted, w_ref, out_ref):
    for step in prepare_all(w_ref, out_ref, wanted):
        step()


POINTS = {2: (0, 1, 2, 5), 3: (0, 1, 2, 3, 5), 4: (0, 1, 2, 3, 4, 5)}


def transform(x, size):
    if size == 2:
        return 4.0 * (x[0] - x[2]), -3.0 * (x[1] + x[2]), 3.0 * (x[1] - x[2]), x[3] - x[1]
    if size == 3:
        a, b = x[3] - x[1], x[3] - 2.0 * x[1]
        return (
            4.0 * (x[0] - x[2]) + 2.0 * a,
            3.0 * (b - x[2]),
            2.0 * x[1] - 3.0 * x[2] + x[3],
            4.0 * a,
            x[4] - x[2] - 2.0 * a,
        )
    a, b = x[4] - 4.0 * x[2], x[3] - 4.0 * x[1]
    c, e = x[4] - x[2], 2.0 * (x[3] - x[1])
    return 4.0 * x[0] - 5.0 * x[2] + x[4], a + b, a - b, c + e, c - e, 4.0 * x[1] - 5.0 * x[3] + x[5]


def outputs(y, size):
    plus, minus = y[1] + y[2], y[1] - y[2]
    if size == 2:
        return y[0] + plus, minus + y[3]
    if size == 3:
        return y[0] + plus + y[3], minus + 2.0 * y[3], plus + 4.0 * y[3] + y[4]
    far, odd = y[3] + y[4], y[3] - y[4]
    return y[0] + plus + far, minus + 2.0 * odd, plus + 4.0 * far, minus + 8.0 * odd + y[5]


def right_operands(w_ref, p):
    zero = jnp.zeros((LANES, LANES), BF16)
    near, far = [], []
    for k in range(3):
        parts = [w_ref[p, k, part] for part in range(2)]
        own = [
            jnp.concatenate([r[:, : 2 * LANES], jnp.concatenate([zero, r[:, :LANES]], 1)], 0) for r in parts
        ]
        later = [
            jnp.concatenate([jnp.concatenate([r[:, 2 * LANES :], zero], 1), r[:, LANES:]], 0) for r in parts
        ]
        near.append(jnp.concatenate([own[0], own[0], own[1]], 1))
        far.append(jnp.concatenate([later[0], later[0], later[1]], 1))
    return jnp.concatenate(near, 0), jnp.concatenate(far, 0)


def product(left, right):
    left = jnp.concatenate([left, left[:, : 2 * LANES]], 1)
    return lax.dot_general(left, right, (((1,), (1,)), ((), ())), preferred_element_type=F32)


def shifted_sum(taps):
    two = 2 * LANES
    return roll(taps[:, :two], -1, 0) + taps[:, two : 2 * two] + roll(taps[:, 2 * two :], 1, 0)


def conv(read, size, width, s_ref, y_ref, w_ref, emit, done=None, beside=()):
    chunks = width // SUB
    points = len(POINTS[size])

    def one(c, carry):
        at = pl.ds(pl.multiple_of(c * SUB, SUB), SUB)
        for t in range(4):
            pair, a = t // 2, t % 2
            x = [read(t, r, at) for r in range(2 * size + 2)]
            for p, pieces in enumerate(zip(transform(x[: size + 2], size), transform(x[size:], size))):
                value = jnp.concatenate(pieces, 0)
                high = value.astype(BF16)
                s_ref[p, c, pair, :, a * LANES : (a + 1) * LANES] = high
                s_ref[p, c, pair, :, (2 + a) * LANES : (3 + a) * LANES] = (value - high.astype(F32)).astype(BF16)
        return carry

    lax.fori_loop(0, chunks, one, 0)

    wide = 4 * LANES
    gap = 2 * points

    def other_work(n):
        for step in beside[n * len(beside) // gap : (n + 1) * len(beside) // gap]:
            step()

    for p in range(points):
        near, far = right_operands(w_ref, p)
        own = product(s_ref[p].reshape(chunks * 4 * SUB, wide), near).reshape(chunks, 2, 2, SUB, 6 * LANES)
        other_work(2 * p)
        later = product(s_ref[p, :, 1].reshape(chunks * 2 * SUB, wide), far).reshape(chunks, 2, SUB, 6 * LANES)
        other_work(2 * p + 1)
        for n in range(2):
            y_ref[0, p, n] = shifted_sum((own[:, 0, n] + later[:, n]).reshape(width, 6 * LANES))
            y_ref[1, p, n] = shifted_sum(own[:, 1, n].reshape(width, 6 * LANES))

    for t in range(4):
        lanes = pl.ds(t % 2 * LANES, LANES)
        for tile in range(2):
            rows = outputs([y_ref[t // 2, p, tile, :, lanes] for p in range(points)], size)
            for o, value in enumerate(rows):
                emit(t, tile * size + o, value)
        if done is not None:
            done(t)


def halo_rows(chans, par, from_even, from_odd, r):
    return ungroup_frames([jnp.where(par == 0, from_even[g, r], from_odd[g, r]) for g in range(3)], chans)


def third_kernel(chans, par_ref, cp_ref, ra0, ra1, rc0, rc1, w_ref, w2_ref, w1_ref, out_ref, u2_ref, u1_ref, x_ref, s_ref, y_ref):
    rows, width = cp_ref.shape[1:3]
    cols = width - SUB
    for r in range(3):
        for at, even, odd, ceven, codd in ((r, ra1, ra0, rc1, rc0), (r + 3, ra0, ra1, rc0, rc1)):
            for t, frame in enumerate(halo_rows(chans, par_ref[0], even, odd, r)):
                x_ref[t, at, 0:cols] = frame
            for t, frame in enumerate(halo_rows(chans, par_ref[0], ceven, codd, r)):
                x_ref[t, at, cols:] = frame

    def read(t, r, at):
        if 3 <= r < 3 + rows:
            return cp_ref[t, r - 3, at]
        return x_ref[t, r if r < 3 else r - rows, at]

    def emit(t, o, value):
        out_ref[t, o] = value

    beside = prepare_all(w2_ref, u2_ref, POINTS[(rows + 2) // 2]) + prepare_all(w1_ref, u1_ref, POINTS[rows // 2])
    conv(read, rows, width, s_ref, y_ref, w_ref, emit, beside=beside)


def last_kernel(chans, par_ref, g_ref, s2_ref, s1_ref, rb0, rb1, rc0, rc1, w2_ref, w1_ref, out_hbm,
                e_ref, x1_ref, s_ref, y_ref, stage_ref, sems):
    frames, rows, width, _ = s2_ref.shape
    cols = width - SUB
    for r in range(3):
        for side, even, odd, ceven, codd in ((0, rb1, rb0, rc1, rc0), (1, rb0, rb1, rc0, rc1)):
            for t, frame in enumerate(halo_rows(chans, par_ref[0], even, odd, r)):
                e_ref[side, r, t, 0:cols] = frame
            for t, frame in enumerate(halo_rows(chans, par_ref[0], ceven, codd, 3 + r)):
                e_ref[side, r, t, cols:] = frame

    def slope2(t, r, at):
        if 2 <= r < 2 + rows:
            return s2_ref[t, r - 2, at]
        return e_ref[0, r, t, at] if r < 2 else e_ref[1, r - 2 - rows, t, at]

    def emit2(t, o, value):
        slope = s1_ref[t, o - 1] if 1 <= o < 1 + rows else e_ref[0 if o < 1 else 1, 2, t]
        x1_ref[t, o] = value * slope

    def emit1(t, o, value):
        stage_ref[t, o] = value[0:cols, 0:chans]

    def copy_out(t):
        return pltpu.make_async_copy(stage_ref.at[t], out_hbm.at[t], sems.at[t])

    conv(lambda t, r, at: g_ref[t, r, at] * slope2(t, r, at), (rows + 2) // 2, width, s_ref, y_ref, w2_ref, emit2)
    conv(
        lambda t, r, at: x1_ref[t, r, at], rows // 2, width, s_ref, y_ref, w1_ref, emit1, lambda t: copy_out(t).start()
    )
    for t in range(frames):
        copy_out(t).wait()


def swap(value, axis, which):
    count = lax.axis_size(axis)
    pairs = []
    for low in range(1 - which, count - 1, 2):
        pairs += [(low, low + 1), (low + 1, low)]
    return lax.ppermute(value, axis, pairs)


def swaps(first, second, axis):
    got = []
    for which, value in enumerate((first, second)):
        got.append(swap(value, axis, which))
    return got


def call(body, out_shape, args, scratch=(), hbm=False, hbm_out=False, alias=None, vmem=40 << 20, flops=0, cost=0):
    hbm_spec = pl.BlockSpec(memory_space=pltpu.HBM)
    where, out = hbm_spec if hbm else VMEM_SPEC, hbm_spec if hbm_out else VMEM_SPEC
    return pl.pallas_call(
        body,
        out_shape=out_shape,
        in_specs=[SMEM_SPEC if a.dtype == jnp.int32 else where for a in args],
        out_specs=jax.tree.map(lambda _: out, out_shape),
        scratch_shapes=list(scratch),
        input_output_aliases=alias or {},
        compiler_params=pltpu.CompilerParams(vmem_limit_bytes=vmem),
        cost_estimate=pl.CostEstimate(flops=flops, bytes_accessed=cost, transcendentals=0),
    )(*args)


def program(cotangent, stored_first, stored_second, w_first, w_second, w_third):
    frames, rows, cols, chans = cotangent.shape
    width = cols + SUB
    par = jnp.stack([(lax.axis_index("ha") + 1) % 2, (lax.axis_index("wa") + 1) % 2]).astype(jnp.int32)

    def arr(*shape, dtype=F32):
        return jax.ShapeDtypeStruct(shape, dtype)

    def vmem(*shape, dtype=F32):
        return pltpu.VMEM(shape, dtype)

    edge = arr(frames, rows, SUB, LANES)
    own = arr(frames, rows, width, LANES)
    message = arr(3, 3, cols, LANES)
    corner = arr(3, 6, SUB, LANES)
    fields = tuple(pltpu.with_memory_space_constraint(x, pltpu.HBM) for x in (cotangent, stored_second, stored_first))
    raw = arr(frames, rows, cols, chans)
    ma0, ma1, wp0, wp1, cp, sec, fst = call(
        pack_kernel,
        (message,) * 2 + (edge,) * 2 + (own, raw, raw),
        (par,) + fields,
        [vmem(frames, rows, cols, chans), vmem(2, 2, frames, rows, SUB, LANES), pltpu.SemaphoreType.DMA((3,))],
        hbm=True,
    )
    ra0, ra1 = swaps(ma0, ma1, "ha")
    rw0, rw1 = swaps(wp0, wp1, "wa")
    mb0, mb1, s2, s1 = call(slope_kernel, (message,) * 2 + (own,) * 2, (par, sec, fst))
    mc0, mc1, cp, s2, s1, mb0, mb1 = call(
        functools.partial(corner_kernel, chans),
        (corner,) * 2 + (own,) * 3 + (message,) * 2,
        (par, rw0, rw1, cp, s2, s1, mb0, mb1),
        alias={n + 3: n + 2 for n in range(5)},
    )
    rc0, rc1 = swaps(mc0, mc1, "ha")
    rb0, rb1 = swaps(mb0, mb1, "ha")

    def weights(size):
        return arr(len(POINTS[size]), 3, 2, LANES, 3 * LANES, dtype=BF16)

    size3, size2, size1 = rows, (rows + 2) // 2, rows // 2
    u3 = call(functools.partial(weight_kernel, POINTS[size3]), weights(size3), (w_third,))

    def scratch(size):
        points = len(POINTS[size])
        return [
            vmem(points, width // SUB, 2, 2 * SUB, 4 * LANES, dtype=BF16),
            vmem(2, points, 2, width, 2 * LANES),
        ]

    grad, u2, u1 = call(
        functools.partial(third_kernel, chans),
        (arr(frames, rows + 4, width, LANES), weights(size2), weights(size1)),
        (par, cp, ra0, ra1, rc0, rc1, u3, w_second, w_first),
        [vmem(frames, 6, width, LANES)] + scratch(size3),
    )
    return call(
        functools.partial(last_kernel, chans),
        arr(frames, rows, cols, chans),
        (par, grad, s2, s1, rb0, rb1, rc0, rc1, u2, u1),
        [vmem(2, 3, frames, width, LANES), vmem(frames, rows + 2, width, LANES)]
        + scratch(size2)
        + [vmem(frames, rows, cols, chans), pltpu.SemaphoreType.DMA((frames,))],
        hbm_out=True,
    )


def solution(mesh):
    in_specs = (
        P("clip", "ha", "wa", None),
        P("clip", "ha", "wa", None),
        P("clip", "ha", "wa", None),
        P(),
        P(),
        P(),
    )
    out_specs = P("clip", "ha", "wa", None)
    return jax.shard_map(program, mesh=mesh, in_specs=in_specs, out_specs=out_specs, check_vma=False)
```

```python
import functools

import jax
import jax.numpy as jnp
from jax import lax
from jax.experimental import pallas as pl
from jax.experimental.pallas import tpu as pltpu
from jax.sharding import PartitionSpec as P


LANES = 128
SUB = 8
F32 = jnp.float32
BF16 = jnp.bfloat16
VMEM_SPEC = pl.BlockSpec(memory_space=pltpu.VMEM)
SMEM_SPEC = pl.BlockSpec(memory_space=pltpu.SMEM)


def silu_slope(value):
    sigma = 1.0 / (1.0 + jnp.exp(-value))
    return sigma * (1.0 + value * (1.0 - sigma))


def roll(value, shift, axis):
    return pltpu.roll(value, shift % value.shape[axis], axis)


def lane_of(shape):
    return lax.broadcasted_iota(jnp.int32, shape, len(shape) - 1)


def sub_of(shape):
    return lax.broadcasted_iota(jnp.int32, shape, len(shape) - 2)


def group_frames(frames, chans):
    first, second, third, fourth = frames
    part = LANES - chans
    lane = lane_of(first.shape)
    packed = []
    for index, frame in enumerate((first, second, third)):
        packed.append(jnp.where(lane < chans, frame, roll(fourth, chans - part * index, 1)))
    return packed


def ungroup_frames(groups, chans):
    part = LANES - chans
    lane = lane_of(groups[0].shape)
    frames = [jnp.where(lane < chans, group, 0.0) for group in groups]
    fourth = jnp.zeros_like(groups[0])
    for index in reversed(range(3)):
        moved = roll(groups[index], part * (index + 1), 1)
        fourth = jnp.where(lane < part * (index + 1), moved, fourth)
    return frames + [jnp.where(lane < chans, fourth, 0.0)]


def group_row(src, h, cols, chans):
    return group_frames([src[t, h, 0:cols] for t in range(4)], chans)


def pack_kernel(par_ref, cot_hbm, sec_hbm, fst_hbm, ma0, ma1, wp0, wp1, cp_ref, sec_ref, fst_ref, raw_ref, edge_ref, sems):
    frames, rows, cols, chans = cot_hbm.shape
    copies = [
        pltpu.make_async_copy(src, dst, sems.at[a])
        for a, (src, dst) in enumerate(((cot_hbm, raw_ref), (sec_hbm, sec_ref), (fst_hbm, fst_ref)))
    ]
    for copy in copies:
        copy.start()
    cp_ref[...] = jnp.zeros(cp_ref.shape, F32)
    edge_ref[...] = jnp.zeros(edge_ref.shape, F32)
    copies[0].wait()
    cp_ref[:, :, 0:cols, 0:chans] = raw_ref[...]

    def rows_out(top, low):
        for r in range(3):
            for dst, h in ((top, r), (low, rows - 3 + r)):
                for g, val in enumerate(group_row(cp_ref, h, cols, chans)):
                    dst[g, r] = val

    @pl.when(par_ref[0] == 0)
    def _():
        rows_out(ma1, ma0)

    @pl.when(par_ref[0] != 0)
    def _():
        rows_out(ma0, ma1)

    for a, ref in ((0, sec_ref), (1, fst_ref)):
        copies[1 + a].wait()
        for side, start in enumerate((0, cols - SUB)):
            edge_ref[a, side, :, :, :, 0:chans] = silu_slope(ref[:, :, start : start + SUB])

    def cols_out(left, right):
        sub = sub_of((SUB, LANES))
        for t in range(frames):
            for h in range(rows):
                c0, a0, b0 = cp_ref[t, h, 0:SUB], edge_ref[0, 0, t, h], edge_ref[1, 0, t, h]
                c7, a7, b7 = cp_ref[t, h, cols - SUB : cols], edge_ref[0, 1, t, h], edge_ref[1, 1, t, h]
                right[t, h] = jnp.where(
                    sub >= 5, c7, jnp.where((sub == 2) | (sub == 3), roll(a7, 4, 0), jnp.where(sub == 1, roll(b7, 2, 0), 0.0))
                )
                left[t, h] = jnp.where(
                    sub < 3, c0, jnp.where((sub == 4) | (sub == 5), roll(a0, 4, 0), jnp.where(sub == 6, roll(b0, 6, 0), 0.0))
                )

    @pl.when(par_ref[1] == 0)
    def _():
        cols_out(wp1, wp0)

    @pl.when(par_ref[1] != 0)
    def _():
        cols_out(wp0, wp1)


def slope_kernel(par_ref, sec_ref, fst_ref, mb0, mb1, s2_ref, s1_ref):
    frames, rows, cols, chans = sec_ref.shape
    blank = jnp.zeros((cols, LANES), F32)
    for src, ref in ((sec_ref, s2_ref), (fst_ref, s1_ref)):
        for t in range(frames):
            for h in range(rows):
                ref[t, h, 0:cols] = blank
                ref[t, h, 0:cols, 0:chans] = silu_slope(src[t, h])

    def rows_out(top, low):
        for src, h, dst, at in (
            (s2_ref, 0, top, 0),
            (s2_ref, 1, top, 1),
            (s1_ref, 0, top, 2),
            (s2_ref, rows - 2, low, 0),
            (s2_ref, rows - 1, low, 1),
            (s1_ref, rows - 1, low, 2),
        ):
            for g, val in enumerate(group_row(src, h, cols, chans)):
                dst[g, at] = val

    @pl.when(par_ref[0] == 0)
    def _():
        rows_out(mb1, mb0)

    @pl.when(par_ref[0] != 0)
    def _():
        rows_out(mb0, mb1)


def corner_kernel(chans, par_ref, rw0, rw1, _c, _s2, _s1, _b0, _b1, mc0, mc1, cp_ref, s2_ref, s1_ref, _mb0, _mb1):
    frames, rows = rw0.shape[:2]
    cols = cp_ref.shape[2] - SUB
    even = par_ref[1] == 0
    sub = sub_of((SUB, LANES))
    for t in range(frames):
        for h in range(rows):
            left = jnp.where(even, rw1[t, h], rw0[t, h])
            right = jnp.where(even, rw0[t, h], rw1[t, h])
            cp_ref[t, h, cols:] = jnp.where(sub < 3, right, jnp.where(sub >= 5, left, 0.0))
            s2_ref[t, h, cols:] = jnp.where(sub < 2, roll(right, 4, 0), jnp.where(sub >= 6, roll(left, 4, 0), 0.0))
            s1_ref[t, h, cols:] = jnp.where(sub == 0, roll(right, 2, 0), jnp.where(sub == 7, roll(left, 6, 0), 0.0))

    def out(top, low):
        def put(src, h, dst, at):
            for g, val in enumerate(group_frames([src[t, h, cols:] for t in range(frames)], chans)):
                dst[g, at] = val

        for r in range(3):
            put(cp_ref, r, top, r)
            put(cp_ref, rows - 3 + r, low, r)
        for r in range(2):
            put(s2_ref, r, top, 3 + r)
            put(s2_ref, rows - 2 + r, low, 3 + r)
        put(s1_ref, 0, top, 5)
        put(s1_ref, rows - 1, low, 5)

    @pl.when(par_ref[0] == 0)
    def _():
        out(mc1, mc0)

    @pl.when(par_ref[0] != 0)
    def _():
        out(mc0, mc1)


def prepare(w_ref, out_ref, wanted, k, i, which):
    chans = w_ref.shape[3]
    blank = jnp.zeros((chans, LANES - chans), F32)
    f0, f1, f2 = (jnp.concatenate([w_ref[i, 2 - m, k], blank], 1) for m in range(3))
    points = {
        0: lambda: f0 * 0.25,
        1: lambda: (f0 + f1 + f2) * (-1 / 6),
        2: lambda: (f1 - f0 - f2) * (1 / 6),
        3: lambda: f0 * (1 / 24) + f1 * (1 / 12) + f2 * (1 / 6),
        4: lambda: f0 * (1 / 24) - f1 * (1 / 12) + f2 * (1 / 6),
        5: lambda: f2,
    }
    lanes = pl.ds((2 - i) * LANES, LANES)
    for n in which:
        value = points[wanted[n]]()
        high = value.astype(BF16)
        out_ref[n, k, 0, 0:chans, lanes] = high
        out_ref[n, k, 1, 0:chans, lanes] = (value - high.astype(F32)).astype(BF16)


def prepare_all(w_ref, out_ref, wanted):
    chans = w_ref.shape[3]

    def clear(n, k):
        out_ref[n, k, :, chans:] = jnp.zeros((2, LANES - chans, 3 * LANES), BF16)

    steps = []
    for k in range(3):
        for n in range(len(wanted)):
            steps.append(functools.partial(clear, n, k))
            for i in range(3):
                steps.append(functools.partial(prepare, w_ref, out_ref, wanted, k, i, (n,)))
    return steps


def weight_kernel(wanted, w_ref, out_ref):
    for step in prepare_all(w_ref, out_ref, wanted):
        step()


SLOTS = (0, 2, 1, 3)
POINTS = {2: (0, 1, 2, 5), 3: (0, 1, 2, 3, 5), 4: (0, 1, 2, 3, 4, 5)}


def transform(x, size):
    if size == 2:
        return 4.0 * (x[0] - x[2]), -3.0 * (x[1] + x[2]), 3.0 * (x[1] - x[2]), x[3] - x[1]
    if size == 3:
        a, b = x[3] - x[1], x[3] - 2.0 * x[1]
        return (
            4.0 * (x[0] - x[2]) + 2.0 * a,
            3.0 * (b - x[2]),
            2.0 * x[1] - 3.0 * x[2] + x[3],
            4.0 * a,
            x[4] - x[2] - 2.0 * a,
        )
    a, b = x[4] - 4.0 * x[2], x[3] - 4.0 * x[1]
    c, e = x[4] - x[2], 2.0 * (x[3] - x[1])
    return 4.0 * x[0] - 5.0 * x[2] + x[4], a + b, a - b, c + e, c - e, 4.0 * x[1] - 5.0 * x[3] + x[5]


def outputs(y, size):
    plus, minus = y[1] + y[2], y[1] - y[2]
    if size == 2:
        return y[0] + plus, minus + y[3]
    if size == 3:
        return y[0] + plus + y[3], minus + 2.0 * y[3], plus + 4.0 * y[3] + y[4]
    far, odd = y[3] + y[4], y[3] - y[4]
    return y[0] + plus + far, minus + 2.0 * odd, plus + 4.0 * far, minus + 8.0 * odd + y[5]


def right_operands(w_ref, p):
    zero = jnp.zeros((LANES, LANES), BF16)
    taps = [[w_ref[p, k, part] for k in range(3)] for part in range(2)]

    def alone(at):
        lanes = slice(at * LANES, (at + 1) * LANES)
        high = [jnp.concatenate([r[:, lanes], r[:, lanes]], 1) for r in taps[0]]
        return high + [jnp.concatenate([r[:, lanes], zero], 1) for r in taps[1]]

    both = []
    for lanes in (slice(LANES, 3 * LANES), slice(0, 2 * LANES)):
        for high, low in zip(*taps):
            both.append(jnp.concatenate([high[:, lanes], high[:, lanes], low[:, lanes]], 1))
    return (
        jnp.concatenate(alone(0), 0),
        jnp.concatenate(alone(2) + alone(1) + alone(0), 0),
        jnp.concatenate(both, 0),
    )


def product(left, right):
    return lax.dot_general(left, right, (((1,), (1,)), ((), ())), preferred_element_type=F32)


def shifted_sum(taps):
    return roll(taps[:, :LANES], -1, 0) + taps[:, LANES : 2 * LANES] + roll(taps[:, 2 * LANES :], 1, 0)


def conv(read, size, width, s_ref, y_ref, w_ref, emit, done=None, beside=()):
    chunks = width // SUB
    points = len(POINTS[size])

    def one(c, carry):
        at = pl.ds(pl.multiple_of(c * SUB, SUB), SUB)
        for t in range(4):
            x = [read(t, r, at) for r in range(2 * size + 2)]
            for p, pieces in enumerate(zip(transform(x[: size + 2], size), transform(x[size:], size))):
                value = jnp.concatenate(pieces, 0)
                high = value.astype(BF16)
                s_ref[p, c, SLOTS[t], :, 0:LANES] = high
                s_ref[p, c, SLOTS[t], :, LANES:] = (value - high.astype(F32)).astype(BF16)
        return carry

    lax.fori_loop(0, chunks, one, 0)

    gap = 3 * points
    part = 3 * LANES

    def other_work(n):
        for step in beside[n * len(beside) // gap : (n + 1) * len(beside) // gap]:
            step()

    def rows_of(out):
        return out.reshape(chunks, -1, 2, SUB, out.shape[1])

    def whole(out, at):
        return out[..., 2 * at * part : (2 * at + 1) * part] + out[..., (2 * at + 1) * part : (2 * at + 2) * part]

    for p in range(points):
        even, last, middle = right_operands(w_ref, p)
        d_even = rows_of(product(s_ref[p, :, 0:2].reshape(chunks * 4 * SUB, 2 * LANES), even))
        other_work(3 * p)
        one_frame, two_frame = (s_ref[p, :, n].reshape(chunks * 2 * SUB, 2 * LANES) for n in (2, 1))
        high = [f[:, :LANES] for f in (one_frame, two_frame)]
        low = [f[:, LANES:] for f in (one_frame, two_frame)]
        d_middle = rows_of(product(jnp.concatenate(high + low + high, 1), middle))
        other_work(3 * p + 1)
        d_last = rows_of(product(s_ref[p, :, 3].reshape(chunks * 2 * SUB, 2 * LANES), last))
        other_work(3 * p + 2)
        for n in range(2):
            first, third = whole(d_even[:, 0, n], 0), whole(d_even[:, 1, n], 0)
            mid, end = d_middle[:, 0, n], d_last[:, 0, n]
            frames = (
                first + mid[..., :part],
                mid[..., part:] + whole(end, 0),
                third + whole(end, 1),
                whole(end, 2),
            )
            for t, taps in enumerate(frames):
                y_ref[t, p, n] = shifted_sum(taps.reshape(width, part))

    for t in range(4):
        for tile in range(2):
            rows = outputs([y_ref[t, p, tile] for p in range(points)], size)
            for o, value in enumerate(rows):
                emit(t, tile * size + o, value)
        if done is not None:
            done(t)


def halo_rows(chans, par, from_even, from_odd, r):
    return ungroup_frames([jnp.where(par == 0, from_even[g, r], from_odd[g, r]) for g in range(3)], chans)


def third_kernel(chans, par_ref, cp_ref, ra0, ra1, rc0, rc1, w_ref, w2_ref, w1_ref, out_ref, u2_ref, u1_ref, x_ref, s_ref, y_ref):
    rows, width = cp_ref.shape[1:3]
    cols = width - SUB
    for r in range(3):
        for at, even, odd, ceven, codd in ((r, ra1, ra0, rc1, rc0), (r + 3, ra0, ra1, rc0, rc1)):
            for t, frame in enumerate(halo_rows(chans, par_ref[0], even, odd, r)):
                x_ref[t, at, 0:cols] = frame
            for t, frame in enumerate(halo_rows(chans, par_ref[0], ceven, codd, r)):
                x_ref[t, at, cols:] = frame

    def read(t, r, at):
        if 3 <= r < 3 + rows:
            return cp_ref[t, r - 3, at]
        return x_ref[t, r if r < 3 else r - rows, at]

    def emit(t, o, value):
        out_ref[t, o] = value

    beside = prepare_all(w2_ref, u2_ref, POINTS[(rows + 2) // 2]) + prepare_all(w1_ref, u1_ref, POINTS[rows // 2])
    conv(read, rows, width, s_ref, y_ref, w_ref, emit, beside=beside)


def last_kernel(chans, par_ref, g_ref, s2_ref, s1_ref, rb0, rb1, rc0, rc1, w2_ref, w1_ref, out_hbm,
                e_ref, x1_ref, s_ref, y_ref, stage_ref, sems):
    frames, rows, width, _ = s2_ref.shape
    cols = width - SUB
    for r in range(3):
        for side, even, odd, ceven, codd in ((0, rb1, rb0, rc1, rc0), (1, rb0, rb1, rc0, rc1)):
            for t, frame in enumerate(halo_rows(chans, par_ref[0], even, odd, r)):
                e_ref[side, r, t, 0:cols] = frame
            for t, frame in enumerate(halo_rows(chans, par_ref[0], ceven, codd, 3 + r)):
                e_ref[side, r, t, cols:] = frame

    def slope2(t, r, at):
        if 2 <= r < 2 + rows:
            return s2_ref[t, r - 2, at]
        return e_ref[0, r, t, at] if r < 2 else e_ref[1, r - 2 - rows, t, at]

    def emit2(t, o, value):
        slope = s1_ref[t, o - 1] if 1 <= o < 1 + rows else e_ref[0 if o < 1 else 1, 2, t]
        x1_ref[t, o] = value * slope

    def emit1(t, o, value):
        stage_ref[t, o] = value[0:cols, 0:chans]

    def copy_out(t):
        return pltpu.make_async_copy(stage_ref.at[t], out_hbm.at[t], sems.at[t])

    conv(lambda t, r, at: g_ref[t, r, at] * slope2(t, r, at), (rows + 2) // 2, width, s_ref, y_ref, w2_ref, emit2)
    conv(
        lambda t, r, at: x1_ref[t, r, at], rows // 2, width, s_ref, y_ref, w1_ref, emit1, lambda t: copy_out(t).start()
    )
    for t in range(frames):
        copy_out(t).wait()


def swap(value, axis, which):
    count = lax.axis_size(axis)
    pairs = []
    for low in range(1 - which, count - 1, 2):
        pairs += [(low, low + 1), (low + 1, low)]
    return lax.ppermute(value, axis, pairs)


def swaps(first, second, axis):
    got = []
    for which, value in enumerate((first, second)):
        got.append(swap(value, axis, which))
    return got


def call(body, out_shape, args, scratch=(), hbm=False, hbm_out=False, alias=None, vmem=40 << 20, flops=0, cost=0):
    hbm_spec = pl.BlockSpec(memory_space=pltpu.HBM)
    where, out = hbm_spec if hbm else VMEM_SPEC, hbm_spec if hbm_out else VMEM_SPEC
    return pl.pallas_call(
        body,
        out_shape=out_shape,
        in_specs=[SMEM_SPEC if a.dtype == jnp.int32 else where for a in args],
        out_specs=jax.tree.map(lambda _: out, out_shape),
        scratch_shapes=list(scratch),
        input_output_aliases=alias or {},
        compiler_params=pltpu.CompilerParams(vmem_limit_bytes=vmem),
        cost_estimate=pl.CostEstimate(flops=flops, bytes_accessed=cost, transcendentals=0),
    )(*args)


def program(cotangent, stored_first, stored_second, w_first, w_second, w_third):
    frames, rows, cols, chans = cotangent.shape
    width = cols + SUB
    par = jnp.stack([(lax.axis_index("ha") + 1) % 2, (lax.axis_index("wa") + 1) % 2]).astype(jnp.int32)

    def arr(*shape, dtype=F32):
        return jax.ShapeDtypeStruct(shape, dtype)

    def vmem(*shape, dtype=F32):
        return pltpu.VMEM(shape, dtype)

    edge = arr(frames, rows, SUB, LANES)
    own = arr(frames, rows, width, LANES)
    message = arr(3, 3, cols, LANES)
    corner = arr(3, 6, SUB, LANES)
    fields = tuple(pltpu.with_memory_space_constraint(x, pltpu.HBM) for x in (cotangent, stored_second, stored_first))
    raw = arr(frames, rows, cols, chans)
    ma0, ma1, wp0, wp1, cp, sec, fst = call(
        pack_kernel,
        (message,) * 2 + (edge,) * 2 + (own, raw, raw),
        (par,) + fields,
        [vmem(frames, rows, cols, chans), vmem(2, 2, frames, rows, SUB, LANES), pltpu.SemaphoreType.DMA((3,))],
        hbm=True,
    )
    ra0, ra1 = swaps(ma0, ma1, "ha")
    rw0, rw1 = swaps(wp0, wp1, "wa")
    mb0, mb1, s2, s1 = call(slope_kernel, (message,) * 2 + (own,) * 2, (par, sec, fst))
    mc0, mc1, cp, s2, s1, mb0, mb1 = call(
        functools.partial(corner_kernel, chans),
        (corner,) * 2 + (own,) * 3 + (message,) * 2,
        (par, rw0, rw1, cp, s2, s1, mb0, mb1),
        alias={n + 3: n + 2 for n in range(5)},
    )
    rc0, rc1 = swaps(mc0, mc1, "ha")
    rb0, rb1 = swaps(mb0, mb1, "ha")

    def weights(size):
        return arr(len(POINTS[size]), 3, 2, LANES, 3 * LANES, dtype=BF16)

    size3, size2, size1 = rows, (rows + 2) // 2, rows // 2
    u3 = call(functools.partial(weight_kernel, POINTS[size3]), weights(size3), (w_third,))

    def scratch(size):
        points = len(POINTS[size])
        return [
            vmem(points, width // SUB, frames, 2 * SUB, 2 * LANES, dtype=BF16),
            vmem(frames, points, 2, width, LANES),
        ]

    grad, u2, u1 = call(
        functools.partial(third_kernel, chans),
        (arr(frames, rows + 4, width, LANES), weights(size2), weights(size1)),
        (par, cp, ra0, ra1, rc0, rc1, u3, w_second, w_first),
        [vmem(frames, 6, width, LANES)] + scratch(size3),
    )
    return call(
        functools.partial(last_kernel, chans),
        arr(frames, rows, cols, chans),
        (par, grad, s2, s1, rb0, rb1, rc0, rc1, u2, u1),
        [vmem(2, 3, frames, width, LANES), vmem(frames, rows + 2, width, LANES)]
        + scratch(size2)
        + [vmem(frames, rows, cols, chans), pltpu.SemaphoreType.DMA((frames,))],
        hbm_out=True,
    )


def solution(mesh):
    in_specs = (
        P("clip", "ha", "wa", None),
        P("clip", "ha", "wa", None),
        P("clip", "ha", "wa", None),
        P(),
        P(),
        P(),
    )
    out_specs = P("clip", "ha", "wa", None)
    return jax.shard_map(program, mesh=mesh, in_specs=in_specs, out_specs=out_specs, check_vma=False)
```

```python
import functools

import jax
import jax.numpy as jnp
from jax import lax
from jax.experimental import pallas as pl
from jax.experimental.pallas import tpu as pltpu
from jax.sharding import PartitionSpec as P


LANES = 128
SUB = 8
F32 = jnp.float32
BF16 = jnp.bfloat16
VMEM_SPEC = pl.BlockSpec(memory_space=pltpu.VMEM)
HBM_SPEC = pl.BlockSpec(memory_space=pltpu.HBM)


def parity(axis):
    return (lax.axis_index(axis) + 1) % 2


def silu_slope(value):
    sigma = 1.0 / (1.0 + jnp.exp(-value))
    return sigma * (1.0 + value * (1.0 - sigma))


def roll(value, shift, axis):
    return pltpu.roll(value, shift % value.shape[axis], axis)


def lane_of(shape):
    return lax.broadcasted_iota(jnp.int32, shape, len(shape) - 1)


def sub_of(shape):
    return lax.broadcasted_iota(jnp.int32, shape, len(shape) - 2)


def group_frames(frames, chans):
    first, second, third, fourth = frames
    part = LANES - chans
    lane = lane_of(first.shape)
    packed = []
    for index, frame in enumerate((first, second, third)):
        packed.append(jnp.where(lane < chans, frame, roll(fourth, chans - part * index, 1)))
    return packed


def ungroup_frames(groups, chans):
    part = LANES - chans
    lane = lane_of(groups[0].shape)
    frames = [jnp.where(lane < chans, group, 0.0) for group in groups]
    fourth = jnp.zeros_like(groups[0])
    for index in reversed(range(3)):
        moved = roll(groups[index], part * (index + 1), 1)
        fourth = jnp.where(lane < part * (index + 1), moved, fourth)
    return frames + [jnp.where(lane < chans, fourth, 0.0)]


def group_row(src, h, cols, chans):
    return group_frames([src[t, h, 0:cols] for t in range(4)], chans)


def pack_kernel(cot_hbm, sec_hbm, fst_hbm, ma0, ma1, wp0, wp1, cp_ref, sec_ref, fst_ref, raw_ref, edge_ref, sems):
    frames, rows, cols, chans = cot_hbm.shape
    copies = [
        pltpu.make_async_copy(src, dst, sems.at[a])
        for a, (src, dst) in enumerate(((cot_hbm, raw_ref), (sec_hbm, sec_ref), (fst_hbm, fst_ref)))
    ]
    for copy in copies:
        copy.start()
    cp_ref[...] = jnp.zeros(cp_ref.shape, F32)
    edge_ref[...] = jnp.zeros(edge_ref.shape, F32)
    copies[0].wait()
    cp_ref[:, :, 0:cols, 0:chans] = raw_ref[...]

    def rows_out(top, low):
        for r in range(3):
            for dst, h in ((top, r), (low, rows - 3 + r)):
                for g, val in enumerate(group_row(cp_ref, h, cols, chans)):
                    dst[g, r] = val

    @pl.when(parity("ha") == 0)
    def _():
        rows_out(ma1, ma0)

    @pl.when(parity("ha") != 0)
    def _():
        rows_out(ma0, ma1)

    for a, ref in ((0, sec_ref), (1, fst_ref)):
        copies[1 + a].wait()
        for side, start in enumerate((0, cols - SUB)):
            edge_ref[a, side, :, :, :, 0:chans] = silu_slope(ref[:, :, start : start + SUB])

    def cols_out(left, right):
        sub = sub_of((SUB, LANES))
        for t in range(frames):
            for h in range(rows):
                c0, a0, b0 = cp_ref[t, h, 0:SUB], edge_ref[0, 0, t, h], edge_ref[1, 0, t, h]
                c7, a7, b7 = cp_ref[t, h, cols - SUB : cols], edge_ref[0, 1, t, h], edge_ref[1, 1, t, h]
                right[t, h] = jnp.where(
                    sub >= 5, c7, jnp.where((sub == 2) | (sub == 3), roll(a7, 4, 0), jnp.where(sub == 1, roll(b7, 2, 0), 0.0))
                )
                left[t, h] = jnp.where(
                    sub < 3, c0, jnp.where((sub == 4) | (sub == 5), roll(a0, 4, 0), jnp.where(sub == 6, roll(b0, 6, 0), 0.0))
                )

    @pl.when(parity("wa") == 0)
    def _():
        cols_out(wp1, wp0)

    @pl.when(parity("wa") != 0)
    def _():
        cols_out(wp0, wp1)


def slope_kernel(wanted, sec_ref, fst_ref, w_hbm, mb0, mb1, s2_ref, s1_ref, u_ref, w_ref, sem):
    frames, rows, cols, chans = sec_ref.shape
    load = pltpu.make_async_copy(w_hbm, w_ref, sem)
    load.start()
    blank = jnp.zeros((cols, LANES), F32)
    for src, ref in ((sec_ref, s2_ref), (fst_ref, s1_ref)):
        for t in range(frames):
            for h in range(rows):
                ref[t, h, 0:cols] = blank
                ref[t, h, 0:cols, 0:chans] = silu_slope(src[t, h])

    def rows_out(top, low):
        for src, h, dst, at in (
            (s2_ref, 0, top, 0),
            (s2_ref, 1, top, 1),
            (s1_ref, 0, top, 2),
            (s2_ref, rows - 2, low, 0),
            (s2_ref, rows - 1, low, 1),
            (s1_ref, rows - 1, low, 2),
        ):
            for g, val in enumerate(group_row(src, h, cols, chans)):
                dst[g, at] = val

    @pl.when(parity("ha") == 0)
    def _():
        rows_out(mb1, mb0)

    @pl.when(parity("ha") != 0)
    def _():
        rows_out(mb0, mb1)

    load.wait()
    for step in prepare_all(w_ref, u_ref, wanted):
        step()


def corner_kernel(chans, rw0, rw1, _c, _s2, _s1, _b0, _b1, mc0, mc1, cp_ref, s2_ref, s1_ref, _mb0, _mb1):
    frames, rows = rw0.shape[:2]
    cols = cp_ref.shape[2] - SUB
    even = parity("wa") == 0
    sub = sub_of((SUB, LANES))
    for t in range(frames):
        for h in range(rows):
            left = jnp.where(even, rw1[t, h], rw0[t, h])
            right = jnp.where(even, rw0[t, h], rw1[t, h])
            cp_ref[t, h, cols:] = jnp.where(sub < 3, right, jnp.where(sub >= 5, left, 0.0))
            s2_ref[t, h, cols:] = jnp.where(sub < 2, roll(right, 4, 0), jnp.where(sub >= 6, roll(left, 4, 0), 0.0))
            s1_ref[t, h, cols:] = jnp.where(sub == 0, roll(right, 2, 0), jnp.where(sub == 7, roll(left, 6, 0), 0.0))

    def out(top, low):
        def put(src, h, dst, at):
            for g, val in enumerate(group_frames([src[t, h, cols:] for t in range(frames)], chans)):
                dst[g, at] = val

        for r in range(3):
            put(cp_ref, r, top, r)
            put(cp_ref, rows - 3 + r, low, r)
        for r in range(2):
            put(s2_ref, r, top, 3 + r)
            put(s2_ref, rows - 2 + r, low, 3 + r)
        put(s1_ref, 0, top, 5)
        put(s1_ref, rows - 1, low, 5)

    @pl.when(parity("ha") == 0)
    def _():
        out(mc1, mc0)

    @pl.when(parity("ha") != 0)
    def _():
        out(mc0, mc1)


def prepare(w_ref, out_ref, wanted, k, i, which):
    chans = w_ref.shape[3]
    blank = jnp.zeros((chans, LANES - chans), F32)
    f0, f1, f2 = (jnp.concatenate([w_ref[i, 2 - m, k], blank], 1) for m in range(3))
    points = {
        0: lambda: f0 * 0.25,
        1: lambda: (f0 + f1 + f2) * (-1 / 6),
        2: lambda: (f1 - f0 - f2) * (1 / 6),
        3: lambda: f0 * (1 / 24) + f1 * (1 / 12) + f2 * (1 / 6),
        4: lambda: f0 * (1 / 24) - f1 * (1 / 12) + f2 * (1 / 6),
        5: lambda: f2,
    }
    lanes = pl.ds((2 - i) * LANES, LANES)
    for n in which:
        value = points[wanted[n]]()
        high = value.astype(BF16)
        out_ref[n, k, 0, 0:chans, lanes] = high
        out_ref[n, k, 1, 0:chans, lanes] = (value - high.astype(F32)).astype(BF16)


def prepare_all(w_ref, out_ref, wanted):
    chans = w_ref.shape[3]

    def clear(n, k):
        out_ref[n, k, :, chans:] = jnp.zeros((2, LANES - chans, 3 * LANES), BF16)

    steps = []
    for k in range(3):
        for n in range(len(wanted)):
            steps.append(functools.partial(clear, n, k))
            for i in range(3):
                steps.append(functools.partial(prepare, w_ref, out_ref, wanted, k, i, (n,)))
    return steps


POINTS = {2: (0, 1, 2, 5), 3: (0, 1, 2, 3, 5), 4: (0, 1, 2, 3, 4, 5)}


def transform(x, size):
    if size == 2:
        return 4.0 * (x[0] - x[2]), -3.0 * (x[1] + x[2]), 3.0 * (x[1] - x[2]), x[3] - x[1]
    if size == 3:
        a, b = x[3] - x[1], x[3] - 2.0 * x[1]
        return (
            4.0 * (x[0] - x[2]) + 2.0 * a,
            3.0 * (b - x[2]),
            2.0 * x[1] - 3.0 * x[2] + x[3],
            4.0 * a,
            x[4] - x[2] - 2.0 * a,
        )
    a, b = x[4] - 4.0 * x[2], x[3] - 4.0 * x[1]
    c, e = x[4] - x[2], 2.0 * (x[3] - x[1])
    return 4.0 * x[0] - 5.0 * x[2] + x[4], a + b, a - b, c + e, c - e, 4.0 * x[1] - 5.0 * x[3] + x[5]


def outputs(y, size):
    plus, minus = y[1] + y[2], y[1] - y[2]
    if size == 2:
        return y[0] + plus, minus + y[3]
    if size == 3:
        return y[0] + plus + y[3], minus + 2.0 * y[3], plus + 4.0 * y[3] + y[4]
    far, odd = y[3] + y[4], y[3] - y[4]
    return y[0] + plus + far, minus + 2.0 * odd, plus + 4.0 * far, minus + 8.0 * odd + y[5]


def right_operands(w_ref, p):
    zero = jnp.zeros((LANES, LANES), BF16)
    near, far = [], []
    for k in range(3):
        parts = [w_ref[p, k, part] for part in range(2)]
        own = [
            jnp.concatenate([r[:, : 2 * LANES], jnp.concatenate([zero, r[:, :LANES]], 1)], 0) for r in parts
        ]
        later = [
            jnp.concatenate([jnp.concatenate([r[:, 2 * LANES :], zero], 1), r[:, LANES:]], 0) for r in parts
        ]
        near.append(jnp.concatenate([own[0], own[0], own[1]], 1))
        far.append(jnp.concatenate([later[0], later[0], later[1]], 1))
    return jnp.concatenate(near, 0), jnp.concatenate(far, 0)


def product(left, right):
    left = jnp.concatenate([left, left[:, : 2 * LANES]], 1)
    return lax.dot_general(left, right, (((1,), (1,)), ((), ())), preferred_element_type=F32)


def shifted_sum(taps):
    two = 2 * LANES
    return roll(taps[:, :two], -1, 0) + taps[:, two : 2 * two] + roll(taps[:, 2 * two :], 1, 0)


def conv(read, size, width, s_ref, y_ref, w_ref, emit, done=None, beside=(), ready=()):
    chunks = width // SUB
    points = len(POINTS[size])

    def one(c, carry):
        at = pl.ds(pl.multiple_of(c * SUB, SUB), SUB)
        for t in range(4):
            pair, a = t // 2, t % 2
            x = [read(t, r, at) for r in range(2 * size + 2)]
            for p, pieces in enumerate(zip(transform(x[: size + 2], size), transform(x[size:], size))):
                value = jnp.concatenate(pieces, 0)
                high = value.astype(BF16)
                s_ref[p, c, pair, :, a * LANES : (a + 1) * LANES] = high
                s_ref[p, c, pair, :, (2 + a) * LANES : (3 + a) * LANES] = (value - high.astype(F32)).astype(BF16)
        return carry

    lax.fori_loop(0, chunks, one, 0)
    for load in ready:
        load.wait()

    wide = 4 * LANES
    gap = 2 * points

    def other_work(n):
        for step in beside[n * len(beside) // gap : (n + 1) * len(beside) // gap]:
            step()

    for p in range(points):
        near, far = right_operands(w_ref, p)
        own = product(s_ref[p].reshape(chunks * 4 * SUB, wide), near).reshape(chunks, 2, 2, SUB, 6 * LANES)
        other_work(2 * p)
        later = product(s_ref[p, :, 1].reshape(chunks * 2 * SUB, wide), far).reshape(chunks, 2, SUB, 6 * LANES)
        other_work(2 * p + 1)
        for n in range(2):
            y_ref[0, p, n] = shifted_sum((own[:, 0, n] + later[:, n]).reshape(width, 6 * LANES))
            y_ref[1, p, n] = shifted_sum(own[:, 1, n].reshape(width, 6 * LANES))

    for t in range(4):
        lanes = pl.ds(t % 2 * LANES, LANES)
        for tile in range(2):
            rows = outputs([y_ref[t // 2, p, tile, :, lanes] for p in range(points)], size)
            for o, value in enumerate(rows):
                emit(t, tile * size + o, value)
        if done is not None:
            done(t)


def halo_rows(chans, from_even, from_odd, r):
    return ungroup_frames([jnp.where(parity("ha") == 0, from_even[g, r], from_odd[g, r]) for g in range(3)], chans)


def third_kernel(chans, cp_ref, ra0, ra1, rc0, rc1, w_ref, w2_hbm, w1_hbm, out_ref, u2_ref, u1_ref, x_ref, s_ref, y_ref,
                 w2_ref, w1_ref, sems):
    loads = [pltpu.make_async_copy(a, b, sems.at[n]) for n, (a, b) in enumerate(((w2_hbm, w2_ref), (w1_hbm, w1_ref)))]
    for load in loads:
        load.start()
    rows, width = cp_ref.shape[1:3]
    cols = width - SUB
    for r in range(3):
        for at, even, odd, ceven, codd in ((r, ra1, ra0, rc1, rc0), (r + 3, ra0, ra1, rc0, rc1)):
            for t, frame in enumerate(halo_rows(chans, even, odd, r)):
                x_ref[t, at, 0:cols] = frame
            for t, frame in enumerate(halo_rows(chans, ceven, codd, r)):
                x_ref[t, at, cols:] = frame

    def read(t, r, at):
        if 3 <= r < 3 + rows:
            return cp_ref[t, r - 3, at]
        return x_ref[t, r if r < 3 else r - rows, at]

    def emit(t, o, value):
        out_ref[t, o] = value

    beside = prepare_all(w2_ref, u2_ref, POINTS[(rows + 2) // 2]) + prepare_all(w1_ref, u1_ref, POINTS[rows // 2])
    conv(read, rows, width, s_ref, y_ref, w_ref, emit, beside=beside, ready=loads)


def last_kernel(chans, g_ref, s2_ref, s1_ref, rb0, rb1, rc0, rc1, w2_ref, w1_ref, out_hbm,
                e_ref, x1_ref, s_ref, y_ref, stage_ref, sems):
    frames, rows, width, _ = s2_ref.shape
    cols = width - SUB
    for r in range(3):
        for side, even, odd, ceven, codd in ((0, rb1, rb0, rc1, rc0), (1, rb0, rb1, rc0, rc1)):
            for t, frame in enumerate(halo_rows(chans, even, odd, r)):
                e_ref[side, r, t, 0:cols] = frame
            for t, frame in enumerate(halo_rows(chans, ceven, codd, 3 + r)):
                e_ref[side, r, t, cols:] = frame

    def slope2(t, r, at):
        if 2 <= r < 2 + rows:
            return s2_ref[t, r - 2, at]
        return e_ref[0, r, t, at] if r < 2 else e_ref[1, r - 2 - rows, t, at]

    def emit2(t, o, value):
        slope = s1_ref[t, o - 1] if 1 <= o < 1 + rows else e_ref[0 if o < 1 else 1, 2, t]
        x1_ref[t, o] = value * slope

    def emit1(t, o, value):
        stage_ref[t, o] = value[0:cols, 0:chans]

    def copy_out(t):
        return pltpu.make_async_copy(stage_ref.at[t], out_hbm.at[t], sems.at[t])

    conv(lambda t, r, at: g_ref[t, r, at] * slope2(t, r, at), (rows + 2) // 2, width, s_ref, y_ref, w2_ref, emit2)
    conv(
        lambda t, r, at: x1_ref[t, r, at], rows // 2, width, s_ref, y_ref, w1_ref, emit1, lambda t: copy_out(t).start()
    )
    for t in range(frames):
        copy_out(t).wait()


def swap(value, axis, which):
    count = lax.axis_size(axis)
    pairs = []
    for low in range(1 - which, count - 1, 2):
        pairs += [(low, low + 1), (low + 1, low)]
    return lax.ppermute(value, axis, pairs)


def swaps(first, second, axis):
    got = []
    for which, value in enumerate((first, second)):
        got.append(swap(value, axis, which))
    return got


def call(body, out_shape, args, scratch=(), hbm=(), hbm_out=False, alias=None, vmem=40 << 20):
    out = HBM_SPEC if hbm_out else VMEM_SPEC
    return pl.pallas_call(
        body,
        out_shape=out_shape,
        in_specs=[HBM_SPEC if n in hbm else VMEM_SPEC for n in range(len(args))],
        out_specs=jax.tree.map(lambda _: out, out_shape),
        scratch_shapes=list(scratch),
        input_output_aliases=alias or {},
        compiler_params=pltpu.CompilerParams(vmem_limit_bytes=vmem),
    )(*args)


def program(cotangent, stored_first, stored_second, w_first, w_second, w_third):
    frames, rows, cols, chans = cotangent.shape
    width = cols + SUB

    def arr(*shape, dtype=F32):
        return jax.ShapeDtypeStruct(shape, dtype)

    def vmem(*shape, dtype=F32):
        return pltpu.VMEM(shape, dtype)

    edge = arr(frames, rows, SUB, LANES)
    own = arr(frames, rows, width, LANES)
    message = arr(3, 3, cols, LANES)
    corner = arr(3, 6, SUB, LANES)
    *fields, third, second, first = (
        pltpu.with_memory_space_constraint(x, pltpu.HBM)
        for x in (cotangent, stored_second, stored_first, w_third, w_second, w_first)
    )
    raw = arr(frames, rows, cols, chans)
    ma0, ma1, wp0, wp1, cp, sec, fst = call(
        pack_kernel,
        (message,) * 2 + (edge,) * 2 + (own, raw, raw),
        tuple(fields),
        [vmem(frames, rows, cols, chans), vmem(2, 2, frames, rows, SUB, LANES), pltpu.SemaphoreType.DMA((3,))],
        hbm=(0, 1, 2),
    )
    ra0, ra1 = swaps(ma0, ma1, "ha")
    rw0, rw1 = swaps(wp0, wp1, "wa")

    def weights(size):
        return arr(len(POINTS[size]), 3, 2, LANES, 3 * LANES, dtype=BF16)

    size3, size2, size1 = rows, (rows + 2) // 2, rows // 2
    mb0, mb1, s2, s1, u3 = call(
        functools.partial(slope_kernel, POINTS[size3]),
        (message,) * 2 + (own,) * 2 + (weights(size3),),
        (sec, fst, third),
        [vmem(*third.shape), pltpu.SemaphoreType.DMA],
        hbm=(2,),
    )
    mc0, mc1, cp, s2, s1, mb0, mb1 = call(
        functools.partial(corner_kernel, chans),
        (corner,) * 2 + (own,) * 3 + (message,) * 2,
        (rw0, rw1, cp, s2, s1, mb0, mb1),
        alias={n + 2: n + 2 for n in range(5)},
    )
    rc0, rc1 = swaps(mc0, mc1, "ha")
    rb0, rb1 = swaps(mb0, mb1, "ha")

    def scratch(size):
        points = len(POINTS[size])
        return [
            vmem(points, width // SUB, 2, 2 * SUB, 4 * LANES, dtype=BF16),
            vmem(2, points, 2, width, 2 * LANES),
        ]

    grad, u2, u1 = call(
        functools.partial(third_kernel, chans),
        (arr(frames, rows + 4, width, LANES), weights(size2), weights(size1)),
        (cp, ra0, ra1, rc0, rc1, u3, second, first),
        [vmem(frames, 6, width, LANES)]
        + scratch(size3)
        + [vmem(*second.shape), vmem(*first.shape), pltpu.SemaphoreType.DMA((2,))],
        hbm=(6, 7),
    )
    return call(
        functools.partial(last_kernel, chans),
        arr(frames, rows, cols, chans),
        (grad, s2, s1, rb0, rb1, rc0, rc1, u2, u1),
        [vmem(2, 3, frames, width, LANES), vmem(frames, rows + 2, width, LANES)]
        + scratch(size2)
        + [vmem(frames, rows, cols, chans), pltpu.SemaphoreType.DMA((frames,))],
        hbm_out=True,
    )


def solution(mesh):
    in_specs = (
        P("clip", "ha", "wa", None),
        P("clip", "ha", "wa", None),
        P("clip", "ha", "wa", None),
        P(),
        P(),
        P(),
    )
    out_specs = P("clip", "ha", "wa", None)
    return jax.shard_map(program, mesh=mesh, in_specs=in_specs, out_specs=out_specs, check_vma=False)
```

```python
import functools

import jax
import jax.numpy as jnp
from jax import lax
from jax.experimental import pallas as pl
from jax.experimental.pallas import tpu as pltpu
from jax.sharding import PartitionSpec as P


LANES = 128
SUB = 8
F32 = jnp.float32
BF16 = jnp.bfloat16
VMEM_SPEC = pl.BlockSpec(memory_space=pltpu.VMEM)
HBM_SPEC = pl.BlockSpec(memory_space=pltpu.HBM)


def parity(axis):
    return (lax.axis_index(axis) + 1) % 2


def silu_slope(value):
    sigma = 1.0 / (1.0 + jnp.exp(-value))
    return sigma * (1.0 + value * (1.0 - sigma))


def roll(value, shift, axis):
    return pltpu.roll(value, shift % value.shape[axis], axis)


def lane_of(shape):
    return lax.broadcasted_iota(jnp.int32, shape, len(shape) - 1)


def sub_of(shape):
    return lax.broadcasted_iota(jnp.int32, shape, len(shape) - 2)


def group_frames(frames, chans):
    first, second, third, fourth = frames
    part = LANES - chans
    lane = lane_of(first.shape)
    packed = []
    for index, frame in enumerate((first, second, third)):
        packed.append(jnp.where(lane < chans, frame, roll(fourth, chans - part * index, 1)))
    return packed


def ungroup_frames(groups, chans):
    part = LANES - chans
    lane = lane_of(groups[0].shape)
    frames = [jnp.where(lane < chans, group, 0.0) for group in groups]
    fourth = jnp.zeros_like(groups[0])
    for index in reversed(range(3)):
        moved = roll(groups[index], part * (index + 1), 1)
        fourth = jnp.where(lane < part * (index + 1), moved, fourth)
    return frames + [jnp.where(lane < chans, fourth, 0.0)]


def group_row(src, h, cols, chans):
    return group_frames([src[t, h, 0:cols] for t in range(4)], chans)


def pack_kernel(cot_hbm, sec_hbm, fst_hbm, ma0, ma1, wp0, wp1, cp_ref, sec_ref, fst_ref, raw_ref, edge_ref, row_ref, sems):
    frames, rows, cols, chans = cot_hbm.shape
    copies = [
        pltpu.make_async_copy(src, dst, sems.at[a])
        for a, (src, dst) in enumerate(((cot_hbm, raw_ref), (sec_hbm, sec_ref), (fst_hbm, fst_ref)))
    ]
    for copy in copies:
        copy.start()
    cp_ref[...] = jnp.zeros(cp_ref.shape, F32)
    edge_ref[...] = jnp.zeros(edge_ref.shape, F32)
    copies[0].wait()
    cp_ref[:, :, 0:cols, 0:chans] = raw_ref[...]

    row_ref[...] = jnp.zeros(row_ref.shape, F32)
    for copy in copies[1:]:
        copy.wait()
    for at, h in enumerate((0, rows - 1)):
        row_ref[:, at, :, 0:chans] = silu_slope(fst_ref[:, h])

    def rows_out(top, low):
        for r in range(3):
            for dst, h in ((top, r), (low, rows - 3 + r)):
                for g, val in enumerate(group_row(cp_ref, h, cols, chans)):
                    dst[g, r] = val
        for at, dst in enumerate((top, low)):
            for g, val in enumerate(group_row(row_ref, at, cols, chans)):
                dst[g, 3] = val

    @pl.when(parity("ha") == 0)
    def _():
        rows_out(ma1, ma0)

    @pl.when(parity("ha") != 0)
    def _():
        rows_out(ma0, ma1)

    for a, ref in ((0, sec_ref), (1, fst_ref)):
        for side, start in enumerate((0, cols - SUB)):
            edge_ref[a, side, :, :, :, 0:chans] = silu_slope(ref[:, :, start : start + SUB])

    def cols_out(left, right):
        sub = sub_of((SUB, LANES))
        for t in range(frames):
            for h in range(rows):
                c0, a0, b0 = cp_ref[t, h, 0:SUB], edge_ref[0, 0, t, h], edge_ref[1, 0, t, h]
                c7, a7, b7 = cp_ref[t, h, cols - SUB : cols], edge_ref[0, 1, t, h], edge_ref[1, 1, t, h]
                right[t, h] = jnp.where(
                    sub >= 5, c7, jnp.where((sub == 2) | (sub == 3), roll(a7, 4, 0), jnp.where(sub == 1, roll(b7, 2, 0), 0.0))
                )
                left[t, h] = jnp.where(
                    sub < 3, c0, jnp.where((sub == 4) | (sub == 5), roll(a0, 4, 0), jnp.where(sub == 6, roll(b0, 6, 0), 0.0))
                )

    @pl.when(parity("wa") == 0)
    def _():
        cols_out(wp1, wp0)

    @pl.when(parity("wa") != 0)
    def _():
        cols_out(wp0, wp1)


def slope_kernel(sec_ref, fst_ref, w_hbm, mb0, mb1, s2_ref, s1_ref, w_ref, sem):
    frames, rows, cols, chans = sec_ref.shape
    load = pltpu.make_async_copy(w_hbm, w_ref, sem)
    load.start()
    blank = jnp.zeros((cols, LANES), F32)
    for src, ref in ((sec_ref, s2_ref), (fst_ref, s1_ref)):
        for t in range(frames):
            for h in range(rows):
                ref[t, h, 0:cols] = blank
                ref[t, h, 0:cols, 0:chans] = silu_slope(src[t, h])

    def rows_out(top, low):
        for src, h, dst, at in (
            (s2_ref, 0, top, 0),
            (s2_ref, 1, top, 1),
            (s2_ref, rows - 2, low, 0),
            (s2_ref, rows - 1, low, 1),
        ):
            for g, val in enumerate(group_row(src, h, cols, chans)):
                dst[g, at] = val

    @pl.when(parity("ha") == 0)
    def _():
        rows_out(mb1, mb0)

    @pl.when(parity("ha") != 0)
    def _():
        rows_out(mb0, mb1)

    load.wait()


def corner_kernel(chans, rw0, rw1, _c, _s2, _s1, _b0, _b1, mc0, mc1, cp_ref, s2_ref, s1_ref, _mb0, _mb1):
    frames, rows = rw0.shape[:2]
    cols = cp_ref.shape[2] - SUB
    even = parity("wa") == 0
    sub = sub_of((SUB, LANES))
    for t in range(frames):
        for h in range(rows):
            left = jnp.where(even, rw1[t, h], rw0[t, h])
            right = jnp.where(even, rw0[t, h], rw1[t, h])
            cp_ref[t, h, cols:] = jnp.where(sub < 3, right, jnp.where(sub >= 5, left, 0.0))
            s2_ref[t, h, cols:] = jnp.where(sub < 2, roll(right, 4, 0), jnp.where(sub >= 6, roll(left, 4, 0), 0.0))
            s1_ref[t, h, cols:] = jnp.where(sub == 0, roll(right, 2, 0), jnp.where(sub == 7, roll(left, 6, 0), 0.0))

    def out(top, low):
        def put(src, h, dst, at):
            for g, val in enumerate(group_frames([src[t, h, cols:] for t in range(frames)], chans)):
                dst[g, at] = val

        for r in range(3):
            put(cp_ref, r, top, r)
            put(cp_ref, rows - 3 + r, low, r)
        for r in range(2):
            put(s2_ref, r, top, 3 + r)
            put(s2_ref, rows - 2 + r, low, 3 + r)
        put(s1_ref, 0, top, 5)
        put(s1_ref, rows - 1, low, 5)

    @pl.when(parity("ha") == 0)
    def _():
        out(mc1, mc0)

    @pl.when(parity("ha") != 0)
    def _():
        out(mc0, mc1)


def prepare(w_ref, out_ref, wanted, k, i, which):
    chans = w_ref.shape[3]
    blank = jnp.zeros((chans, LANES - chans), F32)
    f0, f1, f2 = (jnp.concatenate([w_ref[i, 2 - m, k], blank], 1) for m in range(3))
    points = {
        0: lambda: f0 * 0.25,
        1: lambda: (f0 + f1 + f2) * (-1 / 6),
        2: lambda: (f1 - f0 - f2) * (1 / 6),
        3: lambda: f0 * (1 / 24) + f1 * (1 / 12) + f2 * (1 / 6),
        4: lambda: f0 * (1 / 24) - f1 * (1 / 12) + f2 * (1 / 6),
        5: lambda: f2,
    }
    lanes = pl.ds((2 - i) * LANES, LANES)
    for n in which:
        value = points[wanted[n]]()
        high = value.astype(BF16)
        out_ref[n, k, 0, 0:chans, lanes] = high
        out_ref[n, k, 1, 0:chans, lanes] = (value - high.astype(F32)).astype(BF16)


def prepare_point(w_ref, out_ref, wanted, n):
    chans = w_ref.shape[3]

    def clear(k):
        out_ref[n, k, :, chans:] = jnp.zeros((2, LANES - chans, 3 * LANES), BF16)

    steps = []
    for k in range(3):
        steps.append(functools.partial(clear, k))
        for i in range(3):
            steps.append(functools.partial(prepare, w_ref, out_ref, wanted, k, i, (n,)))
    return steps


def spread(steps, slots):
    return [steps[n * len(steps) // slots : (n + 1) * len(steps) // slots] for n in range(slots)]


POINTS = {2: (0, 1, 2, 5), 3: (0, 1, 2, 3, 5), 4: (0, 1, 2, 3, 4, 5)}


def transform(x, size):
    if size == 2:
        return 4.0 * (x[0] - x[2]), -3.0 * (x[1] + x[2]), 3.0 * (x[1] - x[2]), x[3] - x[1]
    if size == 3:
        a, b = x[3] - x[1], x[3] - 2.0 * x[1]
        return (
            4.0 * (x[0] - x[2]) + 2.0 * a,
            3.0 * (b - x[2]),
            2.0 * x[1] - 3.0 * x[2] + x[3],
            4.0 * a,
            x[4] - x[2] - 2.0 * a,
        )
    a, b = x[4] - 4.0 * x[2], x[3] - 4.0 * x[1]
    c, e = x[4] - x[2], 2.0 * (x[3] - x[1])
    return 4.0 * x[0] - 5.0 * x[2] + x[4], a + b, a - b, c + e, c - e, 4.0 * x[1] - 5.0 * x[3] + x[5]


def outputs(y, size):
    plus, minus = y[1] + y[2], y[1] - y[2]
    if size == 2:
        return y[0] + plus, minus + y[3]
    if size == 3:
        return y[0] + plus + y[3], minus + 2.0 * y[3], plus + 4.0 * y[3] + y[4]
    far, odd = y[3] + y[4], y[3] - y[4]
    return y[0] + plus + far, minus + 2.0 * odd, plus + 4.0 * far, minus + 8.0 * odd + y[5]


def right_operands(w_ref, p):
    zero = jnp.zeros((LANES, LANES), BF16)
    near, far = [], []
    for k in range(3):
        parts = [w_ref[p, k, part] for part in range(2)]
        own = [
            jnp.concatenate([r[:, : 2 * LANES], jnp.concatenate([zero, r[:, :LANES]], 1)], 0) for r in parts
        ]
        later = [
            jnp.concatenate([jnp.concatenate([r[:, 2 * LANES :], zero], 1), r[:, LANES:]], 0) for r in parts
        ]
        near.append(jnp.concatenate([own[0], own[0], own[1]], 1))
        far.append(jnp.concatenate([later[0], later[0], later[1]], 1))
    return jnp.concatenate(near, 0), jnp.concatenate(far, 0)


def product(left, right):
    left = jnp.concatenate([left, left[:, : 2 * LANES]], 1)
    return lax.dot_general(left, right, (((1,), (1,)), ((), ())), preferred_element_type=F32)


def shifted_sum(taps):
    two = 2 * LANES
    return roll(taps[:, :two], -1, 0) + taps[:, two : 2 * two] + roll(taps[:, 2 * two :], 1, 0)


def conv(read, size, width, s_ref, y_ref, w_ref, emit, done=None, beside=None):
    chunks = width // SUB
    points = len(POINTS[size])

    def one(c, carry):
        at = pl.ds(pl.multiple_of(c * SUB, SUB), SUB)
        for t in range(4):
            pair, a = t // 2, t % 2
            x = [read(t, r, at) for r in range(2 * size + 2)]
            for p, pieces in enumerate(zip(transform(x[: size + 2], size), transform(x[size:], size))):
                value = jnp.concatenate(pieces, 0)
                high = value.astype(BF16)
                s_ref[p, c, pair, :, a * LANES : (a + 1) * LANES] = high
                s_ref[p, c, pair, :, (2 + a) * LANES : (3 + a) * LANES] = (value - high.astype(F32)).astype(BF16)
        return carry

    lax.fori_loop(0, chunks, one, 0)
    wide = 4 * LANES

    def other_work(n):
        for step in beside[n] if beside else ():
            step()

    for p in range(points):
        near, far = right_operands(w_ref, p)
        own = product(s_ref[p].reshape(chunks * 4 * SUB, wide), near).reshape(chunks, 2, 2, SUB, 6 * LANES)
        other_work(2 * p)
        later = product(s_ref[p, :, 1].reshape(chunks * 2 * SUB, wide), far).reshape(chunks, 2, SUB, 6 * LANES)
        other_work(2 * p + 1)
        for n in range(2):
            y_ref[0, p, n] = shifted_sum((own[:, 0, n] + later[:, n]).reshape(width, 6 * LANES))
            y_ref[1, p, n] = shifted_sum(own[:, 1, n].reshape(width, 6 * LANES))

    for t in range(4):
        lanes = pl.ds(t % 2 * LANES, LANES)
        for tile in range(2):
            rows = outputs([y_ref[t // 2, p, tile, :, lanes] for p in range(points)], size)
            for o, value in enumerate(rows):
                emit(t, tile * size + o, value)
        if done is not None:
            done(t)


def halo_rows(chans, from_even, from_odd, r):
    return ungroup_frames([jnp.where(parity("ha") == 0, from_even[g, r], from_odd[g, r]) for g in range(3)], chans)


def third_kernel(chans, cp_ref, ra0, ra1, rc0, rc1, w3_ref, w2_hbm, out_ref, u2_ref, x_ref, u3_ref, s_ref, y_ref, w2_ref, sem):
    load = pltpu.make_async_copy(w2_hbm, w2_ref, sem)
    load.start()
    rows, width = cp_ref.shape[1:3]
    cols = width - SUB
    for r in range(3):
        for at, even, odd, ceven, codd in ((r, ra1, ra0, rc1, rc0), (r + 3, ra0, ra1, rc0, rc1)):
            for t, frame in enumerate(halo_rows(chans, even, odd, r)):
                x_ref[t, at, 0:cols] = frame
            for t, frame in enumerate(halo_rows(chans, ceven, codd, r)):
                x_ref[t, at, cols:] = frame

    def read(t, r, at):
        if 3 <= r < 3 + rows:
            return cp_ref[t, r - 3, at]
        return x_ref[t, r if r < 3 else r - rows, at]

    def emit(t, o, value):
        out_ref[t, o] = value

    own, later = POINTS[rows], POINTS[(rows + 2) // 2]
    for step in prepare_point(w3_ref, u3_ref, own, 0):
        step()
    slots = len(own) * 2
    beside = [[] for _ in range(slots)]
    for p in range(1, len(own)):
        for n, steps in enumerate(spread(prepare_point(w3_ref, u3_ref, own, p), 2)):
            beside[2 * p - 2 + n] += steps
    steps = [load.wait]
    for n in range(len(later)):
        steps += prepare_point(w2_ref, u2_ref, later, n)
    for n, some in enumerate(spread(steps, slots - 2)):
        beside[n + 2] += some
    conv(read, rows, width, s_ref, y_ref, u3_ref, emit, beside=beside)


def last_kernel(chans, g_ref, s2_ref, s1_ref, ra0, ra1, rb0, rb1, rc0, rc1, u2_ref, w1_hbm, out_hbm,
                e_ref, x1_ref, u1_ref, s_ref, y_ref, w1_ref, stage_ref, load_sem, sems):
    load = pltpu.make_async_copy(w1_hbm, w1_ref, load_sem)
    load.start()
    frames, rows, width, _ = s2_ref.shape
    cols = width - SUB
    for side, (even, odd) in enumerate(((1, 0), (0, 1))):
        for r in range(3):
            main, at = ((rb0, rb1), r) if r < 2 else ((ra0, ra1), 3)
            for t, frame in enumerate(halo_rows(chans, main[even], main[odd], at)):
                e_ref[side, r, t, 0:cols] = frame
            corners = (rc0, rc1)
            for t, frame in enumerate(halo_rows(chans, corners[even], corners[odd], 3 + r)):
                e_ref[side, r, t, cols:] = frame

    def slope2(t, r, at):
        if 2 <= r < 2 + rows:
            return s2_ref[t, r - 2, at]
        return e_ref[0, r, t, at] if r < 2 else e_ref[1, r - 2 - rows, t, at]

    def emit2(t, o, value):
        slope = s1_ref[t, o - 1] if 1 <= o < 1 + rows else e_ref[0 if o < 1 else 1, 2, t]
        x1_ref[t, o] = value * slope

    def emit1(t, o, value):
        stage_ref[t, o] = value[0:cols, 0:chans]

    def copy_out(t):
        return pltpu.make_async_copy(stage_ref.at[t], out_hbm.at[t], sems.at[t])

    size2, size1 = (rows + 2) // 2, rows // 2
    steps = [load.wait]
    for n in range(len(POINTS[size1])):
        steps += prepare_point(w1_ref, u1_ref, POINTS[size1], n)
    beside = [[], []] + spread(steps, 2 * len(POINTS[size2]) - 2)
    conv(lambda t, r, at: g_ref[t, r, at] * slope2(t, r, at), size2, width, s_ref, y_ref, u2_ref, emit2, beside=beside)
    conv(lambda t, r, at: x1_ref[t, r, at], size1, width, s_ref, y_ref, u1_ref, emit1, lambda t: copy_out(t).start())
    for t in range(frames):
        copy_out(t).wait()


def swap(value, axis, which):
    count = lax.axis_size(axis)
    pairs = []
    for low in range(1 - which, count - 1, 2):
        pairs += [(low, low + 1), (low + 1, low)]
    return lax.ppermute(value, axis, pairs)


def swaps(first, second, axis):
    got = []
    for which, value in enumerate((first, second)):
        got.append(swap(value, axis, which))
    return got


def call(body, out_shape, args, scratch=(), hbm=(), hbm_out=False, alias=None, vmem=40 << 20):
    out = HBM_SPEC if hbm_out else VMEM_SPEC
    return pl.pallas_call(
        body,
        out_shape=out_shape,
        in_specs=[HBM_SPEC if n in hbm else VMEM_SPEC for n in range(len(args))],
        out_specs=jax.tree.map(lambda _: out, out_shape),
        scratch_shapes=list(scratch),
        input_output_aliases=alias or {},
        compiler_params=pltpu.CompilerParams(vmem_limit_bytes=vmem),
    )(*args)


def program(cotangent, stored_first, stored_second, w_first, w_second, w_third):
    frames, rows, cols, chans = cotangent.shape
    width = cols + SUB

    def arr(*shape, dtype=F32):
        return jax.ShapeDtypeStruct(shape, dtype)

    def vmem(*shape, dtype=F32):
        return pltpu.VMEM(shape, dtype)

    edge = arr(frames, rows, SUB, LANES)
    own = arr(frames, rows, width, LANES)
    rows_a, rows_b = arr(3, 4, cols, LANES), arr(3, 2, cols, LANES)
    corner = arr(3, 6, SUB, LANES)
    *fields, third, second, first = (
        pltpu.with_memory_space_constraint(x, pltpu.HBM)
        for x in (cotangent, stored_second, stored_first, w_third, w_second, w_first)
    )
    raw = arr(frames, rows, cols, chans)
    ma0, ma1, wp0, wp1, cp, sec, fst = call(
        pack_kernel,
        (rows_a,) * 2 + (edge,) * 2 + (own, raw, raw),
        tuple(fields),
        [vmem(frames, rows, cols, chans), vmem(2, 2, frames, rows, SUB, LANES), vmem(frames, 2, cols, LANES), pltpu.SemaphoreType.DMA((3,))],
        hbm=(0, 1, 2),
    )
    ra0, ra1 = swaps(ma0, ma1, "ha")
    rw0, rw1 = swaps(wp0, wp1, "wa")

    def weights(size):
        return arr(len(POINTS[size]), 3, 2, LANES, 3 * LANES, dtype=BF16)

    size3, size2, size1 = rows, (rows + 2) // 2, rows // 2
    mb0, mb1, s2, s1, third = call(
        slope_kernel,
        (rows_b,) * 2 + (own,) * 2 + (arr(*third.shape),),
        (sec, fst, third),
        [pltpu.SemaphoreType.DMA],
        hbm=(2,),
    )
    mc0, mc1, cp, s2, s1, mb0, mb1 = call(
        functools.partial(corner_kernel, chans),
        (corner,) * 2 + (own,) * 3 + (rows_b,) * 2,
        (rw0, rw1, cp, s2, s1, mb0, mb1),
        alias={n + 2: n + 2 for n in range(5)},
    )
    rc0, rc1 = swaps(mc0, mc1, "ha")
    rb0, rb1 = swaps(mb0, mb1, "ha")

    def scratch(size):
        points = len(POINTS[size])
        return [
            vmem(points, width // SUB, 2, 2 * SUB, 4 * LANES, dtype=BF16),
            vmem(2, points, 2, width, 2 * LANES),
        ]

    grad, u2 = call(
        functools.partial(third_kernel, chans),
        (arr(frames, rows + 4, width, LANES), weights(size2)),
        (cp, ra0, ra1, rc0, rc1, third, second),
        [vmem(frames, 6, width, LANES), vmem(*weights(size3).shape, dtype=BF16)]
        + scratch(size3)
        + [vmem(*second.shape), pltpu.SemaphoreType.DMA],
        hbm=(6,),
    )
    return call(
        functools.partial(last_kernel, chans),
        arr(frames, rows, cols, chans),
        (grad, s2, s1, ra0, ra1, rb0, rb1, rc0, rc1, u2, first),
        [
            vmem(2, 3, frames, width, LANES),
            vmem(frames, rows + 2, width, LANES),
            vmem(*weights(size1).shape, dtype=BF16),
        ]
        + scratch(size2)
        + [
            vmem(*first.shape),
            vmem(frames, rows, cols, chans),
            pltpu.SemaphoreType.DMA,
            pltpu.SemaphoreType.DMA((frames,)),
        ],
        hbm=(10,),
        hbm_out=True,
    )


def solution(mesh):
    in_specs = (
        P("clip", "ha", "wa", None),
        P("clip", "ha", "wa", None),
        P("clip", "ha", "wa", None),
        P(),
        P(),
        P(),
    )
    out_specs = P("clip", "ha", "wa", None)
    return jax.shard_map(program, mesh=mesh, in_specs=in_specs, out_specs=out_specs, check_vma=False)
```

```python
import functools

import jax
import jax.numpy as jnp
from jax import lax
from jax.experimental import pallas as pl
from jax.experimental.pallas import tpu as pltpu
from jax.sharding import PartitionSpec as P


LANES = 128
SUB = 8
F32 = jnp.float32
BF16 = jnp.bfloat16
VMEM_SPEC = pl.BlockSpec(memory_space=pltpu.VMEM)
HBM_SPEC = pl.BlockSpec(memory_space=pltpu.HBM)


def parity(axis):
    return (lax.axis_index(axis) + 1) % 2


def silu_slope(value):
    sigma = 1.0 / (1.0 + jnp.exp(-value))
    return sigma * (1.0 + value * (1.0 - sigma))


def roll(value, shift, axis):
    return pltpu.roll(value, shift % value.shape[axis], axis)


def lane_of(shape):
    return lax.broadcasted_iota(jnp.int32, shape, len(shape) - 1)


def sub_of(shape):
    return lax.broadcasted_iota(jnp.int32, shape, len(shape) - 2)


def group_frames(frames, chans):
    first, second, third, fourth = frames
    part = LANES - chans
    lane = lane_of(first.shape)
    packed = []
    for index, frame in enumerate((first, second, third)):
        packed.append(jnp.where(lane < chans, frame, roll(fourth, chans - part * index, 1)))
    return packed


def ungroup_frames(groups, chans):
    part = LANES - chans
    lane = lane_of(groups[0].shape)
    frames = [jnp.where(lane < chans, group, 0.0) for group in groups]
    fourth = jnp.zeros_like(groups[0])
    for index in reversed(range(3)):
        moved = roll(groups[index], part * (index + 1), 1)
        fourth = jnp.where(lane < part * (index + 1), moved, fourth)
    return frames + [jnp.where(lane < chans, fourth, 0.0)]


def group_row(src, h, cols, chans):
    return group_frames([src[t, h, 0:cols] for t in range(4)], chans)


def pack_kernel(cot_hbm, sec_hbm, fst_hbm, ma0, ma1, wp0, wp1, cp_ref, sec_ref, fst_ref, raw_ref, edge_ref, row_ref, sems):
    frames, rows, cols, chans = cot_hbm.shape
    copies = [
        pltpu.make_async_copy(src, dst, sems.at[a])
        for a, (src, dst) in enumerate(((cot_hbm, raw_ref), (sec_hbm, sec_ref), (fst_hbm, fst_ref)))
    ]
    for copy in copies:
        copy.start()
    cp_ref[...] = jnp.zeros(cp_ref.shape, F32)
    edge_ref[...] = jnp.zeros(edge_ref.shape, F32)
    copies[0].wait()
    cp_ref[:, :, 0:cols, 0:chans] = raw_ref[...]

    row_ref[...] = jnp.zeros(row_ref.shape, F32)
    for copy in copies[1:]:
        copy.wait()
    for at, h in enumerate((0, rows - 1)):
        row_ref[:, at, :, 0:chans] = silu_slope(fst_ref[:, h])

    def rows_out(top, low):
        for r in range(3):
            for dst, h in ((top, r), (low, rows - 3 + r)):
                for g, val in enumerate(group_row(cp_ref, h, cols, chans)):
                    dst[g, r] = val
        for at, dst in enumerate((top, low)):
            for g, val in enumerate(group_row(row_ref, at, cols, chans)):
                dst[g, 3] = val

    @pl.when(parity("ha") == 0)
    def _():
        rows_out(ma1, ma0)

    @pl.when(parity("ha") != 0)
    def _():
        rows_out(ma0, ma1)

    for a, ref in ((0, sec_ref), (1, fst_ref)):
        for side, start in enumerate((0, cols - SUB)):
            edge_ref[a, side, :, :, :, 0:chans] = silu_slope(ref[:, :, start : start + SUB])

    def cols_out(left, right):
        sub = sub_of((SUB, LANES))
        for t in range(frames):
            for h in range(rows):
                c0, a0, b0 = cp_ref[t, h, 0:SUB], edge_ref[0, 0, t, h], edge_ref[1, 0, t, h]
                c7, a7, b7 = cp_ref[t, h, cols - SUB : cols], edge_ref[0, 1, t, h], edge_ref[1, 1, t, h]
                right[t, h] = jnp.where(
                    sub >= 5, c7, jnp.where((sub == 2) | (sub == 3), roll(a7, 4, 0), jnp.where(sub == 1, roll(b7, 2, 0), 0.0))
                )
                left[t, h] = jnp.where(
                    sub < 3, c0, jnp.where((sub == 4) | (sub == 5), roll(a0, 4, 0), jnp.where(sub == 6, roll(b0, 6, 0), 0.0))
                )

    @pl.when(parity("wa") == 0)
    def _():
        cols_out(wp1, wp0)

    @pl.when(parity("wa") != 0)
    def _():
        cols_out(wp0, wp1)


def slope_kernel(wanted, sec_ref, fst_ref, w3_hbm, w2_hbm, w1_hbm, mb0, mb1, s2_ref, s1_ref, u_ref, w2_ref, w1_ref, w_ref, sems):
    frames, rows, cols, chans = sec_ref.shape
    loads = [
        pltpu.make_async_copy(src, dst, sems.at[n])
        for n, (src, dst) in enumerate(((w3_hbm, w_ref), (w2_hbm, w2_ref), (w1_hbm, w1_ref)))
    ]
    for load in loads:
        load.start()
    blank = jnp.zeros((cols, LANES), F32)
    for src, ref in ((sec_ref, s2_ref), (fst_ref, s1_ref)):
        for t in range(frames):
            for h in range(rows):
                ref[t, h, 0:cols] = blank
                ref[t, h, 0:cols, 0:chans] = silu_slope(src[t, h])

    def rows_out(top, low):
        for src, h, dst, at in (
            (s2_ref, 0, top, 0),
            (s2_ref, 1, top, 1),
            (s2_ref, rows - 2, low, 0),
            (s2_ref, rows - 1, low, 1),
        ):
            for g, val in enumerate(group_row(src, h, cols, chans)):
                dst[g, at] = val

    @pl.when(parity("ha") == 0)
    def _():
        rows_out(mb1, mb0)

    @pl.when(parity("ha") != 0)
    def _():
        rows_out(mb0, mb1)

    loads[0].wait()
    for k in range(3):
        for step in prepare(w_ref, u_ref, wanted, k):
            step()
    for load in loads[1:]:
        load.wait()


def corner_kernel(chans, rw0, rw1, _c, _s2, _s1, _b0, _b1, mc0, mc1, cp_ref, s2_ref, s1_ref, _mb0, _mb1):
    frames, rows = rw0.shape[:2]
    cols = cp_ref.shape[2] - SUB
    even = parity("wa") == 0
    sub = sub_of((SUB, LANES))
    for t in range(frames):
        for h in range(rows):
            left = jnp.where(even, rw1[t, h], rw0[t, h])
            right = jnp.where(even, rw0[t, h], rw1[t, h])
            cp_ref[t, h, cols:] = jnp.where(sub < 3, right, jnp.where(sub >= 5, left, 0.0))
            s2_ref[t, h, cols:] = jnp.where(sub < 2, roll(right, 4, 0), jnp.where(sub >= 6, roll(left, 4, 0), 0.0))
            s1_ref[t, h, cols:] = jnp.where(sub == 0, roll(right, 2, 0), jnp.where(sub == 7, roll(left, 6, 0), 0.0))

    def out(top, low):
        def put(src, h, dst, at):
            for g, val in enumerate(group_frames([src[t, h, cols:] for t in range(frames)], chans)):
                dst[g, at] = val

        for r in range(3):
            put(cp_ref, r, top, r)
            put(cp_ref, rows - 3 + r, low, r)
        for r in range(2):
            put(s2_ref, r, top, 3 + r)
            put(s2_ref, rows - 2 + r, low, 3 + r)
        put(s1_ref, 0, top, 5)
        put(s1_ref, rows - 1, low, 5)

    @pl.when(parity("ha") == 0)
    def _():
        out(mc1, mc0)

    @pl.when(parity("ha") != 0)
    def _():
        out(mc0, mc1)


def prepare(w_ref, out_ref, wanted, k):
    chans = w_ref.shape[3]

    def clear():
        for n in range(len(wanted)):
            out_ref[n, k, :, chans:] = jnp.zeros((2, LANES - chans, 3 * LANES), BF16)

    def time_tap(i):
        blank = jnp.zeros((chans, LANES - chans), F32)
        f0, f1, f2 = (jnp.concatenate([w_ref[i, 2 - m, k], blank], 1) for m in range(3))
        even, odd = (f0 + f2) * (1 / 6), f1 * (1 / 6)
        far, odd2 = f0 * (1 / 24) + f2 * (1 / 6), f1 * (1 / 12)
        points = (f0 * 0.25, -even - odd, odd - even, far + odd2, far - odd2, f2)
        lanes = pl.ds((2 - i) * LANES, LANES)
        for n, p in enumerate(wanted):
            high = points[p].astype(BF16)
            out_ref[n, k, 0, 0:chans, lanes] = high
            out_ref[n, k, 1, 0:chans, lanes] = (points[p] - high.astype(F32)).astype(BF16)

    return [clear] + [functools.partial(time_tap, i) for i in range(3)]


def spread(steps, slots):
    return [steps[n * len(steps) // slots : (n + 1) * len(steps) // slots] for n in range(slots)]


POINTS = {2: (0, 1, 2, 5), 3: (0, 1, 2, 3, 5), 4: (0, 1, 2, 3, 4, 5)}


def transform(x, size):
    if size == 2:
        return 4.0 * (x[0] - x[2]), -3.0 * (x[1] + x[2]), 3.0 * (x[1] - x[2]), x[3] - x[1]
    if size == 3:
        a, b = x[3] - x[1], x[3] - 2.0 * x[1]
        return (
            4.0 * (x[0] - x[2]) + 2.0 * a,
            3.0 * (b - x[2]),
            2.0 * x[1] - 3.0 * x[2] + x[3],
            4.0 * a,
            x[4] - x[2] - 2.0 * a,
        )
    a, b = x[4] - 4.0 * x[2], x[3] - 4.0 * x[1]
    c, e = x[4] - x[2], 2.0 * (x[3] - x[1])
    return 4.0 * x[0] - 5.0 * x[2] + x[4], a + b, a - b, c + e, c - e, 4.0 * x[1] - 5.0 * x[3] + x[5]


def outputs(y, size):
    plus, minus = y[1] + y[2], y[1] - y[2]
    if size == 2:
        return y[0] + plus, minus + y[3]
    if size == 3:
        return y[0] + plus + y[3], minus + 2.0 * y[3], plus + 4.0 * y[3] + y[4]
    far, odd = y[3] + y[4], y[3] - y[4]
    return y[0] + plus + far, minus + 2.0 * odd, plus + 4.0 * far, minus + 8.0 * odd + y[5]


def right_operands(w_ref, p):
    zero = jnp.zeros((LANES, LANES), BF16)
    near, far = [], []
    for k in range(3):
        parts = [w_ref[p, k, part] for part in range(2)]
        own = [
            jnp.concatenate([r[:, : 2 * LANES], jnp.concatenate([zero, r[:, :LANES]], 1)], 0) for r in parts
        ]
        later = [
            jnp.concatenate([jnp.concatenate([r[:, 2 * LANES :], zero], 1), r[:, LANES:]], 0) for r in parts
        ]
        near.append(jnp.concatenate([own[0], own[0], own[1]], 1))
        far.append(jnp.concatenate([later[0], later[0], later[1]], 1))
    return jnp.concatenate(near, 0), jnp.concatenate(far, 0)


def product(left, right):
    left = jnp.concatenate([left, left[:, : 2 * LANES]], 1)
    return lax.dot_general(left, right, (((1,), (1,)), ((), ())), preferred_element_type=F32)


def shifted_sum(taps):
    two = 2 * LANES
    return roll(taps[:, :two], -1, 0) + taps[:, two : 2 * two] + roll(taps[:, 2 * two :], 1, 0)


def conv(read, size, width, s_ref, y_ref, w_ref, emit, done=None, beside=None):
    chunks = width // SUB
    points = len(POINTS[size])

    def one(c, carry):
        at = pl.ds(pl.multiple_of(c * SUB, SUB), SUB)
        for t in range(4):
            pair, a = t // 2, t % 2
            x = [read(t, r, at) for r in range(2 * size + 2)]
            for p, pieces in enumerate(zip(transform(x[: size + 2], size), transform(x[size:], size))):
                value = jnp.concatenate(pieces, 0)
                high = value.astype(BF16)
                s_ref[p, c, pair, :, a * LANES : (a + 1) * LANES] = high
                s_ref[p, c, pair, :, (2 + a) * LANES : (3 + a) * LANES] = (value - high.astype(F32)).astype(BF16)
        return carry

    lax.fori_loop(0, chunks, one, 0)
    wide = 4 * LANES

    def other_work(n):
        for step in beside[n] if beside else ():
            step()

    for p in range(points):
        near, far = right_operands(w_ref, p)
        own = product(s_ref[p].reshape(chunks * 4 * SUB, wide), near).reshape(chunks, 2, 2, SUB, 6 * LANES)
        other_work(2 * p)
        later = product(s_ref[p, :, 1].reshape(chunks * 2 * SUB, wide), far).reshape(chunks, 2, SUB, 6 * LANES)
        other_work(2 * p + 1)
        for n in range(2):
            y_ref[0, p, n] = shifted_sum((own[:, 0, n] + later[:, n]).reshape(width, 6 * LANES))
            y_ref[1, p, n] = shifted_sum(own[:, 1, n].reshape(width, 6 * LANES))

    for t in range(4):
        lanes = pl.ds(t % 2 * LANES, LANES)
        for tile in range(2):
            rows = outputs([y_ref[t // 2, p, tile, :, lanes] for p in range(points)], size)
            for o, value in enumerate(rows):
                emit(t, tile * size + o, value)
        if done is not None:
            done(t)


def halo_rows(chans, from_even, from_odd, r):
    return ungroup_frames([jnp.where(parity("ha") == 0, from_even[g, r], from_odd[g, r]) for g in range(3)], chans)


def third_kernel(chans, cp_ref, ra0, ra1, rc0, rc1, u3_ref, w2_ref, w1_ref, out_ref, u2_ref, u1_ref, x_ref, s_ref, y_ref):
    rows, width = cp_ref.shape[1:3]
    cols = width - SUB
    for r in range(3):
        for at, even, odd, ceven, codd in ((r, ra1, ra0, rc1, rc0), (r + 3, ra0, ra1, rc0, rc1)):
            for t, frame in enumerate(halo_rows(chans, even, odd, r)):
                x_ref[t, at, 0:cols] = frame
            for t, frame in enumerate(halo_rows(chans, ceven, codd, r)):
                x_ref[t, at, cols:] = frame

    def read(t, r, at):
        if 3 <= r < 3 + rows:
            return cp_ref[t, r - 3, at]
        return x_ref[t, r if r < 3 else r - rows, at]

    def emit(t, o, value):
        out_ref[t, o] = value

    steps = []
    for k in range(3):
        steps += prepare(w2_ref, u2_ref, POINTS[(rows + 2) // 2], k) + prepare(w1_ref, u1_ref, POINTS[rows // 2], k)
    beside = spread(steps, 2 * len(POINTS[rows]))
    conv(read, rows, width, s_ref, y_ref, u3_ref, emit, beside=beside)


def last_kernel(chans, g_ref, s2_ref, s1_ref, ra0, ra1, rb0, rb1, rc0, rc1, u2_ref, u1_ref, out_hbm,
                e_ref, x1_ref, s_ref, y_ref, stage_ref, sems):
    frames, rows, width, _ = s2_ref.shape
    cols = width - SUB
    for side, (even, odd) in enumerate(((1, 0), (0, 1))):
        for r in range(3):
            main, at = ((rb0, rb1), r) if r < 2 else ((ra0, ra1), 3)
            for t, frame in enumerate(halo_rows(chans, main[even], main[odd], at)):
                e_ref[side, r, t, 0:cols] = frame
            corners = (rc0, rc1)
            for t, frame in enumerate(halo_rows(chans, corners[even], corners[odd], 3 + r)):
                e_ref[side, r, t, cols:] = frame

    def slope2(t, r, at):
        if 2 <= r < 2 + rows:
            return s2_ref[t, r - 2, at]
        return e_ref[0, r, t, at] if r < 2 else e_ref[1, r - 2 - rows, t, at]

    def emit2(t, o, value):
        slope = s1_ref[t, o - 1] if 1 <= o < 1 + rows else e_ref[0 if o < 1 else 1, 2, t]
        x1_ref[t, o] = value * slope

    def emit1(t, o, value):
        stage_ref[t, o] = value[0:cols, 0:chans]

    def copy_out(t):
        return pltpu.make_async_copy(stage_ref.at[t], out_hbm.at[t], sems.at[t])

    size2, size1 = (rows + 2) // 2, rows // 2
    conv(lambda t, r, at: g_ref[t, r, at] * slope2(t, r, at), size2, width, s_ref, y_ref, u2_ref, emit2)
    conv(lambda t, r, at: x1_ref[t, r, at], size1, width, s_ref, y_ref, u1_ref, emit1, lambda t: copy_out(t).start())
    for t in range(frames):
        copy_out(t).wait()


def swap(value, axis, which):
    count = lax.axis_size(axis)
    pairs = []
    for low in range(1 - which, count - 1, 2):
        pairs += [(low, low + 1), (low + 1, low)]
    return lax.ppermute(value, axis, pairs)


def swaps(first, second, axis):
    got = []
    for which, value in enumerate((first, second)):
        got.append(swap(value, axis, which))
    return got


def call(body, out_shape, args, scratch=(), hbm=(), hbm_out=False, alias=None, vmem=40 << 20):
    out = HBM_SPEC if hbm_out else VMEM_SPEC
    return pl.pallas_call(
        body,
        out_shape=out_shape,
        in_specs=[HBM_SPEC if n in hbm else VMEM_SPEC for n in range(len(args))],
        out_specs=jax.tree.map(lambda _: out, out_shape),
        scratch_shapes=list(scratch),
        input_output_aliases=alias or {},
        compiler_params=pltpu.CompilerParams(vmem_limit_bytes=vmem),
    )(*args)


def program(cotangent, stored_first, stored_second, w_first, w_second, w_third):
    frames, rows, cols, chans = cotangent.shape
    width = cols + SUB

    def arr(*shape, dtype=F32):
        return jax.ShapeDtypeStruct(shape, dtype)

    def vmem(*shape, dtype=F32):
        return pltpu.VMEM(shape, dtype)

    edge = arr(frames, rows, SUB, LANES)
    own = arr(frames, rows, width, LANES)
    rows_a, rows_b = arr(3, 4, cols, LANES), arr(3, 2, cols, LANES)
    corner = arr(3, 6, SUB, LANES)
    *fields, third, second, first = (
        pltpu.with_memory_space_constraint(x, pltpu.HBM)
        for x in (cotangent, stored_second, stored_first, w_third, w_second, w_first)
    )
    raw = arr(frames, rows, cols, chans)
    ma0, ma1, wp0, wp1, cp, sec, fst = call(
        pack_kernel,
        (rows_a,) * 2 + (edge,) * 2 + (own, raw, raw),
        tuple(fields),
        [vmem(frames, rows, cols, chans), vmem(2, 2, frames, rows, SUB, LANES), vmem(frames, 2, cols, LANES), pltpu.SemaphoreType.DMA((3,))],
        hbm=(0, 1, 2),
    )
    ra0, ra1 = swaps(ma0, ma1, "ha")
    rw0, rw1 = swaps(wp0, wp1, "wa")

    def weights(size):
        return arr(len(POINTS[size]), 3, 2, LANES, 3 * LANES, dtype=BF16)

    size3, size2, size1 = rows, (rows + 2) // 2, rows // 2
    mb0, mb1, s2, s1, u3, second, first = call(
        functools.partial(slope_kernel, POINTS[size3]),
        (rows_b,) * 2 + (own,) * 2 + (weights(size3), arr(*second.shape), arr(*first.shape)),
        (sec, fst, third, second, first),
        [vmem(*third.shape), pltpu.SemaphoreType.DMA((3,))],
        hbm=(2, 3, 4),
    )
    mc0, mc1, cp, s2, s1, mb0, mb1 = call(
        functools.partial(corner_kernel, chans),
        (corner,) * 2 + (own,) * 3 + (rows_b,) * 2,
        (rw0, rw1, cp, s2, s1, mb0, mb1),
        alias={n + 2: n + 2 for n in range(5)},
    )
    rc0, rc1 = swaps(mc0, mc1, "ha")
    rb0, rb1 = swaps(mb0, mb1, "ha")

    def scratch(size):
        points = len(POINTS[size])
        return [
            vmem(points, width // SUB, 2, 2 * SUB, 4 * LANES, dtype=BF16),
            vmem(2, points, 2, width, 2 * LANES),
        ]

    grad, u2, u1 = call(
        functools.partial(third_kernel, chans),
        (arr(frames, rows + 4, width, LANES), weights(size2), weights(size1)),
        (cp, ra0, ra1, rc0, rc1, u3, second, first),
        [vmem(frames, 6, width, LANES)] + scratch(size3),
    )
    return call(
        functools.partial(last_kernel, chans),
        arr(frames, rows, cols, chans),
        (grad, s2, s1, ra0, ra1, rb0, rb1, rc0, rc1, u2, u1),
        [vmem(2, 3, frames, width, LANES), vmem(frames, rows + 2, width, LANES)]
        + scratch(size2)
        + [vmem(frames, rows, cols, chans), pltpu.SemaphoreType.DMA((frames,))],
        hbm_out=True,
    )


def solution(mesh):
    in_specs = (
        P("clip", "ha", "wa", None),
        P("clip", "ha", "wa", None),
        P("clip", "ha", "wa", None),
        P(),
        P(),
        P(),
    )
    out_specs = P("clip", "ha", "wa", None)
    return jax.shard_map(program, mesh=mesh, in_specs=in_specs, out_specs=out_specs, check_vma=False)
```

```python
import functools

import jax
import jax.numpy as jnp
from jax import lax
from jax.experimental import pallas as pl
from jax.experimental.pallas import tpu as pltpu
from jax.sharding import PartitionSpec as P


LANES = 128
SUB = 8
F32 = jnp.float32
BF16 = jnp.bfloat16
VMEM_SPEC = pl.BlockSpec(memory_space=pltpu.VMEM)
HBM_SPEC = pl.BlockSpec(memory_space=pltpu.HBM)


def parity(axis):
    return (lax.axis_index(axis) + 1) % 2


def silu_slope(value):
    sigma = 1.0 / (1.0 + jnp.exp(-value))
    return sigma * (1.0 + value * (1.0 - sigma))


def roll(value, shift, axis):
    return pltpu.roll(value, shift % value.shape[axis], axis)


def lane_of(shape):
    return lax.broadcasted_iota(jnp.int32, shape, len(shape) - 1)


def sub_of(shape):
    return lax.broadcasted_iota(jnp.int32, shape, len(shape) - 2)


def group_frames(frames, chans):
    first, second, third, fourth = frames
    part = LANES - chans
    lane = lane_of(first.shape)
    packed = []
    for index, frame in enumerate((first, second, third)):
        packed.append(jnp.where(lane < chans, frame, roll(fourth, chans - part * index, 1)))
    return packed


def ungroup_frames(groups, chans):
    part = LANES - chans
    lane = lane_of(groups[0].shape)
    frames = [jnp.where(lane < chans, group, 0.0) for group in groups]
    fourth = jnp.zeros_like(groups[0])
    for index in reversed(range(3)):
        moved = roll(groups[index], part * (index + 1), 1)
        fourth = jnp.where(lane < part * (index + 1), moved, fourth)
    return frames + [jnp.where(lane < chans, fourth, 0.0)]


def group_row(src, h, cols, chans):
    return group_frames([src[t, h, 0:cols] for t in range(4)], chans)


def pack_kernel(cot_hbm, sec_hbm, fst_hbm, ma0, ma1, wp0, wp1, cp_ref, sec_ref, fst_ref, raw_ref, edge_ref, row_ref, sems):
    frames, rows, cols, chans = cot_hbm.shape
    copies = [
        pltpu.make_async_copy(src, dst, sems.at[a])
        for a, (src, dst) in enumerate(((cot_hbm, raw_ref), (sec_hbm, sec_ref), (fst_hbm, fst_ref)))
    ]
    for copy in copies:
        copy.start()
    cp_ref[...] = jnp.zeros(cp_ref.shape, F32)
    edge_ref[...] = jnp.zeros(edge_ref.shape, F32)
    copies[0].wait()
    cp_ref[:, :, 0:cols, 0:chans] = raw_ref[...]

    row_ref[...] = jnp.zeros(row_ref.shape, F32)
    for copy in copies[1:]:
        copy.wait()
    for at, h in enumerate((0, rows - 1)):
        row_ref[:, at, :, 0:chans] = silu_slope(fst_ref[:, h])

    def rows_out(top, low):
        for r in range(3):
            for dst, h in ((top, r), (low, rows - 3 + r)):
                for g, val in enumerate(group_row(cp_ref, h, cols, chans)):
                    dst[g, r] = val
        for at, dst in enumerate((top, low)):
            for g, val in enumerate(group_row(row_ref, at, cols, chans)):
                dst[g, 3] = val

    @pl.when(parity("ha") == 0)
    def _():
        rows_out(ma1, ma0)

    @pl.when(parity("ha") != 0)
    def _():
        rows_out(ma0, ma1)

    for a, ref in ((0, sec_ref), (1, fst_ref)):
        for side, start in enumerate((0, cols - SUB)):
            edge_ref[a, side, :, :, :, 0:chans] = silu_slope(ref[:, :, start : start + SUB])

    def cols_out(left, right):
        sub = sub_of((SUB, LANES))
        for t in range(frames):
            for h in range(rows):
                c0, a0, b0 = cp_ref[t, h, 0:SUB], edge_ref[0, 0, t, h], edge_ref[1, 0, t, h]
                c7, a7, b7 = cp_ref[t, h, cols - SUB : cols], edge_ref[0, 1, t, h], edge_ref[1, 1, t, h]
                right[t, h] = jnp.where(
                    sub >= 5, c7, jnp.where((sub == 2) | (sub == 3), roll(a7, 4, 0), jnp.where(sub == 1, roll(b7, 2, 0), 0.0))
                )
                left[t, h] = jnp.where(
                    sub < 3, c0, jnp.where((sub == 4) | (sub == 5), roll(a0, 4, 0), jnp.where(sub == 6, roll(b0, 6, 0), 0.0))
                )

    @pl.when(parity("wa") == 0)
    def _():
        cols_out(wp1, wp0)

    @pl.when(parity("wa") != 0)
    def _():
        cols_out(wp0, wp1)


def slope_kernel(wanted, sec_ref, fst_ref, w3_hbm, w2_hbm, w1_hbm, mb0, mb1, s2_ref, s1_ref, u_ref, w2_ref, w1_ref, w_ref, sems):
    frames, rows, cols, chans = sec_ref.shape
    loads = [
        pltpu.make_async_copy(src, dst, sems.at[n])
        for n, (src, dst) in enumerate(((w3_hbm, w_ref), (w2_hbm, w2_ref), (w1_hbm, w1_ref)))
    ]
    for load in loads:
        load.start()
    blank = jnp.zeros((cols, LANES), F32)
    for src, ref in ((sec_ref, s2_ref), (fst_ref, s1_ref)):
        for t in range(frames):
            for h in range(rows):
                ref[t, h, 0:cols] = blank
                ref[t, h, 0:cols, 0:chans] = silu_slope(src[t, h])

    def rows_out(top, low):
        for src, h, dst, at in (
            (s2_ref, 0, top, 0),
            (s2_ref, 1, top, 1),
            (s2_ref, rows - 2, low, 0),
            (s2_ref, rows - 1, low, 1),
        ):
            for g, val in enumerate(group_row(src, h, cols, chans)):
                dst[g, at] = val

    @pl.when(parity("ha") == 0)
    def _():
        rows_out(mb1, mb0)

    @pl.when(parity("ha") != 0)
    def _():
        rows_out(mb0, mb1)

    loads[0].wait()
    for k in range(3):
        for step in prepare(w_ref, u_ref, wanted, k):
            step()
    for load in loads[1:]:
        load.wait()


def corner_kernel(chans, rw0, rw1, _c, _s2, _s1, _b0, _b1, mc0, mc1, cp_ref, s2_ref, s1_ref, _mb0, _mb1):
    frames, rows = rw0.shape[:2]
    cols = cp_ref.shape[2] - SUB
    even = parity("wa") == 0
    sub = sub_of((SUB, LANES))
    for t in range(frames):
        for h in range(rows):
            left = jnp.where(even, rw1[t, h], rw0[t, h])
            right = jnp.where(even, rw0[t, h], rw1[t, h])
            cp_ref[t, h, cols:] = jnp.where(sub < 3, right, jnp.where(sub >= 5, left, 0.0))
            s2_ref[t, h, cols:] = jnp.where(sub < 2, roll(right, 4, 0), jnp.where(sub >= 6, roll(left, 4, 0), 0.0))
            s1_ref[t, h, cols:] = jnp.where(sub == 0, roll(right, 2, 0), jnp.where(sub == 7, roll(left, 6, 0), 0.0))

    def out(top, low):
        def put(src, h, dst, at):
            for g, val in enumerate(group_frames([src[t, h, cols:] for t in range(frames)], chans)):
                dst[g, at] = val

        for r in range(3):
            put(cp_ref, r, top, r)
            put(cp_ref, rows - 3 + r, low, r)
        for r in range(2):
            put(s2_ref, r, top, 3 + r)
            put(s2_ref, rows - 2 + r, low, 3 + r)
        put(s1_ref, 0, top, 5)
        put(s1_ref, rows - 1, low, 5)

    @pl.when(parity("ha") == 0)
    def _():
        out(mc1, mc0)

    @pl.when(parity("ha") != 0)
    def _():
        out(mc0, mc1)


def prepare(w_ref, out_ref, wanted, k):
    chans = w_ref.shape[3]

    def clear():
        for n in range(len(wanted)):
            out_ref[n, k, :, chans:] = jnp.zeros((2, LANES - chans, 3 * LANES), BF16)

    def time_tap(i):
        blank = jnp.zeros((chans, LANES - chans), F32)
        f0, f1, f2 = (jnp.concatenate([w_ref[i, 2 - m, k], blank], 1) for m in range(3))
        even, odd = (f0 + f2) * (1 / 6), f1 * (1 / 6)
        far, odd2 = f0 * (1 / 24) + f2 * (1 / 6), f1 * (1 / 12)
        points = (f0 * 0.25, -even - odd, odd - even, far + odd2, far - odd2, f2)
        lanes = pl.ds((2 - i) * LANES, LANES)
        for n, p in enumerate(wanted):
            high = points[p].astype(BF16)
            out_ref[n, k, 0, 0:chans, lanes] = high
            out_ref[n, k, 1, 0:chans, lanes] = (points[p] - high.astype(F32)).astype(BF16)

    return [clear] + [functools.partial(time_tap, i) for i in range(3)]


def spread(steps, slots):
    return [steps[n * len(steps) // slots : (n + 1) * len(steps) // slots] for n in range(slots)]


POINTS = {2: (0, 1, 2, 5), 3: (0, 1, 2, 3, 5), 4: (0, 1, 2, 3, 4, 5)}


def transform(x, size, p):
    if size == 2:
        return (
            lambda: 4.0 * (x(0) - x(2)),
            lambda: -3.0 * (x(1) + x(2)),
            lambda: 3.0 * (x(1) - x(2)),
            lambda: x(3) - x(1),
        )[p]()
    if size == 3:
        return (
            lambda: 4.0 * (x(0) - x(2)) + 2.0 * (x(3) - x(1)),
            lambda: 3.0 * (x(3) - 2.0 * x(1) - x(2)),
            lambda: 2.0 * x(1) - 3.0 * x(2) + x(3),
            lambda: 4.0 * (x(3) - x(1)),
            lambda: x(4) - x(2) - 2.0 * (x(3) - x(1)),
        )[p]()
    return (
        lambda: 4.0 * x(0) - 5.0 * x(2) + x(4),
        lambda: x(4) - 4.0 * x(2) + (x(3) - 4.0 * x(1)),
        lambda: x(4) - 4.0 * x(2) - (x(3) - 4.0 * x(1)),
        lambda: x(4) - x(2) + 2.0 * (x(3) - x(1)),
        lambda: x(4) - x(2) - 2.0 * (x(3) - x(1)),
        lambda: 4.0 * x(1) - 5.0 * x(3) + x(5),
    )[p]()


def outputs(y, size):
    plus, minus = y[1] + y[2], y[1] - y[2]
    if size == 2:
        return y[0] + plus, minus + y[3]
    if size == 3:
        return y[0] + plus + y[3], minus + 2.0 * y[3], plus + 4.0 * y[3] + y[4]
    far, odd = y[3] + y[4], y[3] - y[4]
    return y[0] + plus + far, minus + 2.0 * odd, plus + 4.0 * far, minus + 8.0 * odd + y[5]


def right_operands(w_ref, p):
    zero = jnp.zeros((LANES, LANES), BF16)
    near, far = [], []
    for k in range(3):
        parts = [w_ref[p, k, part] for part in range(2)]
        own = [
            jnp.concatenate([r[:, : 2 * LANES], jnp.concatenate([zero, r[:, :LANES]], 1)], 0) for r in parts
        ]
        later = [
            jnp.concatenate([jnp.concatenate([r[:, 2 * LANES :], zero], 1), r[:, LANES:]], 0) for r in parts
        ]
        near.append(jnp.concatenate([own[0], own[0], own[1]], 1))
        far.append(jnp.concatenate([later[0], later[0], later[1]], 1))
    return jnp.concatenate(near, 0), jnp.concatenate(far, 0)


def product(left, right):
    left = jnp.concatenate([left, left[:, : 2 * LANES]], 1)
    return lax.dot_general(left, right, (((1,), (1,)), ((), ())), preferred_element_type=F32)


def shifted_sum(taps):
    two = 2 * LANES
    return roll(taps[:, :two], -1, 0) + taps[:, two : 2 * two] + roll(taps[:, 2 * two :], 1, 0)


def conv(read, size, width, s_ref, y_ref, w_ref, emit, done=None, beside=None):
    chunks = width // SUB
    points = len(POINTS[size])

    def fill(p, at, blocks):
        for t in range(4):
            pair, a = t // 2, t % 2
            tiles = []
            for base in (0, size):
                value = transform(lambda r: read(t, base + r, at), size, p)
                tiles.append(value.reshape(-1, 1, SUB, LANES))
            value = jnp.concatenate(tiles, 1).reshape(-1, 2 * SUB, LANES)
            high = value.astype(BF16)
            s_ref[p, blocks, pair, :, a * LANES : (a + 1) * LANES] = high
            s_ref[p, blocks, pair, :, (2 + a) * LANES : (3 + a) * LANES] = (value - high.astype(F32)).astype(BF16)

    def first(c, carry):
        fill(0, pl.ds(pl.multiple_of(c * SUB, SUB), SUB), pl.ds(c, 1))
        return carry

    lax.fori_loop(0, chunks, first, 0)

    wide = 4 * LANES

    def other_work(n):
        for step in beside[n] if beside else ():
            step()

    for p in range(points):
        near, far = right_operands(w_ref, p)
        own = product(s_ref[p].reshape(chunks * 4 * SUB, wide), near).reshape(chunks, 2, 2, SUB, 6 * LANES)
        if p + 1 < points:
            fill(p + 1, slice(0, width), slice(0, chunks))
        other_work(2 * p)
        later = product(s_ref[p, :, 1].reshape(chunks * 2 * SUB, wide), far).reshape(chunks, 2, SUB, 6 * LANES)
        other_work(2 * p + 1)
        for n in range(2):
            y_ref[0, p, n] = shifted_sum((own[:, 0, n] + later[:, n]).reshape(width, 6 * LANES))
            y_ref[1, p, n] = shifted_sum(own[:, 1, n].reshape(width, 6 * LANES))

    for t in range(4):
        lanes = pl.ds(t % 2 * LANES, LANES)
        for tile in range(2):
            rows = outputs([y_ref[t // 2, p, tile, :, lanes] for p in range(points)], size)
            for o, value in enumerate(rows):
                emit(t, tile * size + o, value)
        if done is not None:
            done(t)


def halo_rows(chans, from_even, from_odd, r):
    return ungroup_frames([jnp.where(parity("ha") == 0, from_even[g, r], from_odd[g, r]) for g in range(3)], chans)


def third_kernel(chans, cp_ref, s2_ref, ra0, ra1, rc0, rc1, u3_ref, w2_ref, w1_ref, out_ref, u2_ref, u1_ref, x_ref, s_ref, y_ref):
    rows, width = cp_ref.shape[1:3]
    cols = width - SUB
    for r in range(3):
        for at, even, odd, ceven, codd in ((r, ra1, ra0, rc1, rc0), (r + 3, ra0, ra1, rc0, rc1)):
            for t, frame in enumerate(halo_rows(chans, even, odd, r)):
                x_ref[t, at, 0:cols] = frame
            for t, frame in enumerate(halo_rows(chans, ceven, codd, r)):
                x_ref[t, at, cols:] = frame

    def read(t, r, at):
        if 3 <= r < 3 + rows:
            return cp_ref[t, r - 3, at]
        return x_ref[t, r if r < 3 else r - rows, at]

    def emit(t, o, value):
        out_ref[t, o] = value * s2_ref[t, o - 2] if 2 <= o < 2 + rows else value

    steps = []
    for k in range(3):
        steps += prepare(w2_ref, u2_ref, POINTS[(rows + 2) // 2], k) + prepare(w1_ref, u1_ref, POINTS[rows // 2], k)
    beside = spread(steps, 2 * len(POINTS[rows]))
    conv(read, rows, width, s_ref, y_ref, u3_ref, emit, beside=beside)


def last_kernel(chans, g_ref, s1_ref, ra0, ra1, rb0, rb1, rc0, rc1, u2_ref, u1_ref, out_hbm,
                e_ref, x1_ref, s_ref, y_ref, stage_ref, sems):
    frames, rows, width, _ = s1_ref.shape
    cols = width - SUB
    for side, (even, odd) in enumerate(((1, 0), (0, 1))):
        for r in range(3):
            main, at = ((rb0, rb1), r) if r < 2 else ((ra0, ra1), 3)
            for t, frame in enumerate(halo_rows(chans, main[even], main[odd], at)):
                e_ref[side, r, t, 0:cols] = frame
            corners = (rc0, rc1)
            for t, frame in enumerate(halo_rows(chans, corners[even], corners[odd], 3 + r)):
                e_ref[side, r, t, cols:] = frame

        for t in range(frames):
            for r in range(2):
                e_ref[side, r, t] = e_ref[side, r, t] * g_ref[t, r + side * (rows + 2)]

    def read2(t, r, at):
        if 2 <= r < 2 + rows:
            return g_ref[t, r, at]
        return e_ref[0, r, t, at] if r < 2 else e_ref[1, r - 2 - rows, t, at]

    def emit2(t, o, value):
        slope = s1_ref[t, o - 1] if 1 <= o < 1 + rows else e_ref[0 if o < 1 else 1, 2, t]
        x1_ref[t, o] = value * slope

    def emit1(t, o, value):
        stage_ref[t, o] = value[0:cols, 0:chans]

    def copy_out(t):
        return pltpu.make_async_copy(stage_ref.at[t], out_hbm.at[t], sems.at[t])

    size2, size1 = (rows + 2) // 2, rows // 2
    conv(read2, size2, width, s_ref, y_ref, u2_ref, emit2)
    conv(lambda t, r, at: x1_ref[t, r, at], size1, width, s_ref, y_ref, u1_ref, emit1, lambda t: copy_out(t).start())
    for t in range(frames):
        copy_out(t).wait()


def swap(value, axis, which):
    count = lax.axis_size(axis)
    pairs = []
    for low in range(1 - which, count - 1, 2):
        pairs += [(low, low + 1), (low + 1, low)]
    return lax.ppermute(value, axis, pairs)


def swaps(first, second, axis):
    got = []
    for which, value in enumerate((first, second)):
        got.append(swap(value, axis, which))
    return got


def call(body, out_shape, args, scratch=(), hbm=(), hbm_out=False, alias=None, vmem=40 << 20):
    out = HBM_SPEC if hbm_out else VMEM_SPEC
    return pl.pallas_call(
        body,
        out_shape=out_shape,
        in_specs=[HBM_SPEC if n in hbm else VMEM_SPEC for n in range(len(args))],
        out_specs=jax.tree.map(lambda _: out, out_shape),
        scratch_shapes=list(scratch),
        input_output_aliases=alias or {},
        compiler_params=pltpu.CompilerParams(vmem_limit_bytes=vmem),
    )(*args)


def program(cotangent, stored_first, stored_second, w_first, w_second, w_third):
    frames, rows, cols, chans = cotangent.shape
    width = cols + SUB

    def arr(*shape, dtype=F32):
        return jax.ShapeDtypeStruct(shape, dtype)

    def vmem(*shape, dtype=F32):
        return pltpu.VMEM(shape, dtype)

    edge = arr(frames, rows, SUB, LANES)
    own = arr(frames, rows, width, LANES)
    rows_a, rows_b = arr(3, 4, cols, LANES), arr(3, 2, cols, LANES)
    corner = arr(3, 6, SUB, LANES)
    *fields, third, second, first = (
        pltpu.with_memory_space_constraint(x, pltpu.HBM)
        for x in (cotangent, stored_second, stored_first, w_third, w_second, w_first)
    )
    raw = arr(frames, rows, cols, chans)
    ma0, ma1, wp0, wp1, cp, sec, fst = call(
        pack_kernel,
        (rows_a,) * 2 + (edge,) * 2 + (own, raw, raw),
        tuple(fields),
        [vmem(frames, rows, cols, chans), vmem(2, 2, frames, rows, SUB, LANES), vmem(frames, 2, cols, LANES), pltpu.SemaphoreType.DMA((3,))],
        hbm=(0, 1, 2),
    )
    ra0, ra1 = swaps(ma0, ma1, "ha")
    rw0, rw1 = swaps(wp0, wp1, "wa")

    def weights(size):
        return arr(len(POINTS[size]), 3, 2, LANES, 3 * LANES, dtype=BF16)

    size3, size2, size1 = rows, (rows + 2) // 2, rows // 2
    mb0, mb1, s2, s1, u3, second, first = call(
        functools.partial(slope_kernel, POINTS[size3]),
        (rows_b,) * 2 + (own,) * 2 + (weights(size3), arr(*second.shape), arr(*first.shape)),
        (sec, fst, third, second, first),
        [vmem(*third.shape), pltpu.SemaphoreType.DMA((3,))],
        hbm=(2, 3, 4),
    )
    mc0, mc1, cp, s2, s1, mb0, mb1 = call(
        functools.partial(corner_kernel, chans),
        (corner,) * 2 + (own,) * 3 + (rows_b,) * 2,
        (rw0, rw1, cp, s2, s1, mb0, mb1),
        alias={n + 2: n + 2 for n in range(5)},
    )
    rc0, rc1 = swaps(mc0, mc1, "ha")
    rb0, rb1 = swaps(mb0, mb1, "ha")

    def scratch(size):
        points = len(POINTS[size])
        return [
            vmem(points, width // SUB, 2, 2 * SUB, 4 * LANES, dtype=BF16),
            vmem(2, points, 2, width, 2 * LANES),
        ]

    grad, u2, u1 = call(
        functools.partial(third_kernel, chans),
        (arr(frames, rows + 4, width, LANES), weights(size2), weights(size1)),
        (cp, s2, ra0, ra1, rc0, rc1, u3, second, first),
        [vmem(frames, 6, width, LANES)] + scratch(size3),
    )
    return call(
        functools.partial(last_kernel, chans),
        arr(frames, rows, cols, chans),
        (grad, s1, ra0, ra1, rb0, rb1, rc0, rc1, u2, u1),
        [vmem(2, 3, frames, width, LANES), vmem(frames, rows + 2, width, LANES)]
        + scratch(size2)
        + [vmem(frames, rows, cols, chans), pltpu.SemaphoreType.DMA((frames,))],
        hbm_out=True,
    )


def solution(mesh):
    in_specs = (
        P("clip", "ha", "wa", None),
        P("clip", "ha", "wa", None),
        P("clip", "ha", "wa", None),
        P(),
        P(),
        P(),
    )
    out_specs = P("clip", "ha", "wa", None)
    return jax.shard_map(program, mesh=mesh, in_specs=in_specs, out_specs=out_specs, check_vma=False)
```

```python
import functools

import jax
import jax.numpy as jnp
from jax import lax
from jax.experimental import pallas as pl
from jax.experimental.pallas import tpu as pltpu
from jax.sharding import PartitionSpec as P


LANES = 128
SUB = 8
F32 = jnp.float32
BF16 = jnp.bfloat16
VMEM_SPEC = pl.BlockSpec(memory_space=pltpu.VMEM)
HBM_SPEC = pl.BlockSpec(memory_space=pltpu.HBM)


def parity(axis):
    return (lax.axis_index(axis) + 1) % 2


def silu_slope(value):
    sigma = 1.0 / (1.0 + jnp.exp(-value))
    return sigma * (1.0 + value * (1.0 - sigma))


def roll(value, shift, axis):
    return pltpu.roll(value, shift % value.shape[axis], axis)


def lane_of(shape):
    return lax.broadcasted_iota(jnp.int32, shape, len(shape) - 1)


def sub_of(shape):
    return lax.broadcasted_iota(jnp.int32, shape, len(shape) - 2)


def group_frames(frames, chans):
    first, second, third, fourth = frames
    part = LANES - chans
    lane = lane_of(first.shape)
    packed = []
    for index, frame in enumerate((first, second, third)):
        packed.append(jnp.where(lane < chans, frame, roll(fourth, chans - part * index, 1)))
    return packed


def ungroup_frames(groups, chans):
    part = LANES - chans
    lane = lane_of(groups[0].shape)
    frames = [jnp.where(lane < chans, group, 0.0) for group in groups]
    fourth = jnp.zeros_like(groups[0])
    for index in reversed(range(3)):
        moved = roll(groups[index], part * (index + 1), 1)
        fourth = jnp.where(lane < part * (index + 1), moved, fourth)
    return frames + [jnp.where(lane < chans, fourth, 0.0)]


def group_row(src, h, cols, chans):
    return group_frames([src[t, h, 0:cols] for t in range(4)], chans)


def pack_kernel(cot_hbm, sec_hbm, fst_hbm, ma0, ma1, wp0, wp1, cp_ref, sec_ref, fst_ref, raw_ref, edge_ref, row_ref, sems):
    frames, rows, cols, chans = cot_hbm.shape
    copies = [
        pltpu.make_async_copy(src, dst, sems.at[a])
        for a, (src, dst) in enumerate(((cot_hbm, raw_ref), (sec_hbm, sec_ref), (fst_hbm, fst_ref)))
    ]
    for copy in copies:
        copy.start()
    cp_ref[...] = jnp.zeros(cp_ref.shape, F32)
    edge_ref[...] = jnp.zeros(edge_ref.shape, F32)
    copies[0].wait()
    cp_ref[:, :, 0:cols, 0:chans] = raw_ref[...]

    row_ref[...] = jnp.zeros(row_ref.shape, F32)
    for copy in copies[1:]:
        copy.wait()
    for at, h in enumerate((0, rows - 1)):
        row_ref[:, at, :, 0:chans] = silu_slope(fst_ref[:, h])

    def rows_out(top, low):
        for r in range(3):
            for dst, h in ((top, r), (low, rows - 3 + r)):
                for g, val in enumerate(group_row(cp_ref, h, cols, chans)):
                    dst[g, r] = val
        for at, dst in enumerate((top, low)):
            for g, val in enumerate(group_row(row_ref, at, cols, chans)):
                dst[g, 3] = val

    @pl.when(parity("ha") == 0)
    def _():
        rows_out(ma1, ma0)

    @pl.when(parity("ha") != 0)
    def _():
        rows_out(ma0, ma1)

    for a, ref in ((0, sec_ref), (1, fst_ref)):
        for side, start in enumerate((0, cols - SUB)):
            edge_ref[a, side, :, :, :, 0:chans] = silu_slope(ref[:, :, start : start + SUB])

    def cols_out(left, right):
        sub = sub_of((SUB, LANES))
        for t in range(frames):
            for h in range(rows):
                c0, a0, b0 = cp_ref[t, h, 0:SUB], edge_ref[0, 0, t, h], edge_ref[1, 0, t, h]
                c7, a7, b7 = cp_ref[t, h, cols - SUB : cols], edge_ref[0, 1, t, h], edge_ref[1, 1, t, h]
                right[t, h] = jnp.where(
                    sub >= 5, c7, jnp.where((sub == 2) | (sub == 3), roll(a7, 4, 0), jnp.where(sub == 1, roll(b7, 2, 0), 0.0))
                )
                left[t, h] = jnp.where(
                    sub < 3, c0, jnp.where((sub == 4) | (sub == 5), roll(a0, 4, 0), jnp.where(sub == 6, roll(b0, 6, 0), 0.0))
                )

    @pl.when(parity("wa") == 0)
    def _():
        cols_out(wp1, wp0)

    @pl.when(parity("wa") != 0)
    def _():
        cols_out(wp0, wp1)


def slope_kernel(wanted, sec_ref, fst_ref, w3_hbm, w2_hbm, w1_hbm, mb0, mb1, s2_ref, s1_ref, u_ref, w2_ref, w1_ref, w_ref, sems):
    frames, rows, cols, chans = sec_ref.shape
    loads = [
        pltpu.make_async_copy(src, dst, sems.at[n])
        for n, (src, dst) in enumerate(((w3_hbm, w_ref), (w2_hbm, w2_ref), (w1_hbm, w1_ref)))
    ]
    for load in loads:
        load.start()
    blank = jnp.zeros((cols, LANES), F32)
    for src, ref in ((sec_ref, s2_ref), (fst_ref, s1_ref)):
        for t in range(frames):
            for h in range(rows):
                ref[t, h, 0:cols] = blank
                ref[t, h, 0:cols, 0:chans] = silu_slope(src[t, h])

    def rows_out(top, low):
        for src, h, dst, at in (
            (s2_ref, 0, top, 0),
            (s2_ref, 1, top, 1),
            (s2_ref, rows - 2, low, 0),
            (s2_ref, rows - 1, low, 1),
        ):
            for g, val in enumerate(group_row(src, h, cols, chans)):
                dst[g, at] = val

    @pl.when(parity("ha") == 0)
    def _():
        rows_out(mb1, mb0)

    @pl.when(parity("ha") != 0)
    def _():
        rows_out(mb0, mb1)

    loads[0].wait()
    for k in range(3):
        for step in prepare(w_ref, u_ref, wanted, k):
            step()
    for load in loads[1:]:
        load.wait()


def corner_kernel(chans, rw0, rw1, _c, _s2, _s1, _b0, _b1, mc0, mc1, cp_ref, s2_ref, s1_ref, _mb0, _mb1):
    frames, rows = rw0.shape[:2]
    cols = cp_ref.shape[2] - SUB
    even = parity("wa") == 0
    sub = sub_of((SUB, LANES))
    for t in range(frames):
        for h in range(rows):
            left = jnp.where(even, rw1[t, h], rw0[t, h])
            right = jnp.where(even, rw0[t, h], rw1[t, h])
            cp_ref[t, h, cols:] = jnp.where(sub < 3, right, jnp.where(sub >= 5, left, 0.0))
            s2_ref[t, h, cols:] = jnp.where(sub < 2, roll(right, 4, 0), jnp.where(sub >= 6, roll(left, 4, 0), 0.0))
            s1_ref[t, h, cols:] = jnp.where(sub == 0, roll(right, 2, 0), jnp.where(sub == 7, roll(left, 6, 0), 0.0))

    def out(top, low):
        def put(src, h, dst, at):
            for g, val in enumerate(group_frames([src[t, h, cols:] for t in range(frames)], chans)):
                dst[g, at] = val

        for r in range(3):
            put(cp_ref, r, top, r)
            put(cp_ref, rows - 3 + r, low, r)
        for r in range(2):
            put(s2_ref, r, top, 3 + r)
            put(s2_ref, rows - 2 + r, low, 3 + r)
        put(s1_ref, 0, top, 5)
        put(s1_ref, rows - 1, low, 5)

    @pl.when(parity("ha") == 0)
    def _():
        out(mc1, mc0)

    @pl.when(parity("ha") != 0)
    def _():
        out(mc0, mc1)


def prepare(w_ref, out_ref, wanted, k):
    chans = w_ref.shape[3]

    def clear():
        for n in range(len(wanted)):
            out_ref[n, k, :, chans:] = jnp.zeros((2, LANES - chans, 3 * LANES), BF16)

    def time_tap(i):
        blank = jnp.zeros((chans, LANES - chans), F32)
        f0, f1, f2 = (jnp.concatenate([w_ref[i, 2 - m, k], blank], 1) for m in range(3))
        even, odd = (f0 + f2) * (1 / 6), f1 * (1 / 6)
        far, odd2 = f0 * (1 / 24) + f2 * (1 / 6), f1 * (1 / 12)
        points = (f0 * 0.25, -even - odd, odd - even, far + odd2, far - odd2, f2)
        lanes = pl.ds((2 - i) * LANES, LANES)
        for n, p in enumerate(wanted):
            high = points[p].astype(BF16)
            out_ref[n, k, 0, 0:chans, lanes] = high
            out_ref[n, k, 1, 0:chans, lanes] = (points[p] - high.astype(F32)).astype(BF16)

    return [clear] + [functools.partial(time_tap, i) for i in range(3)]


def spread(steps, slots):
    return [steps[n * len(steps) // slots : (n + 1) * len(steps) // slots] for n in range(slots)]


POINTS = {2: (0, 1, 2, 5), 3: (0, 1, 2, 3, 5), 4: (0, 1, 2, 3, 4, 5)}


def transform(x, size, p):
    if size == 2:
        return (
            lambda: 4.0 * (x(0) - x(2)),
            lambda: -3.0 * (x(1) + x(2)),
            lambda: 3.0 * (x(1) - x(2)),
            lambda: x(3) - x(1),
        )[p]()
    if size == 3:
        return (
            lambda: 4.0 * (x(0) - x(2)) + 2.0 * (x(3) - x(1)),
            lambda: 3.0 * (x(3) - 2.0 * x(1) - x(2)),
            lambda: 2.0 * x(1) - 3.0 * x(2) + x(3),
            lambda: 4.0 * (x(3) - x(1)),
            lambda: x(4) - x(2) - 2.0 * (x(3) - x(1)),
        )[p]()
    return (
        lambda: 4.0 * x(0) - 5.0 * x(2) + x(4),
        lambda: x(4) - 4.0 * x(2) + (x(3) - 4.0 * x(1)),
        lambda: x(4) - 4.0 * x(2) - (x(3) - 4.0 * x(1)),
        lambda: x(4) - x(2) + 2.0 * (x(3) - x(1)),
        lambda: x(4) - x(2) - 2.0 * (x(3) - x(1)),
        lambda: 4.0 * x(1) - 5.0 * x(3) + x(5),
    )[p]()


def outputs(y, size):
    plus, minus = y[1] + y[2], y[1] - y[2]
    if size == 2:
        return y[0] + plus, minus + y[3]
    if size == 3:
        return y[0] + plus + y[3], minus + 2.0 * y[3], plus + 4.0 * y[3] + y[4]
    far, odd = y[3] + y[4], y[3] - y[4]
    return y[0] + plus + far, minus + 2.0 * odd, plus + 4.0 * far, minus + 8.0 * odd + y[5]


def right_operands(w_ref, p):
    zero = jnp.zeros((LANES, LANES), BF16)
    near, far = [], []
    for k in range(3):
        parts = [w_ref[p, k, part] for part in range(2)]
        own = [
            jnp.concatenate([r[:, : 2 * LANES], jnp.concatenate([zero, r[:, :LANES]], 1)], 0) for r in parts
        ]
        later = [
            jnp.concatenate([jnp.concatenate([r[:, 2 * LANES :], zero], 1), r[:, LANES:]], 0) for r in parts
        ]
        near.append(jnp.concatenate([own[0], own[0], own[1]], 1))
        far.append(jnp.concatenate([later[0], later[0], later[1]], 1))
    return jnp.concatenate(near, 0), jnp.concatenate(far, 0)


def product(left, right):
    left = jnp.concatenate([left, left[:, : 2 * LANES]], 1)
    return lax.dot_general(left, right, (((1,), (1,)), ((), ())), preferred_element_type=F32)


def shifted_sum(taps):
    two = 2 * LANES
    return roll(taps[:, :two], -1, 0) + taps[:, two : 2 * two] + roll(taps[:, 2 * two :], 1, 0)


def conv(read, size, width, s_ref, y_ref, w_ref, emit, done=None, beside=None, ahead=False):
    chunks = width // SUB
    points = len(POINTS[size])

    def fill(p, at, blocks):
        for t in range(4):
            pair, a = t // 2, t % 2
            tiles = []
            for base in (0, size):
                value = transform(lambda r: read(t, base + r, at), size, p)
                tiles.append(value.reshape(-1, 1, SUB, LANES))
            value = jnp.concatenate(tiles, 1).reshape(-1, 2 * SUB, LANES)
            high = value.astype(BF16)
            s_ref[p, blocks, pair, :, a * LANES : (a + 1) * LANES] = high
            s_ref[p, blocks, pair, :, (2 + a) * LANES : (3 + a) * LANES] = (value - high.astype(F32)).astype(BF16)

    def first(c, carry):
        for p in range(points if ahead else 1):
            fill(p, pl.ds(pl.multiple_of(c * SUB, SUB), SUB), pl.ds(c, 1))
        return carry

    lax.fori_loop(0, chunks, first, 0)

    wide = 4 * LANES

    def other_work(n):
        for step in beside[n] if beside else ():
            step()

    for p in range(points):
        near, far = right_operands(w_ref, p)
        own = product(s_ref[p].reshape(chunks * 4 * SUB, wide), near).reshape(chunks, 2, 2, SUB, 6 * LANES)
        if p + 1 < points and not ahead:
            fill(p + 1, slice(0, width), slice(0, chunks))
        other_work(2 * p)
        later = product(s_ref[p, :, 1].reshape(chunks * 2 * SUB, wide), far).reshape(chunks, 2, SUB, 6 * LANES)
        other_work(2 * p + 1)
        for n in range(2):
            y_ref[0, p, n] = shifted_sum((own[:, 0, n] + later[:, n]).reshape(width, 6 * LANES))
            y_ref[1, p, n] = shifted_sum(own[:, 1, n].reshape(width, 6 * LANES))

    for t in range(4):
        lanes = pl.ds(t % 2 * LANES, LANES)
        for tile in range(2):
            rows = outputs([y_ref[t // 2, p, tile, :, lanes] for p in range(points)], size)
            for o, value in enumerate(rows):
                emit(t, tile * size + o, value)
        if done is not None:
            done(t)


def halo_rows(chans, from_even, from_odd, r):
    return ungroup_frames([jnp.where(parity("ha") == 0, from_even[g, r], from_odd[g, r]) for g in range(3)], chans)


def third_kernel(chans, cp_ref, ra0, ra1, rc0, rc1, u3_ref, w2_ref, w1_ref, out_ref, u2_ref, u1_ref, x_ref, s_ref, y_ref):
    rows, width = cp_ref.shape[1:3]
    cols = width - SUB
    for r in range(3):
        for at, even, odd, ceven, codd in ((r, ra1, ra0, rc1, rc0), (r + 3, ra0, ra1, rc0, rc1)):
            for t, frame in enumerate(halo_rows(chans, even, odd, r)):
                x_ref[t, at, 0:cols] = frame
            for t, frame in enumerate(halo_rows(chans, ceven, codd, r)):
                x_ref[t, at, cols:] = frame

    def read(t, r, at):
        if 3 <= r < 3 + rows:
            return cp_ref[t, r - 3, at]
        return x_ref[t, r if r < 3 else r - rows, at]

    def emit(t, o, value):
        out_ref[t, o] = value

    steps = []
    for k in range(3):
        steps += prepare(w2_ref, u2_ref, POINTS[(rows + 2) // 2], k) + prepare(w1_ref, u1_ref, POINTS[rows // 2], k)
    beside = spread(steps, 2 * len(POINTS[rows]))
    conv(read, rows, width, s_ref, y_ref, u3_ref, emit, beside=beside, ahead=True)


def last_kernel(chans, g_ref, s2_ref, s1_ref, ra0, ra1, rb0, rb1, rc0, rc1, u2_ref, u1_ref, out_hbm,
                e_ref, x2_ref, x1_ref, s_ref, y_ref, stage_ref, sems):
    frames, rows, width, _ = s1_ref.shape
    cols = width - SUB
    for side, (even, odd) in enumerate(((1, 0), (0, 1))):
        for r in range(3):
            main, at = ((rb0, rb1), r) if r < 2 else ((ra0, ra1), 3)
            for t, frame in enumerate(halo_rows(chans, main[even], main[odd], at)):
                e_ref[side, r, t, 0:cols] = frame
            corners = (rc0, rc1)
            for t, frame in enumerate(halo_rows(chans, corners[even], corners[odd], 3 + r)):
                e_ref[side, r, t, cols:] = frame

        for t in range(frames):
            for r in range(2):
                at = r + side * (rows + 2)
                x2_ref[t, at] = e_ref[side, r, t] * g_ref[t, at]
    x2_ref[:, 2 : 2 + rows] = s2_ref[...] * g_ref[:, 2 : 2 + rows]

    def emit2(t, o, value):
        slope = s1_ref[t, o - 1] if 1 <= o < 1 + rows else e_ref[0 if o < 1 else 1, 2, t]
        x1_ref[t, o] = value * slope

    def emit1(t, o, value):
        stage_ref[t, o] = value[0:cols, 0:chans]

    def copy_out(t):
        return pltpu.make_async_copy(stage_ref.at[t], out_hbm.at[t], sems.at[t])

    size2, size1 = (rows + 2) // 2, rows // 2
    conv(lambda t, r, at: x2_ref[t, r, at], size2, width, s_ref, y_ref, u2_ref, emit2)
    conv(lambda t, r, at: x1_ref[t, r, at], size1, width, s_ref, y_ref, u1_ref, emit1, lambda t: copy_out(t).start())
    for t in range(frames):
        copy_out(t).wait()


def swap(value, axis, which):
    count = lax.axis_size(axis)
    pairs = []
    for low in range(1 - which, count - 1, 2):
        pairs += [(low, low + 1), (low + 1, low)]
    return lax.ppermute(value, axis, pairs)


def swaps(first, second, axis):
    got = []
    for which, value in enumerate((first, second)):
        got.append(swap(value, axis, which))
    return got


def call(body, out_shape, args, scratch=(), hbm=(), hbm_out=False, alias=None, vmem=24 << 20):
    out = HBM_SPEC if hbm_out else VMEM_SPEC
    return pl.pallas_call(
        body,
        out_shape=out_shape,
        in_specs=[HBM_SPEC if n in hbm else VMEM_SPEC for n in range(len(args))],
        out_specs=jax.tree.map(lambda _: out, out_shape),
        scratch_shapes=list(scratch),
        input_output_aliases=alias or {},
        compiler_params=pltpu.CompilerParams(vmem_limit_bytes=vmem),
    )(*args)


def program(cotangent, stored_first, stored_second, w_first, w_second, w_third):
    frames, rows, cols, chans = cotangent.shape
    width = cols + SUB

    def arr(*shape, dtype=F32):
        return jax.ShapeDtypeStruct(shape, dtype)

    def vmem(*shape, dtype=F32):
        return pltpu.VMEM(shape, dtype)

    edge = arr(frames, rows, SUB, LANES)
    own = arr(frames, rows, width, LANES)
    rows_a, rows_b = arr(3, 4, cols, LANES), arr(3, 2, cols, LANES)
    corner = arr(3, 6, SUB, LANES)
    *fields, third, second, first = (
        pltpu.with_memory_space_constraint(x, pltpu.HBM)
        for x in (cotangent, stored_second, stored_first, w_third, w_second, w_first)
    )
    raw = arr(frames, rows, cols, chans)
    ma0, ma1, wp0, wp1, cp, sec, fst = call(
        pack_kernel,
        (rows_a,) * 2 + (edge,) * 2 + (own, raw, raw),
        tuple(fields),
        [vmem(frames, rows, cols, chans), vmem(2, 2, frames, rows, SUB, LANES), vmem(frames, 2, cols, LANES), pltpu.SemaphoreType.DMA((3,))],
        hbm=(0, 1, 2),
    )
    ra0, ra1 = swaps(ma0, ma1, "ha")
    rw0, rw1 = swaps(wp0, wp1, "wa")

    def weights(size):
        return arr(len(POINTS[size]), 3, 2, LANES, 3 * LANES, dtype=BF16)

    size3, size2, size1 = rows, (rows + 2) // 2, rows // 2
    mb0, mb1, s2, s1, u3, second, first = call(
        functools.partial(slope_kernel, POINTS[size3]),
        (rows_b,) * 2 + (own,) * 2 + (weights(size3), arr(*second.shape), arr(*first.shape)),
        (sec, fst, third, second, first),
        [vmem(*third.shape), pltpu.SemaphoreType.DMA((3,))],
        hbm=(2, 3, 4),
    )
    mc0, mc1, cp, s2, s1, mb0, mb1 = call(
        functools.partial(corner_kernel, chans),
        (corner,) * 2 + (own,) * 3 + (rows_b,) * 2,
        (rw0, rw1, cp, s2, s1, mb0, mb1),
        alias={n + 2: n + 2 for n in range(5)},
    )
    rc0, rc1 = swaps(mc0, mc1, "ha")
    rb0, rb1 = swaps(mb0, mb1, "ha")

    def scratch(size):
        points = len(POINTS[size])
        return [
            vmem(points, width // SUB, 2, 2 * SUB, 4 * LANES, dtype=BF16),
            vmem(2, points, 2, width, 2 * LANES),
        ]

    grad, u2, u1 = call(
        functools.partial(third_kernel, chans),
        (arr(frames, rows + 4, width, LANES), weights(size2), weights(size1)),
        (cp, ra0, ra1, rc0, rc1, u3, second, first),
        [vmem(frames, 6, width, LANES)] + scratch(size3),
    )
    return call(
        functools.partial(last_kernel, chans),
        arr(frames, rows, cols, chans),
        (grad, s2, s1, ra0, ra1, rb0, rb1, rc0, rc1, u2, u1),
        [
            vmem(2, 3, frames, width, LANES),
            vmem(frames, rows + 4, width, LANES),
            vmem(frames, rows + 2, width, LANES),
        ]
        + scratch(size2)
        + [vmem(frames, rows, cols, chans), pltpu.SemaphoreType.DMA((frames,))],
        hbm_out=True,
    )


def solution(mesh):
    in_specs = (
        P("clip", "ha", "wa", None),
        P("clip", "ha", "wa", None),
        P("clip", "ha", "wa", None),
        P(),
        P(),
        P(),
    )
    out_specs = P("clip", "ha", "wa", None)
    return jax.shard_map(program, mesh=mesh, in_specs=in_specs, out_specs=out_specs, check_vma=False)
```

```python
import functools

import jax
import jax.numpy as jnp
from jax import lax
from jax.experimental import pallas as pl
from jax.experimental.pallas import tpu as pltpu
from jax.sharding import PartitionSpec as P


LANES = 128
SUB = 8
F32 = jnp.float32
BF16 = jnp.bfloat16
VMEM_SPEC = pl.BlockSpec(memory_space=pltpu.VMEM)
HBM_SPEC = pl.BlockSpec(memory_space=pltpu.HBM)


def parity(axis):
    return (lax.axis_index(axis) + 1) % 2


def silu_slope(value):
    sigma = 1.0 / (1.0 + jnp.exp(-value))
    return sigma * (1.0 + value * (1.0 - sigma))


def roll(value, shift, axis):
    return pltpu.roll(value, shift % value.shape[axis], axis)


def lane_of(shape):
    return lax.broadcasted_iota(jnp.int32, shape, len(shape) - 1)


def sub_of(shape):
    return lax.broadcasted_iota(jnp.int32, shape, len(shape) - 2)


def group_frames(frames, chans):
    first, second, third, fourth = frames
    part = LANES - chans
    lane = lane_of(first.shape)
    packed = []
    for index, frame in enumerate((first, second, third)):
        packed.append(jnp.where(lane < chans, frame, roll(fourth, chans - part * index, 1)))
    return packed


def ungroup_frames(groups, chans):
    part = LANES - chans
    lane = lane_of(groups[0].shape)
    frames = [jnp.where(lane < chans, group, 0.0) for group in groups]
    fourth = jnp.zeros_like(groups[0])
    for index in reversed(range(3)):
        moved = roll(groups[index], part * (index + 1), 1)
        fourth = jnp.where(lane < part * (index + 1), moved, fourth)
    return frames + [jnp.where(lane < chans, fourth, 0.0)]


def group_row(src, h, cols, chans):
    return group_frames([src[t, h, 0:cols] for t in range(4)], chans)


def pack_kernel(cot_hbm, sec_hbm, fst_hbm, ma0, ma1, wp0, wp1, cp_ref, sec_ref, fst_ref, raw_ref, edge_ref, row_ref, sems):
    frames, rows, cols, chans = cot_hbm.shape
    copies = [
        pltpu.make_async_copy(src, dst, sems.at[a])
        for a, (src, dst) in enumerate(((cot_hbm, raw_ref), (sec_hbm, sec_ref), (fst_hbm, fst_ref)))
    ]
    for copy in copies:
        copy.start()
    cp_ref[...] = jnp.zeros(cp_ref.shape, F32)
    edge_ref[...] = jnp.zeros(edge_ref.shape, F32)
    copies[0].wait()
    cp_ref[:, :, 0:cols, 0:chans] = raw_ref[...]

    row_ref[...] = jnp.zeros(row_ref.shape, F32)

    def rows_out(top, low):
        for r in range(3):
            for dst, h in ((top, r), (low, rows - 3 + r)):
                for g, val in enumerate(group_row(cp_ref, h, cols, chans)):
                    dst[g, r] = val

    @pl.when(parity("ha") == 0)
    def _():
        rows_out(ma1, ma0)

    @pl.when(parity("ha") != 0)
    def _():
        rows_out(ma0, ma1)

    for copy in copies[1:]:
        copy.wait()
    for at, h in enumerate((0, rows - 1)):
        row_ref[:, at, :, 0:chans] = silu_slope(fst_ref[:, h])

    def slope_out(top, low):
        for at, dst in enumerate((top, low)):
            for g, val in enumerate(group_row(row_ref, at, cols, chans)):
                dst[g, 3] = val

    @pl.when(parity("ha") == 0)
    def _():
        slope_out(ma1, ma0)

    @pl.when(parity("ha") != 0)
    def _():
        slope_out(ma0, ma1)

    for a, ref in ((0, sec_ref), (1, fst_ref)):
        for side, start in enumerate((0, cols - SUB)):
            edge_ref[a, side, :, :, :, 0:chans] = silu_slope(ref[:, :, start : start + SUB])

    def cols_out(left, right):
        sub = sub_of((SUB, LANES))
        for t in range(frames):
            for h in range(rows):
                c0, a0, b0 = cp_ref[t, h, 0:SUB], edge_ref[0, 0, t, h], edge_ref[1, 0, t, h]
                c7, a7, b7 = cp_ref[t, h, cols - SUB : cols], edge_ref[0, 1, t, h], edge_ref[1, 1, t, h]
                right[t, h] = jnp.where(
                    sub >= 5, c7, jnp.where((sub == 2) | (sub == 3), roll(a7, 4, 0), jnp.where(sub == 1, roll(b7, 2, 0), 0.0))
                )
                left[t, h] = jnp.where(
                    sub < 3, c0, jnp.where((sub == 4) | (sub == 5), roll(a0, 4, 0), jnp.where(sub == 6, roll(b0, 6, 0), 0.0))
                )

    @pl.when(parity("wa") == 0)
    def _():
        cols_out(wp1, wp0)

    @pl.when(parity("wa") != 0)
    def _():
        cols_out(wp0, wp1)


def slope_kernel(wanted, sec_ref, fst_ref, w3_hbm, w2_hbm, w1_hbm, mb0, mb1, s2_ref, s1_ref, u_ref, w2_ref, w1_ref, w_ref, sems):
    frames, rows, cols, chans = sec_ref.shape
    loads = [
        pltpu.make_async_copy(src, dst, sems.at[n])
        for n, (src, dst) in enumerate(((w3_hbm, w_ref), (w2_hbm, w2_ref), (w1_hbm, w1_ref)))
    ]
    for load in loads:
        load.start()
    blank = jnp.zeros((cols, LANES), F32)
    for src, ref in ((sec_ref, s2_ref), (fst_ref, s1_ref)):
        for t in range(frames):
            for h in range(rows):
                ref[t, h, 0:cols] = blank
                ref[t, h, 0:cols, 0:chans] = silu_slope(src[t, h])

    def rows_out(top, low):
        for src, h, dst, at in (
            (s2_ref, 0, top, 0),
            (s2_ref, 1, top, 1),
            (s2_ref, rows - 2, low, 0),
            (s2_ref, rows - 1, low, 1),
        ):
            for g, val in enumerate(group_row(src, h, cols, chans)):
                dst[g, at] = val

    @pl.when(parity("ha") == 0)
    def _():
        rows_out(mb1, mb0)

    @pl.when(parity("ha") != 0)
    def _():
        rows_out(mb0, mb1)

    loads[0].wait()
    for k in range(3):
        for step in prepare(w_ref, u_ref, wanted, k):
            step()
    for load in loads[1:]:
        load.wait()


def corner_kernel(chans, rw0, rw1, _c, _s2, _s1, _b0, _b1, mc0, mc1, cp_ref, s2_ref, s1_ref, _mb0, _mb1):
    frames, rows = rw0.shape[:2]
    cols = cp_ref.shape[2] - SUB
    even = parity("wa") == 0
    sub = sub_of((SUB, LANES))
    for t in range(frames):
        for h in range(rows):
            left = jnp.where(even, rw1[t, h], rw0[t, h])
            right = jnp.where(even, rw0[t, h], rw1[t, h])
            cp_ref[t, h, cols:] = jnp.where(sub < 3, right, jnp.where(sub >= 5, left, 0.0))
            s2_ref[t, h, cols:] = jnp.where(sub < 2, roll(right, 4, 0), jnp.where(sub >= 6, roll(left, 4, 0), 0.0))
            s1_ref[t, h, cols:] = jnp.where(sub == 0, roll(right, 2, 0), jnp.where(sub == 7, roll(left, 6, 0), 0.0))

    def out(top, low):
        def put(src, h, dst, at):
            for g, val in enumerate(group_frames([src[t, h, cols:] for t in range(frames)], chans)):
                dst[g, at] = val

        for r in range(3):
            put(cp_ref, r, top, r)
            put(cp_ref, rows - 3 + r, low, r)
        for r in range(2):
            put(s2_ref, r, top, 3 + r)
            put(s2_ref, rows - 2 + r, low, 3 + r)
        put(s1_ref, 0, top, 5)
        put(s1_ref, rows - 1, low, 5)

    @pl.when(parity("ha") == 0)
    def _():
        out(mc1, mc0)

    @pl.when(parity("ha") != 0)
    def _():
        out(mc0, mc1)


def prepare(w_ref, out_ref, wanted, k):
    chans = w_ref.shape[3]

    def clear():
        for n in range(len(wanted)):
            out_ref[n, k, :, chans:] = jnp.zeros((2, LANES - chans, 3 * LANES), BF16)

    def time_tap(i):
        blank = jnp.zeros((chans, LANES - chans), F32)
        f0, f1, f2 = (jnp.concatenate([w_ref[i, 2 - m, k], blank], 1) for m in range(3))
        even, odd = (f0 + f2) * (1 / 6), f1 * (1 / 6)
        far, odd2 = f0 * (1 / 24) + f2 * (1 / 6), f1 * (1 / 12)
        points = (f0 * 0.25, -even - odd, odd - even, far + odd2, far - odd2, f2)
        lanes = pl.ds((2 - i) * LANES, LANES)
        for n, p in enumerate(wanted):
            high = points[p].astype(BF16)
            out_ref[n, k, 0, 0:chans, lanes] = high
            out_ref[n, k, 1, 0:chans, lanes] = (points[p] - high.astype(F32)).astype(BF16)

    return [clear] + [functools.partial(time_tap, i) for i in range(3)]


def spread(steps, slots):
    return [steps[n * len(steps) // slots : (n + 1) * len(steps) // slots] for n in range(slots)]


POINTS = {2: (0, 1, 2, 5), 3: (0, 1, 2, 3, 5), 4: (0, 1, 2, 3, 4, 5)}


def transform(x, size, p):
    if size == 2:
        return (
            lambda: 4.0 * (x(0) - x(2)),
            lambda: -3.0 * (x(1) + x(2)),
            lambda: 3.0 * (x(1) - x(2)),
            lambda: x(3) - x(1),
        )[p]()
    if size == 3:
        return (
            lambda: 4.0 * (x(0) - x(2)) + 2.0 * (x(3) - x(1)),
            lambda: 3.0 * (x(3) - 2.0 * x(1) - x(2)),
            lambda: 2.0 * x(1) - 3.0 * x(2) + x(3),
            lambda: 4.0 * (x(3) - x(1)),
            lambda: x(4) - x(2) - 2.0 * (x(3) - x(1)),
        )[p]()
    return (
        lambda: 4.0 * x(0) - 5.0 * x(2) + x(4),
        lambda: x(4) - 4.0 * x(2) + (x(3) - 4.0 * x(1)),
        lambda: x(4) - 4.0 * x(2) - (x(3) - 4.0 * x(1)),
        lambda: x(4) - x(2) + 2.0 * (x(3) - x(1)),
        lambda: x(4) - x(2) - 2.0 * (x(3) - x(1)),
        lambda: 4.0 * x(1) - 5.0 * x(3) + x(5),
    )[p]()


def outputs(y, size):
    plus, minus = y[1] + y[2], y[1] - y[2]
    if size == 2:
        return y[0] + plus, minus + y[3]
    if size == 3:
        return y[0] + plus + y[3], minus + 2.0 * y[3], plus + 4.0 * y[3] + y[4]
    far, odd = y[3] + y[4], y[3] - y[4]
    return y[0] + plus + far, minus + 2.0 * odd, plus + 4.0 * far, minus + 8.0 * odd + y[5]


def right_operands(w_ref, p):
    zero = jnp.zeros((LANES, LANES), BF16)
    near, far = [], []
    for k in range(3):
        parts = [w_ref[p, k, part] for part in range(2)]
        own = [
            jnp.concatenate([r[:, : 2 * LANES], jnp.concatenate([zero, r[:, :LANES]], 1)], 0) for r in parts
        ]
        later = [
            jnp.concatenate([jnp.concatenate([r[:, 2 * LANES :], zero], 1), r[:, LANES:]], 0) for r in parts
        ]
        near.append(jnp.concatenate([own[0], own[0], own[1]], 1))
        far.append(jnp.concatenate([later[0], later[0], later[1]], 1))
    return jnp.concatenate(near, 0), jnp.concatenate(far, 0)


def product(left, right):
    left = jnp.concatenate([left, left[:, : 2 * LANES]], 1)
    return lax.dot_general(left, right, (((1,), (1,)), ((), ())), preferred_element_type=F32)


def shifted_sum(taps):
    two = 2 * LANES
    return roll(taps[:, :two], -1, 0) + taps[:, two : 2 * two] + roll(taps[:, 2 * two :], 1, 0)


def conv(read, size, width, s_ref, y_ref, w_ref, emit, done=None, beside=None, ahead=False):
    chunks = width // SUB
    points = len(POINTS[size])

    def fill(p, at, blocks):
        for t in range(4):
            pair, a = t // 2, t % 2
            tiles = []
            for base in (0, size):
                value = transform(lambda r: read(t, base + r, at), size, p)
                tiles.append(value.reshape(-1, 1, SUB, LANES))
            value = jnp.concatenate(tiles, 1).reshape(-1, 2 * SUB, LANES)
            high = value.astype(BF16)
            s_ref[p, blocks, pair, :, a * LANES : (a + 1) * LANES] = high
            s_ref[p, blocks, pair, :, (2 + a) * LANES : (3 + a) * LANES] = (value - high.astype(F32)).astype(BF16)

    def first(c, carry):
        for p in range(points if ahead else 1):
            fill(p, pl.ds(pl.multiple_of(c * SUB, SUB), SUB), pl.ds(c, 1))
        return carry

    lax.fori_loop(0, chunks, first, 0)

    wide = 4 * LANES

    def other_work(n):
        for step in beside[n] if beside else ():
            step()

    for p in range(points):
        near, far = right_operands(w_ref, p)
        own = product(s_ref[p].reshape(chunks * 4 * SUB, wide), near).reshape(chunks, 2, 2, SUB, 6 * LANES)
        if p + 1 < points and not ahead:
            fill(p + 1, slice(0, width), slice(0, chunks))
        other_work(2 * p)
        later = product(s_ref[p, :, 1].reshape(chunks * 2 * SUB, wide), far).reshape(chunks, 2, SUB, 6 * LANES)
        other_work(2 * p + 1)
        for n in range(2):
            y_ref[0, p, n] = shifted_sum((own[:, 0, n] + later[:, n]).reshape(width, 6 * LANES))
            y_ref[1, p, n] = shifted_sum(own[:, 1, n].reshape(width, 6 * LANES))

    for t in range(4):
        lanes = pl.ds(t % 2 * LANES, LANES)
        for tile in range(2):
            rows = outputs([y_ref[t // 2, p, tile, :, lanes] for p in range(points)], size)
            for o, value in enumerate(rows):
                emit(t, tile * size + o, value)
        if done is not None:
            done(t)


def halo_rows(chans, from_even, from_odd, r):
    return ungroup_frames([jnp.where(parity("ha") == 0, from_even[g, r], from_odd[g, r]) for g in range(3)], chans)


def third_kernel(chans, cp_ref, ra0, ra1, rc0, rc1, u3_ref, w2_ref, w1_ref, out_ref, u2_ref, u1_ref, x_ref, s_ref, y_ref):
    rows, width = cp_ref.shape[1:3]
    cols = width - SUB
    for r in range(3):
        for at, even, odd, ceven, codd in ((r, ra1, ra0, rc1, rc0), (r + 3, ra0, ra1, rc0, rc1)):
            for t, frame in enumerate(halo_rows(chans, even, odd, r)):
                x_ref[t, at, 0:cols] = frame
            for t, frame in enumerate(halo_rows(chans, ceven, codd, r)):
                x_ref[t, at, cols:] = frame

    def read(t, r, at):
        if 3 <= r < 3 + rows:
            return cp_ref[t, r - 3, at]
        return x_ref[t, r if r < 3 else r - rows, at]

    def emit(t, o, value):
        out_ref[t, o] = value

    steps = []
    for k in range(3):
        steps += prepare(w2_ref, u2_ref, POINTS[(rows + 2) // 2], k) + prepare(w1_ref, u1_ref, POINTS[rows // 2], k)
    beside = spread(steps, 2 * len(POINTS[rows]))
    conv(read, rows, width, s_ref, y_ref, u3_ref, emit, beside=beside)


def last_kernel(chans, g_ref, s2_ref, s1_ref, ra0, ra1, rb0, rb1, rc0, rc1, u2_ref, u1_ref, out_hbm,
                e_ref, x2_ref, x1_ref, s_ref, y_ref, stage_ref, sems):
    frames, rows, width, _ = s1_ref.shape
    cols = width - SUB
    for side, (even, odd) in enumerate(((1, 0), (0, 1))):
        for r in range(3):
            main, at = ((rb0, rb1), r) if r < 2 else ((ra0, ra1), 3)
            for t, frame in enumerate(halo_rows(chans, main[even], main[odd], at)):
                e_ref[side, r, t, 0:cols] = frame
            corners = (rc0, rc1)
            for t, frame in enumerate(halo_rows(chans, corners[even], corners[odd], 3 + r)):
                e_ref[side, r, t, cols:] = frame

        for t in range(frames):
            for r in range(2):
                at = r + side * (rows + 2)
                x2_ref[t, at] = e_ref[side, r, t] * g_ref[t, at]
    x2_ref[:, 2 : 2 + rows] = s2_ref[...] * g_ref[:, 2 : 2 + rows]

    def emit2(t, o, value):
        slope = s1_ref[t, o - 1] if 1 <= o < 1 + rows else e_ref[0 if o < 1 else 1, 2, t]
        x1_ref[t, o] = value * slope

    def emit1(t, o, value):
        stage_ref[t, o] = value[0:cols, 0:chans]

    def copy_out(t):
        return pltpu.make_async_copy(stage_ref.at[t], out_hbm.at[t], sems.at[t])

    size2, size1 = (rows + 2) // 2, rows // 2
    conv(lambda t, r, at: x2_ref[t, r, at], size2, width, s_ref, y_ref, u2_ref, emit2)
    conv(lambda t, r, at: x1_ref[t, r, at], size1, width, s_ref, y_ref, u1_ref, emit1, lambda t: copy_out(t).start())
    for t in range(frames):
        copy_out(t).wait()


def swap(value, axis, which):
    count = lax.axis_size(axis)
    pairs = []
    for low in range(1 - which, count - 1, 2):
        pairs += [(low, low + 1), (low + 1, low)]
    return lax.ppermute(value, axis, pairs)


def swaps(first, second, axis):
    got = []
    for which, value in enumerate((first, second)):
        got.append(swap(value, axis, which))
    return got


def call(body, out_shape, args, scratch=(), hbm=(), hbm_out=False, alias=None, vmem=24 << 20):
    out = HBM_SPEC if hbm_out else VMEM_SPEC
    return pl.pallas_call(
        body,
        out_shape=out_shape,
        in_specs=[HBM_SPEC if n in hbm else VMEM_SPEC for n in range(len(args))],
        out_specs=jax.tree.map(lambda _: out, out_shape),
        scratch_shapes=list(scratch),
        input_output_aliases=alias or {},
        compiler_params=pltpu.CompilerParams(vmem_limit_bytes=vmem),
    )(*args)


def program(cotangent, stored_first, stored_second, w_first, w_second, w_third):
    frames, rows, cols, chans = cotangent.shape
    width = cols + SUB

    def arr(*shape, dtype=F32):
        return jax.ShapeDtypeStruct(shape, dtype)

    def vmem(*shape, dtype=F32):
        return pltpu.VMEM(shape, dtype)

    edge = arr(frames, rows, SUB, LANES)
    own = arr(frames, rows, width, LANES)
    rows_a, rows_b = arr(3, 4, cols, LANES), arr(3, 2, cols, LANES)
    corner = arr(3, 6, SUB, LANES)
    *fields, third, second, first = (
        pltpu.with_memory_space_constraint(x, pltpu.HBM)
        for x in (cotangent, stored_second, stored_first, w_third, w_second, w_first)
    )
    raw = arr(frames, rows, cols, chans)
    ma0, ma1, wp0, wp1, cp, sec, fst = call(
        pack_kernel,
        (rows_a,) * 2 + (edge,) * 2 + (own, raw, raw),
        tuple(fields),
        [vmem(frames, rows, cols, chans), vmem(2, 2, frames, rows, SUB, LANES), vmem(frames, 2, cols, LANES), pltpu.SemaphoreType.DMA((3,))],
        hbm=(0, 1, 2),
    )
    ra0, ra1 = swaps(ma0, ma1, "ha")
    rw0, rw1 = swaps(wp0, wp1, "wa")

    def weights(size):
        return arr(len(POINTS[size]), 3, 2, LANES, 3 * LANES, dtype=BF16)

    size3, size2, size1 = rows, (rows + 2) // 2, rows // 2
    mb0, mb1, s2, s1, u3, second, first = call(
        functools.partial(slope_kernel, POINTS[size3]),
        (rows_b,) * 2 + (own,) * 2 + (weights(size3), arr(*second.shape), arr(*first.shape)),
        (sec, fst, third, second, first),
        [vmem(*third.shape), pltpu.SemaphoreType.DMA((3,))],
        hbm=(2, 3, 4),
    )
    mc0, mc1, cp, s2, s1, mb0, mb1 = call(
        functools.partial(corner_kernel, chans),
        (corner,) * 2 + (own,) * 3 + (rows_b,) * 2,
        (rw0, rw1, cp, s2, s1, mb0, mb1),
        alias={n + 2: n + 2 for n in range(5)},
    )
    rc0, rc1 = swaps(mc0, mc1, "ha")
    rb0, rb1 = swaps(mb0, mb1, "ha")

    def scratch(size):
        points = len(POINTS[size])
        return [
            vmem(points, width // SUB, 2, 2 * SUB, 4 * LANES, dtype=BF16),
            vmem(2, points, 2, width, 2 * LANES),
        ]

    grad, u2, u1 = call(
        functools.partial(third_kernel, chans),
        (arr(frames, rows + 4, width, LANES), weights(size2), weights(size1)),
        (cp, ra0, ra1, rc0, rc1, u3, second, first),
        [vmem(frames, 6, width, LANES)] + scratch(size3),
    )
    return call(
        functools.partial(last_kernel, chans),
        arr(frames, rows, cols, chans),
        (grad, s2, s1, ra0, ra1, rb0, rb1, rc0, rc1, u2, u1),
        [
            vmem(2, 3, frames, width, LANES),
            vmem(frames, rows + 4, width, LANES),
            vmem(frames, rows + 2, width, LANES),
        ]
        + scratch(size2)
        + [vmem(frames, rows, cols, chans), pltpu.SemaphoreType.DMA((frames,))],
        hbm_out=True,
    )


def solution(mesh):
    in_specs = (
        P("clip", "ha", "wa", None),
        P("clip", "ha", "wa", None),
        P("clip", "ha", "wa", None),
        P(),
        P(),
        P(),
    )
    out_specs = P("clip", "ha", "wa", None)
    return jax.shard_map(program, mesh=mesh, in_specs=in_specs, out_specs=out_specs, check_vma=False)
```
